32 devices in a mesh: seq: 2 (over x), fsdp: 16 (over z, y, core).
Axes of the slice: x: 2, y: 2, z: 4, core: 2. Of those that a mesh axis runs over, the one named last changes fastest.
Arguments:
- inputs: bfloat16 [16, 1024, 1024], P('fsdp', 'seq'), may hold values from -6 to 6
- ln_gain: bfloat16 [1024], P('fsdp'), may hold values from 0.5 to 1.5
- ln_shift: bfloat16 [1024], P('fsdp'), may hold values from -1.75 to 1.75
- w_query: bfloat16 [1024, 1024], P('fsdp'), may hold values from -0.1875 to 0.1875
- w_key: bfloat16 [1024, 1024], P('fsdp'), may hold values from -0.1875 to 0.1875
- w_value: bfloat16 [1024, 1024], P('fsdp'), may hold values from -0.1875 to 0.1875
- w_output: bfloat16 [1024, 1024], P('fsdp'), may hold values from -0.75 to 0.75
- exp_gain1: bfloat16 [16, 512], P('fsdp'), may hold values from 0.5 to 1.5
- exp_shift1: bfloat16 [16, 512], P('fsdp'), may hold values from -1.75 to 1.75
- w_in1: bfloat16 [16, 2048, 1024], P('fsdp', 'seq'), may hold values from -0.1875 to 0.1875
- b_in1: bfloat16 [16, 2048], P('fsdp'), may hold values from -1.75 to 1.75
- w_out1: bfloat16 [16, 2048, 1024], P('fsdp', 'seq'), may hold values from -0.1875 to 0.1875
- b_out1: bfloat16 [16, 512], P('fsdp'), may hold values from -1.75 to 1.75
- exp_gain2: bfloat16 [16, 512], P('fsdp'), may hold values from 0.5 to 1.5
- exp_shift2: bfloat16 [16, 512], P('fsdp'), may hold values from -1.75 to 1.75
- w_in2: bfloat16 [16, 2048, 1024], P('fsdp', 'seq'), may hold values from -0.1875 to 0.1875
- b_in2: bfloat16 [16, 2048], P('fsdp'), may hold values from -1.75 to 1.75
- w_out2: bfloat16 [16, 2048, 1024], P('fsdp', 'seq'), may hold values from -0.1875 to 0.1875
- b_out2: bfloat16 [16, 512], P('fsdp'), may hold values from -1.75 to 1.75
- centroid: bfloat16 [16, 512], P('fsdp'), may hold values from -0.125 to 0.125
- order: int32 [16, 1024], P('fsdp', 'seq'), may hold values from 0 to 511, as said below
- inverse: int32 [16, 1024], P('fsdp', 'seq'), may hold values from 0 to 511, as said below
- cotangent: bfloat16 [16, 1024, 1024], P('fsdp', 'seq'), may hold values from -6 to 6
Outputs:
- layer_out: bfloat16 [16, 1024, 1024], P('fsdp', 'seq')
- grad_inputs: float32 [16, 1024, 1024], P('fsdp', 'seq')
- grad_ln_gain: float32 [1024], P('fsdp')
- grad_ln_shift: float32 [1024], P('fsdp')
- grad_w_query: float32 [1024, 1024], P('fsdp')
- grad_w_key: float32 [1024, 1024], P('fsdp')
- grad_w_value: float32 [1024, 1024], P('fsdp')
- grad_w_output: float32 [1024, 1024], P('fsdp')
- grad_exp_gain1: float32 [16, 512], P('fsdp')
- grad_exp_shift1: float32 [16, 512], P('fsdp')
- grad_w_in1: float32 [16, 2048, 1024], P('fsdp', 'seq')
- grad_b_in1: float32 [16, 2048], P('fsdp')
- grad_w_out1: float32 [16, 2048, 1024], P('fsdp', 'seq')
- grad_b_out1: float32 [16, 512], P('fsdp')
- grad_exp_gain2: float32 [16, 512], P('fsdp')
- grad_exp_shift2: float32 [16, 512], P('fsdp')
- grad_w_in2: float32 [16, 2048, 1024], P('fsdp', 'seq')
- grad_b_in2: float32 [16, 2048], P('fsdp')
- grad_w_out2: float32 [16, 2048, 1024], P('fsdp', 'seq')
- grad_b_out2: float32 [16, 512], P('fsdp')
- grad_centroid: float32 [16, 512], P('fsdp')
The draws below stay inside these ranges and needn't reach their ends.
Inputs may be any that keep to these rules, and one draw needn't show every extreme that they name: `order`: within each row, every aligned block of 512 places holds each of 0 to 511 once, so every expert receives exactly 64 tokens of every block and 2048 in all. Within each aligned block of 512 places, the inverse of order: order[b, inverse[b, p]] = p.
All inputs are finite; a program needn't handle non-finite values.
Results may differ from the reference program's by a relative error of at most 0.018.
Values may be sent and summed in bfloat16 or wider, within the bound.
A program may use at most 384 MiB of HBM per device.

```python
import jax
import jax.numpy as jnp
from jax import lax

D = 1024
HEADS = 16
FF = 4096
TOK_DEV = 512
HEAD_DIM = 64
LENGTH = 1024
SEQS = 16
EXPERTS = 8


def routing_pair(key):
    blocks = SEQS * (LENGTH // TOK_DEV)
    block_keys = jax.random.split(jax.random.fold_in(key, 7), blocks)
    placed = jax.vmap(lambda block_key: jax.random.permutation(block_key, TOK_DEV))(block_keys).astype(jnp.int32)
    reverted = jnp.argsort(placed, axis=-1, stable=True).astype(jnp.int32)
    return (placed.reshape(SEQS, LENGTH), reverted.reshape(SEQS, LENGTH))


def draw_order(key, part):
    return routing_pair(key)[0]


def draw_inverse(key, part):
    return routing_pair(key)[1]


def level_of(stream_key, shape, shards, low, top_value):
    def one(dim, shards_of):
        steps = jax.random.uniform(jax.random.fold_in(jax.random.fold_in(stream_key, 6), dim), (shards_of,), jnp.float32, low / len(shards), top_value / len(shards))
        return jnp.repeat(jnp.exp(steps), shape[dim] // shards_of).reshape((-1,) + (1,) * (len(shape) - dim - 1))

    gain = one(*shards[0])
    for cut in shards[1:]:
        gain = gain * one(*cut)
    return gain


def noise(rng, dims, scale, most, pieces=(), held_as=jnp.bfloat16):
    level = level_of(rng, dims, pieces, -0.22, 0.18) if pieces else 1.0
    values = jax.random.normal(rng, dims, jnp.float32) * scale * level
    return jnp.minimum(jnp.maximum(values, -most), most).astype(held_as)


def setup_inputs(seed: int = 0) -> dict:
    splits = jax.random.split(jax.random.key(seed), 24)
    inputs = noise(splits[0], (SEQS, LENGTH, D), 1.0, 6.0, ((0, 16), (1, 2)))
    ln_gain = jnp.clip(1.0 + 0.1 * jax.random.normal(splits[1], (D,), jnp.float32), 0.5, 1.5).astype(jnp.bfloat16)
    ln_shift = noise(splits[2], (D,), 0.3, 1.75, ((0, 16),))
    w_query = noise(splits[3], (D, D), D ** -0.5, 0.1875, ((0, 16),))
    w_key = noise(splits[4], (D, D), D ** -0.5, 0.1875, ((0, 16),))
    w_value = noise(splits[5], (D, D), D ** -0.5, 0.1875, ((0, 16),))
    w_output = noise(splits[6], (D, D), (D // 16) ** -0.5, 0.75, ((0, 16),))
    exp_gain1 = jnp.clip(1.0 + 0.1 * jax.random.normal(splits[7], (2 * EXPERTS, D // 2), jnp.float32), 0.5, 1.5).astype(jnp.bfloat16)
    exp_shift1 = noise(splits[8], (2 * EXPERTS, D // 2), 0.3, 1.75, ((0, 16),))
    w_in1 = noise(splits[9], (2 * EXPERTS, FF // 2, D), D ** -0.5, 0.1875, ((0, 16), (1, 2)))
    b_in1 = noise(splits[10], (2 * EXPERTS, FF // 2), 0.3, 1.75, ((0, 16),))
    w_out1 = noise(splits[11], (2 * EXPERTS, FF // 2, D), (FF // 4) ** -0.5, 0.1875, ((0, 16), (1, 2)))
    b_out1 = noise(splits[12], (2 * EXPERTS, D // 2), 0.3, 1.75, ((0, 16),))
    exp_gain2 = jnp.clip(1.0 + 0.1 * jax.random.normal(splits[13], (2 * EXPERTS, D // 2), jnp.float32), 0.5, 1.5).astype(jnp.bfloat16)
    exp_shift2 = noise(splits[14], (2 * EXPERTS, D // 2), 0.3, 1.75, ((0, 16),))
    w_in2 = noise(splits[15], (2 * EXPERTS, FF // 2, D), D ** -0.5, 0.1875, ((0, 16), (1, 2)))
    b_in2 = noise(splits[16], (2 * EXPERTS, FF // 2), 0.3, 1.75, ((0, 16),))
    w_out2 = noise(splits[17], (2 * EXPERTS, FF // 2, D), (FF // 4) ** -0.5, 0.1875, ((0, 16), (1, 2)))
    b_out2 = noise(splits[18], (2 * EXPERTS, D // 2), 0.3, 1.75, ((0, 16),))
    centroid = noise(splits[19], (2 * EXPERTS, D // 2), (2 * D) ** -0.5, 0.125, ((0, 16),))
    order = draw_order(jax.random.fold_in(splits[23], 71), 0)
    inverse = draw_inverse(jax.random.fold_in(splits[23], 71), 0)
    cotangent = noise(splits[22], (SEQS, LENGTH, D), 1.0, 6.0, ((0, 16), (1, 2)))
    return dict(inputs=inputs, ln_gain=ln_gain, ln_shift=ln_shift, w_query=w_query, w_key=w_key, w_value=w_value, w_output=w_output, exp_gain1=exp_gain1, exp_shift1=exp_shift1, w_in1=w_in1, b_in1=b_in1, w_out1=w_out1, b_out1=b_out1, exp_gain2=exp_gain2, exp_shift2=exp_shift2, w_in2=w_in2, b_in2=b_in2, w_out2=w_out2, b_out2=b_out2, centroid=centroid, order=order, inverse=inverse, cotangent=cotangent)


@jax.custom_vjp
def low(v):
    return lax.optimization_barrier(v.astype(jnp.bfloat16)).astype(jnp.float32)

@jax.custom_vjp
def low_back(v):
    return v

def low_keep(v):
    return (low(v), None)

def low_pass(kept, grad):
    return (grad,)

def back_keep(v):
    return (v, None)

def back_low(kept, grad):
    return (low(grad),)
low.defvjp(low_keep, low_pass)
low_back.defvjp(back_keep, back_low)
epsilon = 1e-05
highest = lax.Precision.HIGHEST

def rounded(values):
    return low(low_back(values))

def product(left, right):
    return jnp.dot(left, right, precision=highest, preferred_element_type=jnp.float32)

def layer_norm(values, gain_row, shift_row):
    row_mean = lax.optimization_barrier(jnp.mean(values, axis=-1, keepdims=True))
    centred = values - row_mean
    spread = lax.optimization_barrier(jnp.mean(centred * centred, axis=-1, keepdims=True))
    return centred * lax.rsqrt(spread + epsilon) * gain_row + shift_row

def attention_block(token_rows, params):
    ln_gain, ln_shift, w_query, w_key, w_value, w_output = params
    length = token_rows.shape[0]
    normed = low(layer_norm(token_rows, ln_gain, ln_shift))
    query = rounded(product(normed, w_query)).reshape(length, HEADS, HEAD_DIM)
    key_heads = rounded(product(normed, w_key)).reshape(length, HEADS, HEAD_DIM)
    value_heads = rounded(product(normed, w_value)).reshape(length, HEADS, HEAD_DIM)
    scores = jnp.einsum('qhd,khd->hqk', query, key_heads, precision=highest) * HEAD_DIM ** (-0.5)
    places = jnp.arange(length)
    causal = places[None, :] <= places[:, None]
    scores = low_back(jnp.where(causal[None], scores, -1e+30))
    weights = low(jax.nn.softmax(scores, axis=-1))
    mixed_heads = jnp.einsum('hqk,khd->qhd', weights, value_heads, precision=highest).reshape(length, D)
    mixed_heads = rounded(mixed_heads)
    return token_rows + low_back(product(mixed_heads, w_output))

def sublayer(token_rows, gain_row, shift_row, in_rows, in_bias, out_rows, out_bias):
    normed = low(layer_norm(token_rows, gain_row, shift_row))
    inner_sum = low_back(jnp.dot(normed, in_rows.T, precision=highest, preferred_element_type=jnp.float32) + in_bias)
    active = low(jax.nn.gelu(inner_sum, approximate=False))
    return low_back(product(active, out_rows) + out_bias)

def expert_branch(token_rows, gain_one, shift_one, in_one, in_bias_one, out_one, out_bias_one, gain_two, shift_two, in_two, in_bias_two, out_two, out_bias_two, centroid):
    first = sublayer(token_rows, gain_one, shift_one, in_one, in_bias_one, out_one, out_bias_one)
    second = sublayer(token_rows + first, gain_two, shift_two, in_two, in_bias_two, out_two, out_bias_two)
    gate_value = jax.nn.sigmoid(lax.optimization_barrier(jnp.sum(token_rows * centroid, axis=-1, keepdims=True)))
    return gate_value * (first + second)

def forward(inputs, attn_params, expert_params, order, inverse):

    def one_sequence(carried, token_rows):
        return (carried, jax.checkpoint(attention_block)(token_rows, attn_params))
    _, middle = lax.scan(one_sequence, jnp.int32(0), inputs)
    blocks = inputs.shape[0] * (inputs.shape[1] // TOK_DEV)
    per_expert = TOK_DEV // EXPERTS
    flat_rows = middle.reshape(blocks, TOK_DEV, D)
    sent_rows = rounded(flat_rows)
    order_rows = order.reshape(blocks, TOK_DEV).astype(jnp.int32)
    inverse_rows = inverse.reshape(blocks, TOK_DEV).astype(jnp.int32)
    slot_rows = jnp.take_along_axis(sent_rows, order_rows[:, :, None], axis=1)
    grouped = slot_rows.reshape(blocks, EXPERTS, per_expert, D).transpose(1, 0, 2, 3).reshape(EXPERTS, blocks * per_expert, D)
    tables = tuple((item.reshape((EXPERTS, -1) + item.shape[2:]) for item in expert_params))

    def one_expert(expert_item):
        return jax.checkpoint(expert_branch)(*expert_item)
    returned = lax.map(one_expert, (grouped,) + tables)
    returned = rounded(returned)
    returned = returned.reshape(EXPERTS, blocks, per_expert, D).transpose(1, 0, 2, 3).reshape(blocks, TOK_DEV, D)
    home_rows = jnp.take_along_axis(returned, inverse_rows[:, :, None], axis=1)
    return (flat_rows + home_rows).reshape(inputs.shape)

def widen(array):
    return array.astype(jnp.float32)

def reference(inputs, ln_gain, ln_shift, w_query, w_key, w_value, w_output, exp_gain1, exp_shift1, w_in1, b_in1, w_out1, b_out1, exp_gain2, exp_shift2, w_in2, b_in2, w_out2, b_out2, centroid, order, inverse, cotangent):
    attn_params = (widen(ln_gain), widen(ln_shift), widen(w_query), widen(w_key), widen(w_value), widen(w_output))
    expert_params = (widen(exp_gain1), widen(exp_shift1), widen(w_in1), widen(b_in1), widen(w_out1), widen(b_out1), widen(exp_gain2), widen(exp_shift2), widen(w_in2), widen(b_in2), widen(w_out2), widen(b_out2), widen(centroid))

    def whole(source, attn_group, expert_group):
        return forward(source, attn_group, expert_group, order, inverse)
    result, pullback = jax.vjp(whole, widen(inputs), attn_params, expert_params)
    grad_input, grad_attn, grad_expert = pullback(widen(cotangent))
    return (result.astype(jnp.bfloat16), grad_input, grad_attn[0], grad_attn[1], grad_attn[2], grad_attn[3], grad_attn[4], grad_attn[5], grad_expert[0], grad_expert[1], grad_expert[2], grad_expert[3], grad_expert[4], grad_expert[5], grad_expert[6], grad_expert[7], grad_expert[8], grad_expert[9], grad_expert[10], grad_expert[11], grad_expert[12])
```

```python
import functools

import jax
import jax.numpy as jnp
from jax import lax
from jax.experimental import pallas as pl
from jax.experimental.pallas import tpu as pltpu
from jax.sharding import PartitionSpec as P

HEADS = 16
EPS = 1e-05
MASKED = -1e30
BLOCK = 256
CHUNK = 512
BF16 = jnp.bfloat16
F32 = jnp.float32
VMEM_LIMIT = 56 * 1024 * 1024


def swapped(value, axis):
    pairs = [(source, source ^ 1) for source in range(lax.axis_size(axis))]
    return lax.ppermute(value, axis, pairs)


def dot_last(left, right):
    return lax.dot_general(left, right, (((1,), (1,)), ((), ())), preferred_element_type=F32)


def dot_first(left, right):
    return lax.dot_general(left, right, (((0,), (0,)), ((), ())), preferred_element_type=F32)


def dot(left, right):
    return jnp.dot(left, right, preferred_element_type=F32)


def normalised(values):
    centred = values - jnp.mean(values, axis=-1, keepdims=True)
    spread = jnp.mean(centred * centred, axis=-1, keepdims=True)
    rate = lax.rsqrt(spread + EPS)
    return centred * rate, rate


def norm_back(grad, xhat, rate, gain):
    scaled = grad * gain
    inner = jnp.mean(scaled * xhat, axis=-1, keepdims=True)
    return rate * (scaled - jnp.mean(scaled, axis=-1, keepdims=True) - xhat * inner)


def causal_mask(scores):
    keys = lax.broadcasted_iota(jnp.int32, scores.shape, 0)
    queries = lax.broadcasted_iota(jnp.int32, scores.shape, 1)
    return jnp.where(keys <= queries, scores, MASKED)


def attention_forward_kernel(size, q_ref, k_ref, v_ref, o_ref, log_ref):
    length = q_ref.shape[0]
    for head in range(q_ref.shape[1] // size):
        lanes = slice(head * size, (head + 1) * size)
        for start in range(0, length, BLOCK):
            query = q_ref[start : start + BLOCK, lanes] * BF16(size**-0.5)
            last = causal_mask(dot_last(k_ref[start : start + BLOCK, lanes], query))
            peak = jnp.max(last, axis=0, keepdims=True)
            if start:
                early = dot_last(k_ref[:start, lanes], query)
                peak = jnp.maximum(peak, jnp.max(early, axis=0, keepdims=True))
            last = jnp.exp(last - peak)
            total = jnp.sum(last, axis=0, keepdims=True)
            out = dot_first(v_ref[start : start + BLOCK, lanes], last.astype(BF16))
            if start:
                early = jnp.exp(early - peak)
                total = total + jnp.sum(early, axis=0, keepdims=True)
                out = out + dot_first(v_ref[:start, lanes], early.astype(BF16))
            o_ref[start : start + BLOCK, lanes] = (out / total).T.astype(BF16)
            log_ref[0, head : head + 1, start : start + BLOCK] = peak + jnp.log(total)


def attention_backward_kernel(size, q_ref, k_ref, v_ref, g_ref, log_ref, d_ref, dk_sum, dv_sum):
    length = q_ref.shape[0]
    scale = size**-0.5
    for head in range(q_ref.shape[1] // size):
        lanes = slice(head * size, (head + 1) * size)
        dk_sum[...] = jnp.zeros_like(dk_sum)
        dv_sum[...] = jnp.zeros_like(dv_sum)
        for start in range(0, length, BLOCK):
            rows = slice(start, start + BLOCK)
            query = q_ref[rows, lanes] * BF16(scale)
            grad = g_ref[rows, lanes]
            log_total = log_ref[0, head : head + 1, rows]
            spans = ([slice(0, start)] if start else []) + [rows]
            probs, weighted = [], []
            inner = jnp.zeros((1, BLOCK), F32)
            for span in spans:
                scores = dot_last(k_ref[span, lanes], query)
                if span is rows:
                    scores = causal_mask(scores)
                prob = jnp.exp(scores - log_total)
                grad_prob = dot_last(v_ref[span, lanes], grad)
                inner = inner + jnp.sum(prob * grad_prob, axis=0, keepdims=True)
                probs.append(prob)
                weighted.append(grad_prob)
            grad_query = jnp.zeros((BLOCK, size), F32)
            for span, prob, grad_prob in zip(spans, probs, weighted):
                low = (prob * (grad_prob - inner)).astype(BF16)
                dv_sum[span, :] += dot(prob.astype(BF16), grad)
                dk_sum[span, :] += dot(low, query)
                grad_query = grad_query + dot_first(low, k_ref[span, lanes])
            d_ref[0, rows, lanes] = (grad_query * scale).astype(BF16)
        d_ref[1, :, lanes] = dk_sum[...].astype(BF16)
        d_ref[2, :, lanes] = dv_sum[...].astype(BF16)


def attention_specs(length, half):
    parts = half // 128
    column = lambda which: pl.BlockSpec((length, 128), lambda i: (0, which * parts + i))
    return parts, column


def attention_forward(qkv, size):
    length, half = qkv.shape[0], qkv.shape[1] // 3
    parts, column = attention_specs(length, half)
    per = 128 // size
    return pl.pallas_call(
        functools.partial(attention_forward_kernel, size),
        grid=(parts,),
        out_shape=(
            jax.ShapeDtypeStruct((length, half), BF16),
            jax.ShapeDtypeStruct((parts, per, length), F32),
        ),
        in_specs=[column(0), column(1), column(2)],
        out_specs=(column(0), pl.BlockSpec((1, per, length), lambda i: (i, 0, 0))),
        compiler_params=pltpu.CompilerParams(vmem_limit_bytes=VMEM_LIMIT),
        cost_estimate=pl.CostEstimate(
            flops=8 * length * length * half, bytes_accessed=10 * length * half, transcendentals=0
        ),
        name="attention_forward",
    )(qkv, qkv, qkv)


def attention_backward(qkv, grad, logs, size):
    length, half = grad.shape
    parts, column = attention_specs(length, half)
    per = 128 // size
    return pl.pallas_call(
        functools.partial(attention_backward_kernel, size),
        grid=(parts,),
        out_shape=jax.ShapeDtypeStruct((3, length, half), BF16),
        in_specs=[
            column(0),
            column(1),
            column(2),
            column(0),
            pl.BlockSpec((1, per, length), lambda i: (i, 0, 0)),
        ],
        out_specs=pl.BlockSpec((3, length, 128), lambda i: (0, 0, i)),
        scratch_shapes=[pltpu.VMEM((length, size), F32), pltpu.VMEM((length, size), F32)],
        compiler_params=pltpu.CompilerParams(vmem_limit_bytes=VMEM_LIMIT),
        cost_estimate=pl.CostEstimate(
            flops=20 * length * length * half, bytes_accessed=16 * length * half, transcendentals=0
        ),
        name="attention_backward",
    )(qkv, qkv, qkv, grad, logs)


def stream(step, steps, parts, pairs, buffers, sems):
    per = steps // parts

    def fetch(which):
        slot = lax.rem(which, 2)
        row = pl.multiple_of(lax.rem(which, per) * CHUNK, CHUNK)
        for quarter in range(parts):

            @pl.when(which // per == quarter)
            def _():
                for m, refs in enumerate(pairs):
                    pltpu.make_async_copy(
                        refs[quarter].at[pl.ds(row, CHUNK)], buffers[m].at[slot], sems.at[m, slot]
                    ).start()

    @pl.when(step == 0)
    def _():
        fetch(step)

    @pl.when(step + 1 < steps)
    def _():
        fetch(step + 1)

    slot = lax.rem(step, 2)
    for m, refs in enumerate(pairs):
        pltpu.make_async_copy(
            refs[0].at[pl.ds(0, CHUNK)], buffers[m].at[slot], sems.at[m, slot]
        ).wait()
    return slot


def gelu_parts(inner):
    cdf = 0.5 * (1.0 + lax.erf(inner * 0.7071067811865476))
    slope = cdf + inner * (jnp.exp(-0.5 * inner * inner) * 0.3989422804014327)
    return inner * cdf, slope


def forward_first_kernel(parts, steps, *refs):
    z_ref, gain_ref, shift_ref, bias_ref, out_bias_ref = refs[:5]
    win, wout = refs[5 : 5 + parts], refs[5 + parts : 5 + 2 * parts]
    first_ref, normed_ref, active_ref, slope_ref, in_buf, out_buf, sems = refs[5 + 2 * parts :]
    step = pl.program_id(0)

    @pl.when(step == 0)
    def _():
        xhat, _ = normalised(z_ref[...].astype(F32))
        normed_ref[...] = (xhat * gain_ref[...] + shift_ref[...]).astype(BF16)
        first_ref[...] = jnp.broadcast_to(out_bias_ref[...], first_ref.shape)

    slot = stream(step, steps, parts, (win, wout), (in_buf, out_buf), sems)
    active, slope = gelu_parts(dot_last(normed_ref[...], in_buf[slot]) + bias_ref[0])
    low = active.astype(BF16)
    active_ref[...] = low
    slope_ref[...] = slope.astype(BF16)
    first_ref[...] += dot(low, out_buf[slot])


def forward_second_kernel(parts, steps, *refs):
    z_ref, first_ref, cot_ref, centre_ref, gain_ref, shift_ref, bias_ref, out_bias_ref = refs[:8]
    win, wout = refs[8 : 8 + parts], refs[8 + parts : 8 + 2 * parts]
    normed_ref, active_ref, slope_ref, gated_ref, grad_ref, score_ref = refs[
        8 + 2 * parts : 14 + 2 * parts
    ]
    total, in_buf, out_buf, sems = refs[14 + 2 * parts :]
    step = pl.program_id(0)

    @pl.when(step == 0)
    def _():
        xhat, _ = normalised(z_ref[...].astype(F32) + first_ref[...])
        normed_ref[...] = (xhat * gain_ref[...] + shift_ref[...]).astype(BF16)
        total[...] = first_ref[...] + out_bias_ref[...]

    slot = stream(step, steps, parts, (win, wout), (in_buf, out_buf), sems)
    active, slope = gelu_parts(dot_last(normed_ref[...], in_buf[slot]) + bias_ref[0])
    low = active.astype(BF16)
    active_ref[...] = low
    slope_ref[...] = slope.astype(BF16)
    total[...] += dot(low, out_buf[slot])

    @pl.when(step == steps - 1)
    def _():
        branch = total[...]
        grad_gated = cot_ref[...].astype(F32)
        logit = jnp.sum(z_ref[...].astype(F32) * centre_ref[...], axis=-1, keepdims=True)
        gate = jax.nn.sigmoid(logit)
        gated_ref[...] = (gate * branch).astype(BF16)
        grad_ref[...] = (gate * grad_gated).astype(BF16)
        grad_gate = jnp.sum(grad_gated * branch, axis=-1, keepdims=True)
        score_ref[...] = jnp.broadcast_to(grad_gate * gate * (1.0 - gate), score_ref.shape)


def backward_kernel(second, parts, steps, *refs):
    grad_ref, normed_ref, active_ref, slope_ref, z_ref, centre_ref, gain_ref = refs[:7]
    extra_one, extra_two = refs[7:9]
    win, wout = refs[9 : 9 + parts], refs[9 + parts : 9 + 2 * parts]
    base = 9 + 2 * parts
    result = refs[base : base + (2 if second else 1)]
    base += len(result)
    vector_ref, bias_ref = refs[base : base + 2]
    gwin, gwout = refs[base + 2 : base + 2 + parts], refs[base + 2 + parts : base + 2 + 2 * parts]
    total, in_buf, out_buf, sems = refs[base + 2 + 2 * parts :]
    step = pl.program_id(0)
    per = steps // parts

    @pl.when(step == 0)
    def _():
        total[...] = jnp.zeros_like(total)

    slot = stream(step, steps, parts, (win, wout), (in_buf, out_buf), sems)
    grad = grad_ref[...]
    inner = (slope_ref[...].astype(F32) * dot_last(grad, out_buf[slot])).astype(BF16)
    bias_ref[0] = jnp.sum(inner.astype(F32), axis=0, keepdims=True)
    total[...] += dot(inner, in_buf[slot])
    grad_out = dot_first(active_ref[...], grad).astype(BF16)
    grad_in = dot_first(inner, normed_ref[...]).astype(BF16)
    for quarter in range(parts):

        @pl.when(step // per == quarter)
        def _():
            gwin[quarter][...] = grad_in
            gwout[quarter][...] = grad_out

    @pl.when(step == steps - 1)
    def _():
        z = z_ref[...].astype(F32)
        source = z + extra_one[...] if second else z
        xhat, rate = normalised(source)
        grad_normed = total[...]
        grad_rows = norm_back(grad_normed, xhat, rate, gain_ref[...])
        vector_ref[...] = jnp.zeros_like(vector_ref)
        vector_ref[0:1] = jnp.sum(grad_normed * xhat, axis=0, keepdims=True)
        vector_ref[1:2] = jnp.sum(grad_normed, axis=0, keepdims=True)
        vector_ref[2:3] = jnp.sum(grad.astype(F32), axis=0, keepdims=True)
        if second:
            gate = jax.nn.sigmoid(jnp.sum(z * centre_ref[...], axis=-1, keepdims=True))
            result[0][...] = grad_rows
            result[1][...] = (gate * extra_two[...].astype(F32) + grad_rows).astype(BF16)
        else:
            score = extra_two[:, 0:1]
            vector_ref[3:4] = jnp.sum(score * z, axis=0, keepdims=True)
            result[0][...] = (extra_one[...] + grad_rows + score * centre_ref[...]).astype(BF16)


def expert_call(kernel, name, steps, rows, inputs, weights, outs, scratch, flops):
    whole = lambda shape: pl.BlockSpec(shape, lambda c: (0,) * len(shape))
    spec = lambda shape, block, at: whole(shape) if block is None else pl.BlockSpec(block, at)
    features = weights[0].shape[1]
    return pl.pallas_call(
        kernel,
        grid=(steps,),
        out_shape=tuple(s for s, _, _ in outs),
        in_specs=[spec(a.shape, b, m) for a, b, m in inputs]
        + [pl.BlockSpec(memory_space=pl.ANY)] * len(weights),
        out_specs=tuple(spec(s.shape, b, m) for s, b, m in outs),
        scratch_shapes=scratch
        + [
            pltpu.VMEM((2, CHUNK, features), BF16),
            pltpu.VMEM((2, CHUNK, features), BF16),
            pltpu.SemaphoreType.DMA((2, 2)),
        ],
        compiler_params=pltpu.CompilerParams(vmem_limit_bytes=VMEM_LIMIT),
        cost_estimate=pl.CostEstimate(
            flops=flops, bytes_accessed=2 * sum(w.size for w in weights), transcendentals=0
        ),
        name=name,
    )(*[a for a, _, _ in inputs], *weights)


def expert(z, cot, vectors, biases, one, two):
    rows, features = z.shape
    parts = len(one[0])
    hidden = sum(w.shape[0] for w in one[0])
    steps = hidden // CHUNK
    per = steps // parts
    line = lambda i: (vectors[i : i + 1], None, None)
    shape = jax.ShapeDtypeStruct
    wide = ((rows, CHUNK), lambda c: (0, c))
    thin = ((1, 1, CHUNK), lambda c: (c, 0, 0))
    chunked = biases.reshape(2, steps, 1, CHUNK)
    hidden_out = [
        (shape((rows, features), BF16), None, None),
        (shape((rows, hidden), BF16), *wide),
        (shape((rows, hidden), BF16), *wide),
    ]
    matmul = 2 * rows * hidden * features
    first, normed_one, active_one, slope_one = expert_call(
        functools.partial(forward_first_kernel, parts, steps),
        "forward_first",
        steps,
        rows,
        [(z, None, None), line(0), line(1), (chunked[0], *thin), line(2)],
        one[0] + one[1],
        [(shape((rows, features), F32), None, None)] + hidden_out,
        [],
        2 * matmul,
    )
    normed_two, active_two, slope_two, gated, grad_second, score = expert_call(
        functools.partial(forward_second_kernel, parts, steps),
        "forward_second",
        steps,
        rows,
        [
            (z, None, None),
            (first, None, None),
            (cot, None, None),
            line(6),
            line(3),
            line(4),
            (chunked[1], *thin),
            line(5),
        ],
        two[0] + two[1],
        hidden_out
        + [
            (shape((rows, features), BF16), None, None),
            (shape((rows, features), BF16), None, None),
            (shape((rows, 128), F32), None, None),
        ],
        [pltpu.VMEM((rows, features), F32)],
        2 * matmul,
    )

    def quarter_outs():
        return [
            (
                shape((hidden // parts, features), BF16),
                (CHUNK, features),
                lambda c, q=q: (jnp.clip(c - q * per, 0, per - 1), 0),
            )
            for q in range(parts)
        ]

    sums = [
        (shape((8, features), F32), None, None),
        (shape((steps, 1, CHUNK), F32), *thin),
    ]

    def back(second, grad, normed, active, slope, gain, extra_one, extra_two, weights, results):
        outs = expert_call(
            functools.partial(backward_kernel, second, parts, steps),
            "backward_second" if second else "backward_first",
            steps,
            rows,
            [
                (grad, None, None),
                (normed, None, None),
                (active, *wide),
                (slope, *wide),
                (z, None, None),
                line(6),
                line(gain),
                (extra_one, None, None),
                (extra_two, None, None),
            ],
            weights[0] + weights[1],
            results + sums + quarter_outs() + quarter_outs(),
            [pltpu.VMEM((rows, features), F32)],
            4 * matmul,
        )
        n = len(results)
        tail = outs[n + 2 :]
        return outs[:n], outs[n], outs[n + 1].reshape(hidden), tail[:parts], tail[parts:]

    (grad_in_two, grad_first), sums_two, bias_two, gwin_two, gwout_two = back(
        True,
        grad_second,
        normed_two,
        active_two,
        slope_two,
        3,
        first,
        cot,
        two,
        [
            (shape((rows, features), F32), None, None),
            (shape((rows, features), BF16), None, None),
        ],
    )
    (grad_sent,), sums_one, bias_one, gwin_one, gwout_one = back(
        False,
        grad_first,
        normed_one,
        active_one,
        slope_one,
        0,
        grad_in_two,
        score,
        one,
        [(shape((rows, features), BF16), None, None)],
    )
    vector_grads = jnp.concatenate([sums_one[:3], sums_two[:3], sums_one[3:4]], axis=0)
    bias_grads = jnp.stack([bias_one, bias_two])
    return gated, grad_sent, vector_grads, bias_grads, (gwin_one, gwout_one), (gwin_two, gwout_two)


def body(
    inputs,
    ln_gain,
    ln_shift,
    w_query,
    w_key,
    w_value,
    w_output,
    exp_gain1,
    exp_shift1,
    w_in1,
    b_in1,
    w_out1,
    b_out1,
    exp_gain2,
    exp_shift2,
    w_in2,
    b_in2,
    w_out2,
    b_out2,
    centroid,
    order,
    inverse,
    cotangent,
):
    seq, peer = lax.axis_index("seq"), lax.axis_index("fsdp")
    peers = lax.axis_size("fsdp")
    rows = inputs[0]
    tokens, features = rows.shape
    half = features // 2
    size = features // HEADS
    left, even = seq == 0, lax.rem(peer, 2) == 0
    over = lambda value: swapped(value, "seq")
    beside = lambda value: swapped(value, "fsdp")
    ordered = lambda flag, mine, other, axis: jnp.where(
        flag, jnp.concatenate([mine, other], axis), jnp.concatenate([other, mine], axis)
    )

    other_rows = over(rows)
    columns = lambda w: lax.dynamic_slice_in_dim(w, seq * half, half, 1)
    norm_vectors = jnp.pad(jnp.stack([ln_gain, ln_shift], axis=1), ((0, 0), (0, 126)))
    gathered = lax.all_gather(
        jnp.concatenate([columns(w_query), columns(w_key), columns(w_value), norm_vectors], axis=1),
        "fsdp",
        axis=0,
        tiled=True,
    )
    output_full = lax.all_gather(w_output, "fsdp", axis=0, tiled=True)
    own_vectors = jnp.concatenate(
        [exp_gain1, exp_shift1, b_out1, exp_gain2, exp_shift2, b_out2, centroid], axis=0
    )
    own_biases = jnp.concatenate([b_in1, b_in2], axis=0)
    pair = beside(jnp.concatenate([own_vectors.reshape(-1), own_biases.reshape(-1)]))
    other_vectors = pair[: own_vectors.size].reshape(own_vectors.shape)
    other_biases = pair[own_vectors.size :].reshape(own_biases.shape)
    vectors = ordered(even, own_vectors, other_vectors, 1).astype(F32)

    quarter = w_in1.shape[1]
    pick = lambda table, which: lax.dynamic_slice_in_dim(table, which * quarter, quarter, 1)
    biases = jnp.concatenate(
        [
            pick(own_biases, seq),
            pick(other_biases, seq),
            pick(own_biases, 1 - seq),
            pick(other_biases, 1 - seq),
        ],
        axis=1,
    ).astype(F32)

    def holders(weight):
        mine = weight[0]
        far = over(mine)
        return [mine, beside(mine), far, beside(far)]

    one = (holders(w_in1), holders(w_out1))
    two = (holders(w_in2), holders(w_out2))
    cot = cotangent[0]
    exchange = lambda value: lax.all_to_all(
        value.reshape(peers, tokens // peers, features),
        "fsdp",
        split_axis=0,
        concat_axis=0,
        tiled=True,
    ).reshape(tokens, features)
    cot_slots = exchange(jnp.take(cot, order[0], axis=0))

    sequence = ordered(left, rows, other_rows, 0).astype(F32)
    gain, shift = gathered[:, 3 * half].astype(F32), gathered[:, 3 * half + 1].astype(F32)
    xhat, rate = normalised(sequence)
    normed = (xhat * gain + shift).astype(BF16)
    qkv_weight = gathered[:, : 3 * half]
    qkv = dot(normed, qkv_weight).astype(BF16)
    mixed_heads, logs = attention_forward(qkv, size)
    block_of = lambda value, which: lax.dynamic_slice_in_dim(value, which * tokens, tokens, 0)
    mixed = ordered(
        left, block_of(mixed_heads, seq), over(block_of(mixed_heads, 1 - seq)), 1
    )
    middle = rows.astype(F32) + dot(mixed, output_full)

    z = exchange(jnp.take(middle.astype(BF16), order[0], axis=0))
    gated, grad_sent, vector_grads, bias_grads, grads_one, grads_two = expert(
        z, cot_slots, vectors, biases, one, two
    )
    home = jnp.take(exchange(gated), inverse[0], axis=0)
    layer_out = (middle + home.astype(F32)).astype(BF16)
    coming = jnp.take(exchange(grad_sent), inverse[0], axis=0)
    grad_middle = cot.astype(F32) + coming.astype(F32)

    def holders_sum(quarters):
        mine, near, far, cross = quarters
        mine = mine.astype(F32) + beside(near).astype(F32)
        far = (far.astype(F32) + beside(cross).astype(F32)).astype(BF16)
        return mine + over(far).astype(F32)

    grad_win_two, grad_wout_two = [holders_sum(g) for g in grads_two]
    grad_win_one, grad_wout_one = [holders_sum(g) for g in grads_one]

    own_half = lambda table, which: lax.dynamic_slice_in_dim(table, which * half, half, 1)
    core = lax.rem(peer, 2)
    bias_quarters = bias_grads.reshape(2, 4, quarter)
    bias_rows = lambda first: ordered(left, bias_quarters[:, first], bias_quarters[:, first + 2], 1)
    flat = lambda table, bias: jnp.concatenate([table.reshape(-1), bias.reshape(-1)])
    small = flat(own_half(vector_grads, core), bias_rows(0)) + beside(
        flat(own_half(vector_grads, 1 - core), bias_rows(1))
    )
    small = small + over(small)
    count = vector_grads.shape[0]
    vector_out = small[: count * half].reshape(count, 1, half)
    bias_out = small[count * half :].reshape(2, 1, 2 * quarter)

    grad_attn = grad_middle.astype(BF16)
    grad_wo = lax.psum_scatter(
        dot_first(mixed, grad_attn).astype(BF16), "fsdp", scatter_dimension=0, tiled=True
    ).astype(F32)
    grad_wo = grad_wo + over(grad_wo)
    grad_mixed = dot_last(grad_attn, output_full).astype(BF16)
    part_of = lambda value, which: lax.dynamic_slice_in_dim(value, which * half, half, 1)
    grad_heads = ordered(left, part_of(grad_mixed, seq), over(part_of(grad_mixed, 1 - seq)), 0)
    parts = attention_backward(qkv, grad_heads, logs, size)
    grad_normed = dot_last(parts[0], qkv_weight[:, :half])
    grad_normed = grad_normed + dot_last(parts[1], qkv_weight[:, half : 2 * half])
    grad_normed = grad_normed + dot_last(parts[2], qkv_weight[:, 2 * half :])
    norm_sums = jnp.stack([jnp.sum(grad_normed * xhat, axis=0), jnp.sum(grad_normed, axis=0)], axis=1)
    packed = jnp.concatenate(
        [dot_first(normed, parts[i]).astype(BF16) for i in range(3)]
        + [jnp.pad(norm_sums, ((0, 0), (0, 126))).astype(BF16)],
        axis=1,
    )
    shard = lax.psum_scatter(packed, "fsdp", scatter_dimension=0, tiled=True)
    other_shard = over(shard)
    join = lambda which: ordered(
        left,
        shard[:, which * half : (which + 1) * half],
        other_shard[:, which * half : (which + 1) * half],
        1,
    ).astype(F32)
    norm_grads = shard[:, 3 * half : 3 * half + 2].astype(F32)
    norm_grads = norm_grads + other_shard[:, 3 * half : 3 * half + 2].astype(F32)
    arrived = over(block_of(grad_normed, 1 - seq).astype(BF16)).astype(F32)
    grad_own = block_of(grad_normed, seq) + arrived
    own_xhat, own_rate = normalised(rows.astype(F32))
    grad_inputs = grad_middle + norm_back(grad_own, own_xhat, own_rate, gain)
    return (
        layer_out[None],
        grad_inputs[None],
        norm_grads[:, 0],
        norm_grads[:, 1],
        join(0),
        join(1),
        join(2),
        grad_wo,
        vector_out[0],
        vector_out[1],
        grad_win_one[None],
        bias_out[0],
        grad_wout_one[None],
        vector_out[2],
        vector_out[3],
        vector_out[4],
        grad_win_two[None],
        bias_out[1],
        grad_wout_two[None],
        vector_out[5],
        vector_out[6],
    )


def solution(mesh):
    both, rows, vector = P("fsdp", "seq", None), P("fsdp", None), P("fsdp")
    return jax.shard_map(
        body,
        mesh=mesh,
        in_specs=(both, vector, vector, rows, rows, rows, rows)
        + (rows, rows, both, rows, both, rows) * 2
        + (rows, P("fsdp", "seq"), P("fsdp", "seq"), both),
        out_specs=(both, both, vector, vector, rows, rows, rows, rows)
        + (rows, rows, both, rows, both, rows) * 2
        + (rows,),
        check_vma=False,
    )
```

```python
import functools

import jax
import jax.numpy as jnp
from jax import lax
from jax.experimental import pallas as pl
from jax.experimental.pallas import tpu as pltpu
from jax.sharding import PartitionSpec as P

HEADS = 16
EPS = 1e-05
MASKED = -1e30
BLOCK = 256
CHUNK = 512
BF16 = jnp.bfloat16
F32 = jnp.float32
VMEM_LIMIT = 56 * 1024 * 1024


def swapped(value, axis):
    pairs = [(source, source ^ 1) for source in range(lax.axis_size(axis))]
    return lax.ppermute(value, axis, pairs)


def after(value, *others):
    return lax.optimization_barrier((value, *others))[0]


def dot_last(left, right):
    return lax.dot_general(left, right, (((1,), (1,)), ((), ())), preferred_element_type=F32)


def dot_first(left, right):
    return lax.dot_general(left, right, (((0,), (0,)), ((), ())), preferred_element_type=F32)


def dot(left, right):
    return jnp.dot(left, right, preferred_element_type=F32)


def normalised(values):
    centred = values - jnp.mean(values, axis=-1, keepdims=True)
    spread = jnp.mean(centred * centred, axis=-1, keepdims=True)
    rate = lax.rsqrt(spread + EPS)
    return centred * rate, rate


def norm_back(grad, xhat, rate, gain):
    scaled = grad * gain
    inner = jnp.mean(scaled * xhat, axis=-1, keepdims=True)
    return rate * (scaled - jnp.mean(scaled, axis=-1, keepdims=True) - xhat * inner)


def causal_mask(scores):
    keys = lax.broadcasted_iota(jnp.int32, scores.shape, 0)
    queries = lax.broadcasted_iota(jnp.int32, scores.shape, 1)
    return jnp.where(keys <= queries, scores, MASKED)


def attention_forward_kernel(size, q_ref, k_ref, v_ref, o_ref, log_ref):
    length = q_ref.shape[0]
    for head in range(q_ref.shape[1] // size):
        lanes = slice(head * size, (head + 1) * size)
        for start in range(0, length, BLOCK):
            query = q_ref[start : start + BLOCK, lanes] * BF16(size**-0.5)
            last = causal_mask(dot_last(k_ref[start : start + BLOCK, lanes], query))
            peak = jnp.max(last, axis=0, keepdims=True)
            if start:
                early = dot_last(k_ref[:start, lanes], query)
                peak = jnp.maximum(peak, jnp.max(early, axis=0, keepdims=True))
            last = jnp.exp(last - peak)
            total = jnp.sum(last, axis=0, keepdims=True)
            out = dot_first(v_ref[start : start + BLOCK, lanes], last.astype(BF16))
            if start:
                early = jnp.exp(early - peak)
                total = total + jnp.sum(early, axis=0, keepdims=True)
                out = out + dot_first(v_ref[:start, lanes], early.astype(BF16))
            o_ref[start : start + BLOCK, lanes] = (out / total).T.astype(BF16)
            log_ref[0, head : head + 1, start : start + BLOCK] = peak + jnp.log(total)


def attention_backward_kernel(size, q_ref, k_ref, v_ref, g_ref, log_ref, d_ref, dk_sum, dv_sum):
    length = q_ref.shape[0]
    scale = size**-0.5
    for head in range(q_ref.shape[1] // size):
        lanes = slice(head * size, (head + 1) * size)
        dk_sum[...] = jnp.zeros_like(dk_sum)
        dv_sum[...] = jnp.zeros_like(dv_sum)
        for start in range(0, length, BLOCK):
            rows = slice(start, start + BLOCK)
            query = q_ref[rows, lanes] * BF16(scale)
            grad = g_ref[rows, lanes]
            log_total = log_ref[0, head : head + 1, rows]
            spans = ([slice(0, start)] if start else []) + [rows]
            probs, weighted = [], []
            inner = jnp.zeros((1, BLOCK), F32)
            for span in spans:
                scores = dot_last(k_ref[span, lanes], query)
                if span is rows:
                    scores = causal_mask(scores)
                prob = jnp.exp(scores - log_total)
                grad_prob = dot_last(v_ref[span, lanes], grad)
                inner = inner + jnp.sum(prob * grad_prob, axis=0, keepdims=True)
                probs.append(prob)
                weighted.append(grad_prob)
            grad_query = jnp.zeros((BLOCK, size), F32)
            for span, prob, grad_prob in zip(spans, probs, weighted):
                low = (prob * (grad_prob - inner)).astype(BF16)
                dv_sum[span, :] += dot(prob.astype(BF16), grad)
                dk_sum[span, :] += dot(low, query)
                grad_query = grad_query + dot_first(low, k_ref[span, lanes])
            d_ref[0, rows, lanes] = (grad_query * scale).astype(BF16)
        d_ref[1, :, lanes] = dk_sum[...].astype(BF16)
        d_ref[2, :, lanes] = dv_sum[...].astype(BF16)


def attention_specs(length, half):
    parts = half // 128
    column = lambda which: pl.BlockSpec((length, 128), lambda i: (0, which * parts + i))
    return parts, column


def attention_forward(qkv, size):
    length, half = qkv.shape[0], qkv.shape[1] // 3
    parts, column = attention_specs(length, half)
    per = 128 // size
    return pl.pallas_call(
        functools.partial(attention_forward_kernel, size),
        grid=(parts,),
        out_shape=(
            jax.ShapeDtypeStruct((length, half), BF16),
            jax.ShapeDtypeStruct((parts, per, length), F32),
        ),
        in_specs=[column(0), column(1), column(2)],
        out_specs=(column(0), pl.BlockSpec((1, per, length), lambda i: (i, 0, 0))),
        compiler_params=pltpu.CompilerParams(vmem_limit_bytes=VMEM_LIMIT),
        cost_estimate=pl.CostEstimate(
            flops=8 * length * length * half, bytes_accessed=10 * length * half, transcendentals=0
        ),
        name="attention_forward",
    )(qkv, qkv, qkv)


def attention_backward(qkv, grad, logs, size):
    length, half = grad.shape
    parts, column = attention_specs(length, half)
    per = 128 // size
    return pl.pallas_call(
        functools.partial(attention_backward_kernel, size),
        grid=(parts,),
        out_shape=jax.ShapeDtypeStruct((3, length, half), BF16),
        in_specs=[
            column(0),
            column(1),
            column(2),
            column(0),
            pl.BlockSpec((1, per, length), lambda i: (i, 0, 0)),
        ],
        out_specs=pl.BlockSpec((3, length, 128), lambda i: (0, 0, i)),
        scratch_shapes=[pltpu.VMEM((length, size), F32), pltpu.VMEM((length, size), F32)],
        compiler_params=pltpu.CompilerParams(vmem_limit_bytes=VMEM_LIMIT),
        cost_estimate=pl.CostEstimate(
            flops=20 * length * length * half, bytes_accessed=16 * length * half, transcendentals=0
        ),
        name="attention_backward",
    )(qkv, qkv, qkv, grad, logs)


def stream(step, steps, pairs, buffers, sems):
    def fetch(which):
        slot = lax.rem(which, 2)
        for m, refs in enumerate(pairs):
            first = 0
            for ref in refs:
                count = ref.shape[0] // CHUNK

                @pl.when(jnp.logical_and(which >= first, which < first + count))
                def _(m=m, ref=ref, first=first):
                    row = pl.multiple_of((which - first) * CHUNK, CHUNK)
                    pltpu.make_async_copy(
                        ref.at[pl.ds(row, CHUNK)], buffers[m].at[slot], sems.at[m, slot]
                    ).start()

                first += count

    @pl.when(step == 0)
    def _():
        fetch(step)

    @pl.when(step + 1 < steps)
    def _():
        fetch(step + 1)

    slot = lax.rem(step, 2)
    for m, refs in enumerate(pairs):
        pltpu.make_async_copy(
            refs[0].at[pl.ds(0, CHUNK)], buffers[m].at[slot], sems.at[m, slot]
        ).wait()
    return slot


def gelu_parts(inner):
    cdf = 0.5 * (1.0 + lax.erf(inner * 0.7071067811865476))
    slope = cdf + inner * (jnp.exp(-0.5 * inner * inner) * 0.3989422804014327)
    return inner * cdf, slope


def forward_first_kernel(ins, count, steps, *refs):
    z_ref, gain_ref, shift_ref, out_bias_ref, gain_two, shift_two, bias_ref = refs[:7]
    win, wout = refs[7 : 7 + ins], refs[7 + ins : 7 + count]
    first_ref, normed_ref, active_ref, slope_ref, normed_two = refs[7 + count : 12 + count]
    in_buf, out_buf, sems = refs[12 + count :]
    step = pl.program_id(0)

    @pl.when(step == 0)
    def _():
        z = z_ref[...].astype(F32)
        xhat, _ = normalised(z)
        normed_ref[...] = (xhat * gain_ref[...] + shift_ref[...]).astype(BF16)
        first_ref[...] = jnp.broadcast_to(out_bias_ref[...], first_ref.shape)

    slot = stream(step, steps, (win, wout), (in_buf, out_buf), sems)
    active, slope = gelu_parts(dot_last(normed_ref[...], in_buf[slot]) + bias_ref[0])
    low = active.astype(BF16)
    active_ref[...] = low
    slope_ref[...] = slope.astype(BF16)
    first_ref[...] += dot(low, out_buf[slot])

    @pl.when(step == steps - 1)
    def _():
        xhat, _ = normalised(z_ref[...].astype(F32) + first_ref[...])
        normed_two[...] = (xhat * gain_two[...] + shift_two[...]).astype(BF16)


def forward_second_kernel(parts, steps, normed_ref, bias_ref, *refs):
    win, wout = refs[:parts], refs[parts : 2 * parts]
    part_ref, active_ref, slope_ref, total, in_buf, out_buf, sems = refs[2 * parts :]
    step = pl.program_id(0)

    @pl.when(step == 0)
    def _():
        total[...] = jnp.zeros_like(total)

    slot = stream(step, steps, (win, wout), (in_buf, out_buf), sems)
    active, slope = gelu_parts(dot_last(normed_ref[...], in_buf[slot]) + bias_ref[0])
    low = active.astype(BF16)
    active_ref[...] = low
    slope_ref[...] = slope.astype(BF16)
    total[...] += dot(low, out_buf[slot])

    @pl.when(step == steps - 1)
    def _():
        part_ref[...] = total[...].astype(part_ref.dtype)


def backward_second_kernel(parts, steps, grad_ref, slope_ref, *refs):
    win, wout = refs[:parts], refs[parts : 2 * parts]
    part_ref, inner_ref, total, in_buf, out_buf, sems = refs[2 * parts :]
    step = pl.program_id(0)

    @pl.when(step == 0)
    def _():
        total[...] = jnp.zeros_like(total)

    slot = stream(step, steps, (win, wout), (in_buf, out_buf), sems)
    inner = (slope_ref[...].astype(F32) * dot_last(grad_ref[...], out_buf[slot])).astype(BF16)
    inner_ref[...] = inner
    total[...] += dot(inner, in_buf[slot])

    @pl.when(step == steps - 1)
    def _():
        part_ref[...] = total[...].astype(part_ref.dtype)


def weights_second_kernel(parts, steps, *refs):
    inner, active, normed, grad = refs[:2], refs[2:4], refs[4:6], refs[6:8]
    bias_ref = refs[8]
    gwin, gwout = refs[9 : 9 + parts], refs[9 + parts : 9 + 2 * parts]
    step = pl.program_id(0)
    per = steps // parts
    one, two = inner[0][...], inner[1][...]
    bias_ref[0] = jnp.sum(one.astype(F32), axis=0, keepdims=True) + jnp.sum(
        two.astype(F32), axis=0, keepdims=True
    )
    grad_in = (dot_first(one, normed[0][...]) + dot_first(two, normed[1][...])).astype(BF16)
    grad_out = (
        dot_first(active[0][...], grad[0][...]) + dot_first(active[1][...], grad[1][...])
    ).astype(BF16)
    for quarter in range(parts):

        @pl.when(step // per == quarter)
        def _():
            gwin[quarter][...] = grad_in
            gwout[quarter][...] = grad_out


def backward_first_kernel(ins, count, parts, steps, *refs):
    own_ref, arrived_ref, grad_two_ref, z_ref, first_ref, cot_ref, score_ref = refs[:7]
    normed_ref, active_ref, slope_ref, gain_ref, gain_two, centre_ref = refs[7:13]
    win, wout = refs[13 : 13 + ins], refs[13 + ins : 13 + count]
    sent_ref, vector_ref, bias_ref = refs[13 + count : 16 + count]
    rest = refs[16 + count :]
    gwin, gwout = rest[:parts], rest[parts : 2 * parts]
    total, grad_in, grad_low, in_buf, out_buf, sems = rest[2 * parts :]
    step = pl.program_id(0)
    per = steps // parts
    down = lambda value: jnp.sum(value, axis=0, keepdims=True)

    @pl.when(step == 0)
    def _():
        total[...] = jnp.zeros_like(total)
        z = z_ref[...].astype(F32)
        xhat, rate = normalised(z + first_ref[...])
        grad_normed = own_ref[...] + arrived_ref[...].astype(F32)
        grad_rows = norm_back(grad_normed, xhat, rate, gain_two[...])
        grad_in[...] = grad_rows
        gate = jax.nn.sigmoid(jnp.sum(z * centre_ref[...], axis=-1, keepdims=True))
        low = (gate * cot_ref[...].astype(F32) + grad_rows).astype(BF16)
        grad_low[...] = low
        vector_ref[2:3] = down(low.astype(F32))
        vector_ref[3:4] = down(grad_normed * xhat)
        vector_ref[4:5] = down(grad_normed)
        vector_ref[5:6] = down(grad_two_ref[...].astype(F32))
        vector_ref[6:7] = down(score_ref[:, 0:1] * z)
        vector_ref[7:8] = jnp.zeros_like(vector_ref[7:8])

    slot = stream(step, steps, (win, wout), (in_buf, out_buf), sems)
    grad = grad_low[...]
    inner = (slope_ref[...].astype(F32) * dot_last(grad, out_buf[slot])).astype(BF16)
    bias_ref[0] = down(inner.astype(F32))
    total[...] += dot(inner, in_buf[slot])
    low_out = dot_first(active_ref[...], grad).astype(BF16)
    low_in = dot_first(inner, normed_ref[...]).astype(BF16)
    for quarter in range(parts):

        @pl.when(step // per == quarter)
        def _():
            gwin[quarter][...] = low_in
            gwout[quarter][...] = low_out

    @pl.when(step == steps - 1)
    def _():
        xhat, rate = normalised(z_ref[...].astype(F32))
        grad_normed = total[...]
        vector_ref[0:1] = down(grad_normed * xhat)
        vector_ref[1:2] = down(grad_normed)
        grad_rows = norm_back(grad_normed, xhat, rate, gain_ref[...])
        score = score_ref[:, 0:1]
        sent_ref[...] = (grad_in[...] + grad_rows + score * centre_ref[...]).astype(BF16)


def expert_call(kernel, name, steps, inputs, weights, outs, scratch, flops):
    whole = lambda shape: pl.BlockSpec(shape, lambda c: (0,) * len(shape))
    spec = lambda shape, block, at: whole(shape) if block is None else pl.BlockSpec(block, at)
    if weights:
        features = weights[0].shape[1]
        scratch = scratch + [
            pltpu.VMEM((2, CHUNK, features), BF16),
            pltpu.VMEM((2, CHUNK, features), BF16),
            pltpu.SemaphoreType.DMA((2, 2)),
        ]
    moved = sum(a.size * a.dtype.itemsize for a, _, _ in inputs + outs)
    return pl.pallas_call(
        kernel,
        grid=(steps,),
        out_shape=tuple(s for s, _, _ in outs),
        in_specs=[spec(a.shape, b, m) for a, b, m in inputs]
        + [pl.BlockSpec(memory_space=pl.ANY)] * len(weights),
        out_specs=tuple(spec(s.shape, b, m) for s, b, m in outs),
        scratch_shapes=scratch,
        compiler_params=pltpu.CompilerParams(vmem_limit_bytes=VMEM_LIMIT),
        cost_estimate=pl.CostEstimate(
            flops=2 * flops,
            bytes_accessed=moved + 2 * sum(w.size for w in weights),
            transcendentals=0,
        ),
        name=name,
    )(*[a for a, _, _ in inputs], *weights)


def expert(z, cot, vectors, biases, one, two, over):
    rows, features = z.shape
    hidden = biases.shape[1]
    steps = hidden // CHUNK
    near = steps // 2
    line = lambda i: (vectors[i : i + 1], None, None)
    flat = lambda array: (array, None, None)
    shape = jax.ShapeDtypeStruct
    low_rows, wide_rows = flat(shape((rows, features), BF16)), flat(shape((rows, features), F32))
    wide = ((rows, CHUNK), lambda c: (0, c))
    thin = ((1, 1, CHUNK), lambda c: (c, 0, 0))
    chunked = biases.reshape(2, steps, 1, CHUNK)
    matmul = 2 * rows * hidden * features

    def quarter_outs(parts, count):
        per = count // parts
        return [
            (
                shape((per * CHUNK, features), BF16),
                (CHUNK, features),
                lambda c, q=q: (jnp.clip(c - q * per, 0, per - 1), 0),
            )
            for q in range(parts)
        ]

    lines = [line(i) for i in range(7)]
    counts = len(one[0]), len(one[0]) + len(one[1])
    wide_z, wide_cot = z.astype(F32), cot.astype(F32)
    gate = jax.nn.sigmoid(jnp.sum(wide_z * vectors[6], axis=-1, keepdims=True))
    grad_two = (gate * wide_cot).astype(BF16)
    grad_far = over(grad_two)
    first, normed_one, active_one, slope_one, normed_two = expert_call(
        functools.partial(forward_first_kernel, *counts, steps),
        "forward_first",
        steps,
        [flat(z)] + lines[:5] + [(chunked[0], *thin)],
        one[0] + one[1],
        [wide_rows, low_rows] + [(shape((rows, hidden), BF16), *wide)] * 2 + [low_rows],
        [],
        2 * matmul,
    )
    normed_far = over(after(normed_two, grad_far))

    def forward_second(normed, kind):
        return expert_call(
            functools.partial(forward_second_kernel, 2, near),
            "forward_second",
            near,
            [flat(normed), (chunked[1, :near], *thin)],
            two[0] + two[1],
            [flat(shape((rows, features), kind))]
            + [(shape((rows, hidden // 2), BF16), *wide)] * 2,
            [pltpu.VMEM((rows, features), F32)],
            matmul,
        )

    def backward_second(grad, slope, kind):
        return expert_call(
            functools.partial(backward_second_kernel, 2, near),
            "backward_second",
            near,
            [flat(grad), (slope, *wide)],
            two[0] + two[1],
            [flat(shape((rows, features), kind)), (shape((rows, hidden // 2), BF16), *wide)],
            [pltpu.VMEM((rows, features), F32)],
            matmul,
        )

    own_part, active_own, slope_own = forward_second(normed_two, F32)
    far_part, active_far, slope_far = forward_second(normed_far, BF16)
    grad_far_part, inner_far = backward_second(grad_far, slope_far, BF16)
    grad_own_part, inner_own = backward_second(grad_two, slope_own, F32)
    outs = expert_call(
        functools.partial(weights_second_kernel, 2, near),
        "weights_second",
        near,
        [(a, *wide) for a in (inner_own, inner_far, active_own, active_far)]
        + [flat(a) for a in (normed_two, normed_far, grad_two, grad_far)],
        [],
        [(shape((near, 1, CHUNK), F32), *thin)] + quarter_outs(2, near) + quarter_outs(2, near),
        [],
        2 * matmul,
    )
    bias_two, gwin_two, gwout_two = outs[0].reshape(hidden // 2), outs[1:3], outs[3:5]

    branch = first + (own_part + over(far_part).astype(F32) + vectors[5])
    gated = (gate * branch).astype(BF16)
    grad_gate = jnp.sum(wide_cot * branch, axis=-1, keepdims=True)
    score = jnp.broadcast_to(grad_gate * gate * (1.0 - gate), (rows, 128))

    grad_arrived = after(over(grad_far_part), outs[0])
    outs = expert_call(
        functools.partial(backward_first_kernel, *counts, 4, steps),
        "backward_first",
        steps,
        [flat(a) for a in (grad_own_part, grad_arrived, grad_two, z, first, cot, score)]
        + [flat(normed_one), (active_one, *wide), (slope_one, *wide)]
        + [line(0), line(3), line(6)],
        one[0] + one[1],
        [low_rows, flat(shape((8, features), F32)), (shape((steps, 1, CHUNK), F32), *thin)]
        + quarter_outs(4, steps)
        + quarter_outs(4, steps),
        [
            pltpu.VMEM((rows, features), F32),
            pltpu.VMEM((rows, features), F32),
            pltpu.VMEM((rows, features), BF16),
        ],
        4 * matmul,
    )
    grad_sent, sums, bias_one = outs[0], outs[1], outs[2].reshape(hidden)
    return gated, grad_sent, sums[:7], bias_one, bias_two, (outs[3:7], outs[7:11]), (gwin_two, gwout_two)


def body(
    inputs,
    ln_gain,
    ln_shift,
    w_query,
    w_key,
    w_value,
    w_output,
    exp_gain1,
    exp_shift1,
    w_in1,
    b_in1,
    w_out1,
    b_out1,
    exp_gain2,
    exp_shift2,
    w_in2,
    b_in2,
    w_out2,
    b_out2,
    centroid,
    order,
    inverse,
    cotangent,
):
    seq, peer = lax.axis_index("seq"), lax.axis_index("fsdp")
    peers = lax.axis_size("fsdp")
    rows = inputs[0]
    tokens, features = rows.shape
    half = features // 2
    size = features // HEADS
    left, even = seq == 0, lax.rem(peer, 2) == 0
    over = lambda value: swapped(value, "seq")
    beside = lambda value: swapped(value, "fsdp")
    ordered = lambda flag, mine, other, axis: jnp.where(
        flag, jnp.concatenate([mine, other], axis), jnp.concatenate([other, mine], axis)
    )

    other_rows = over(rows)
    columns = lambda w: lax.dynamic_slice_in_dim(w, seq * half, half, 1)
    norm_vectors = jnp.pad(jnp.stack([ln_gain, ln_shift], axis=1), ((0, 0), (0, 126)))
    gathered = lax.all_gather(
        jnp.concatenate([columns(w_query), columns(w_key), columns(w_value), norm_vectors], axis=1),
        "fsdp",
        axis=0,
        tiled=True,
    )
    output_full = lax.all_gather(w_output, "fsdp", axis=0, tiled=True)
    own_vectors = jnp.concatenate(
        [exp_gain1, exp_shift1, b_out1, exp_gain2, exp_shift2, b_out2, centroid], axis=0
    )
    own_biases = jnp.concatenate([b_in1, b_in2], axis=0)
    pair = beside(jnp.concatenate([own_vectors.reshape(-1), own_biases.reshape(-1)]))
    other_vectors = pair[: own_vectors.size].reshape(own_vectors.shape)
    other_biases = pair[own_vectors.size :].reshape(own_biases.shape)
    vectors = ordered(even, own_vectors, other_vectors, 1).astype(F32)

    quarter = w_in1.shape[1]
    pick = lambda table, which: lax.dynamic_slice_in_dim(table, which * quarter, quarter, 1)
    biases = jnp.concatenate(
        [
            pick(own_biases, seq),
            pick(other_biases, seq),
            pick(own_biases, 1 - seq),
            pick(other_biases, 1 - seq),
        ],
        axis=1,
    ).astype(F32)

    def holders(mine, far):
        return [mine, beside(mine), far, beside(far)]

    far_in = over(after(w_in1[0], other_rows))
    far_out = over(after(w_out1[0], far_in))
    one = (holders(w_in1[0], far_in), holders(w_out1[0], far_out))
    two = ([w_in2[0], beside(w_in2[0])], [w_out2[0], beside(w_out2[0])])
    cot = cotangent[0]
    exchange = lambda value: lax.all_to_all(
        value.reshape(peers, tokens // peers, features),
        "fsdp",
        split_axis=0,
        concat_axis=0,
        tiled=True,
    ).reshape(tokens, features)
    cot_slots = exchange(jnp.take(cot, order[0], axis=0))

    gathered = after(gathered, cot_slots)

    sequence = ordered(left, rows, other_rows, 0).astype(F32)
    gain, shift = gathered[:, 3 * half].astype(F32), gathered[:, 3 * half + 1].astype(F32)
    xhat, rate = normalised(sequence)
    normed = (xhat * gain + shift).astype(BF16)
    qkv_weight = gathered[:, : 3 * half]
    qkv = dot(normed, qkv_weight).astype(BF16)
    qkv = after(qkv, far_in)
    mixed_heads, logs = attention_forward(qkv, size)
    block_of = lambda value, which: lax.dynamic_slice_in_dim(value, which * tokens, tokens, 0)
    other_mixed = over(block_of(mixed_heads, 1 - seq))
    mixed = ordered(left, block_of(mixed_heads, seq), other_mixed, 1)
    middle = rows.astype(F32) + dot(mixed, output_full)

    z = exchange(after(jnp.take(middle.astype(BF16), order[0], axis=0), far_out))
    gated, grad_sent, vector_grads, bias_one, bias_two, grads_one, grads_two = expert(
        z, cot_slots, vectors, biases, one, two, over
    )
    home = jnp.take(exchange(gated), inverse[0], axis=0)
    layer_out = (middle + home.astype(F32)).astype(BF16)
    add = lambda *values: sum(value.astype(F32) for value in values)
    cut = quarter // 2
    far_sums = []
    for _, _, far, cross in grads_one:
        near = beside(cross)
        far_sums += [add(far[at : at + cut], near[at : at + cut]).astype(BF16) for at in (0, cut)]
    coming = jnp.take(after(exchange(grad_sent), *far_sums), inverse[0], axis=0)
    grads_far = [over(far_sums[0])]
    grad_middle = cot.astype(F32) + coming.astype(F32)

    grad_win_two, grad_wout_two = [
        mine.astype(F32) + beside(near).astype(F32) for mine, near in grads_two
    ]

    own_half = lambda table, which: lax.dynamic_slice_in_dim(table, which * half, half, 1)
    core = lax.rem(peer, 2)
    bias_quarters = jnp.stack(
        [bias_one, jnp.concatenate([bias_two, jnp.zeros_like(bias_two)])]
    ).reshape(2, 4, quarter)
    bias_rows = lambda first: ordered(left, bias_quarters[:, first], bias_quarters[:, first + 2], 1)
    flat = lambda table, bias: jnp.concatenate([table.reshape(-1), bias.reshape(-1)])
    small = flat(own_half(vector_grads, core), bias_rows(0)) + beside(
        flat(own_half(vector_grads, 1 - core), bias_rows(1))
    )
    small = small + over(small)
    count = vector_grads.shape[0]
    vector_out = small[: count * half].reshape(count, 1, half)
    bias_out = small[count * half :].reshape(2, 1, 2 * quarter)

    grad_attn = grad_middle.astype(BF16)
    grad_wo = lax.psum_scatter(
        dot_first(mixed, grad_attn).astype(BF16), "fsdp", scatter_dimension=0, tiled=True
    ).astype(F32)
    grad_wo = grad_wo + over(grad_wo)
    grad_mixed = dot_last(grad_attn, output_full).astype(BF16)
    part_of = lambda value, which: lax.dynamic_slice_in_dim(value, which * half, half, 1)
    other_grad = over(after(part_of(grad_mixed, 1 - seq), grads_far[0]))
    grad_heads = ordered(left, part_of(grad_mixed, seq), other_grad, 0)
    for value in far_sums[1:]:
        grads_far.append(over(after(value, other_grad, grads_far[-1])))
    grad_win_one, grad_wout_one = [
        add(g[0], beside(g[1]), jnp.concatenate(grads_far[i : i + 2], axis=0))
        for g, i in zip(grads_one, (0, 2))
    ]
    parts = after(attention_backward(qkv, grad_heads, logs, size), grads_far[1])
    grad_normed = dot_last(parts[0], qkv_weight[:, :half])
    grad_normed = grad_normed + dot_last(parts[1], qkv_weight[:, half : 2 * half])
    grad_normed = grad_normed + dot_last(parts[2], qkv_weight[:, 2 * half :])
    norm_sums = jnp.stack([jnp.sum(grad_normed * xhat, axis=0), jnp.sum(grad_normed, axis=0)], axis=1)
    packed = jnp.concatenate(
        [dot_first(normed, parts[i]).astype(BF16) for i in range(3)]
        + [jnp.pad(norm_sums, ((0, 0), (0, 126))).astype(BF16)],
        axis=1,
    )
    packed = after(packed, grads_far[2])
    shard = lax.psum_scatter(packed, "fsdp", scatter_dimension=0, tiled=True)
    other_shard = over(shard)
    join = lambda which: ordered(
        left,
        shard[:, which * half : (which + 1) * half],
        other_shard[:, which * half : (which + 1) * half],
        1,
    ).astype(F32)
    norm_grads = shard[:, 3 * half : 3 * half + 2].astype(F32)
    norm_grads = norm_grads + other_shard[:, 3 * half : 3 * half + 2].astype(F32)
    arrived = over(block_of(grad_normed, 1 - seq).astype(BF16)).astype(F32)
    arrived = after(arrived, grads_far[3])
    grad_own = block_of(grad_normed, seq) + arrived
    own_xhat, own_rate = normalised(rows.astype(F32))
    grad_inputs = grad_middle + norm_back(grad_own, own_xhat, own_rate, gain)
    return (
        layer_out[None],
        grad_inputs[None],
        norm_grads[:, 0],
        norm_grads[:, 1],
        join(0),
        join(1),
        join(2),
        grad_wo,
        vector_out[0],
        vector_out[1],
        grad_win_one[None],
        bias_out[0],
        grad_wout_one[None],
        vector_out[2],
        vector_out[3],
        vector_out[4],
        grad_win_two[None],
        bias_out[1],
        grad_wout_two[None],
        vector_out[5],
        vector_out[6],
    )


def solution(mesh):
    both, rows, vector = P("fsdp", "seq", None), P("fsdp", None), P("fsdp")
    return jax.shard_map(
        body,
        mesh=mesh,
        in_specs=(both, vector, vector, rows, rows, rows, rows)
        + (rows, rows, both, rows, both, rows) * 2
        + (rows, P("fsdp", "seq"), P("fsdp", "seq"), both),
        out_specs=(both, both, vector, vector, rows, rows, rows, rows)
        + (rows, rows, both, rows, both, rows) * 2
        + (rows,),
        check_vma=False,
    )
```

```python
import functools

import jax
import jax.numpy as jnp
from jax import lax
from jax.experimental import pallas as pl
from jax.experimental.pallas import tpu as pltpu
from jax.sharding import PartitionSpec as P

HEADS = 16
EPS = 1e-05
MASKED = -1e30
BLOCK = 256
CHUNK = 512
BF16 = jnp.bfloat16
F32 = jnp.float32
VMEM_LIMIT = 56 * 1024 * 1024
MESH = pl.DeviceIdType.MESH


def swapped(value, axis):
    pairs = [(source, source ^ 1) for source in range(lax.axis_size(axis))]
    return lax.ppermute(value, axis, pairs)


def after(value, *others):
    return lax.optimization_barrier((value, *others))[0]


def dot_last(left, right):
    return lax.dot_general(left, right, (((1,), (1,)), ((), ())), preferred_element_type=F32)


def dot_first(left, right):
    return lax.dot_general(left, right, (((0,), (0,)), ((), ())), preferred_element_type=F32)


def dot(left, right):
    return jnp.dot(left, right, preferred_element_type=F32)


def normalised(values):
    centred = values - jnp.mean(values, axis=-1, keepdims=True)
    spread = jnp.mean(centred * centred, axis=-1, keepdims=True)
    rate = lax.rsqrt(spread + EPS)
    return centred * rate, rate


def norm_back(grad, xhat, rate, gain):
    scaled = grad * gain
    inner = jnp.mean(scaled * xhat, axis=-1, keepdims=True)
    return rate * (scaled - jnp.mean(scaled, axis=-1, keepdims=True) - xhat * inner)


def bits_of(peers):
    return peers.bit_length() - 1


def greet(partners):
    barrier = pltpu.get_barrier_semaphore()
    for device in partners:
        pl.semaphore_signal(barrier, inc=1, device_id=device, device_id_type=MESH)
    pl.semaphore_wait(barrier, len(partners))


def remote(source, target, sends, recvs, device):
    return pltpu.make_async_remote_copy(
        src_ref=source,
        dst_ref=target,
        send_sem=sends,
        recv_sem=recvs,
        device_id=device,
        device_id_type=MESH,
    )


class Halving:
    def __init__(self, peers, held, landed, sends, recvs):
        peer = lax.axis_index("fsdp")
        self.stages = bits_of(peers)
        self.bit = [lax.rem(peer // (1 << s), 2) for s in range(self.stages)]
        self.partner = [
            {"fsdp": peer + (1 - 2 * self.bit[s]) * (1 << s)} for s in range(self.stages)
        ]
        self.held, self.landed, self.sends, self.recvs = held, landed, sends, recvs

    def copy(self, chunk, s):
        return remote(
            self.held[chunk][s].at[:, 1 - self.bit[s]],
            self.landed[chunk][s],
            self.sends.at[chunk, s],
            self.recvs.at[chunk, s],
            self.partner[s],
        )

    def start(self, chunk):
        self.copy(chunk, 0).start()

    def put(self, chunk, value):
        self.held[chunk][0][...] = value.astype(BF16).reshape(self.held[chunk][0].shape)
        self.start(chunk)

    def finish(self, chunk, s):
        self.copy(chunk, s).wait_recv()
        total = self.held[chunk][s][:, self.bit[s]].astype(F32)
        total = total + self.landed[chunk][s][...].astype(F32)
        if s + 1 < self.stages:
            held = self.held[chunk][s + 1]
            held[...] = total.astype(BF16).reshape(held.shape)
            self.copy(chunk, s + 1).start()
        return total[0]

    def drain(self, chunks):
        for chunk in range(chunks):
            for s in range(self.stages):
                self.copy(chunk, s).wait_send()


def halving_buffers(peers, rows, widths, first=True):
    stages = bits_of(peers)
    held = [
        pltpu.VMEM((peers >> (s + 1), 2, rows, w), BF16)
        for w in widths
        for s in range(0 if first else 1, stages)
    ]
    landed = [pltpu.VMEM((peers >> (s + 1), rows, w), BF16) for w in widths for s in range(stages)]
    return held + landed + [pltpu.SemaphoreType.DMA((len(widths), stages))] * 2


def causal_mask(scores):
    keys = lax.broadcasted_iota(jnp.int32, scores.shape, 0)
    queries = lax.broadcasted_iota(jnp.int32, scores.shape, 1)
    return jnp.where(keys <= queries, scores, MASKED)


def attention_forward_kernel(size, q_ref, k_ref, v_ref, o_ref, log_ref):
    length = q_ref.shape[0]
    for head in range(q_ref.shape[1] // size):
        lanes = slice(head * size, (head + 1) * size)
        for start in range(0, length, BLOCK):
            query = q_ref[start : start + BLOCK, lanes] * BF16(size**-0.5)
            last = causal_mask(dot_last(k_ref[start : start + BLOCK, lanes], query))
            peak = jnp.max(last, axis=0, keepdims=True)
            if start:
                early = dot_last(k_ref[:start, lanes], query)
                peak = jnp.maximum(peak, jnp.max(early, axis=0, keepdims=True))
            last = jnp.exp(last - peak)
            total = jnp.sum(last, axis=0, keepdims=True)
            out = dot_first(v_ref[start : start + BLOCK, lanes], last.astype(BF16))
            if start:
                early = jnp.exp(early - peak)
                total = total + jnp.sum(early, axis=0, keepdims=True)
                out = out + dot_first(v_ref[:start, lanes], early.astype(BF16))
            o_ref[start : start + BLOCK, lanes] = (out / total).T.astype(BF16)
            log_ref[0, head : head + 1, start : start + BLOCK] = peak + jnp.log(total)


def attention_backward_kernel(peers, size, *refs):
    q_ref, k_ref, v_ref, g_ref, log_ref, term_ref, d_ref, sum_ref, dk_sum, dv_sum = refs[:10]
    stages = bits_of(peers)
    held = [[term_ref, *refs[10 : 9 + stages]]]
    landed = [refs[9 + stages : 9 + 2 * stages]]
    reducer = Halving(peers, held, landed, *refs[9 + 2 * stages :])
    step, steps = pl.program_id(0), 4

    @pl.when(step == 0)
    def _():
        greet(reducer.partner)
        reducer.start(0)

    for s in range(stages - 1):

        @pl.when(step == min(1 + s, steps - 1))
        def _():
            reducer.finish(0, s)

    length = q_ref.shape[0]
    scale = size**-0.5
    for head in range(q_ref.shape[1] // size):
        lanes = slice(head * size, (head + 1) * size)
        dk_sum[...] = jnp.zeros_like(dk_sum)
        dv_sum[...] = jnp.zeros_like(dv_sum)
        for start in range(0, length, BLOCK):
            rows = slice(start, start + BLOCK)
            query = q_ref[rows, lanes] * BF16(scale)
            grad = g_ref[rows, lanes]
            log_total = log_ref[0, head : head + 1, rows]
            spans = ([slice(0, start)] if start else []) + [rows]
            probs, weighted = [], []
            inner = jnp.zeros((1, BLOCK), F32)
            for span in spans:
                scores = dot_last(k_ref[span, lanes], query)
                if span is rows:
                    scores = causal_mask(scores)
                prob = jnp.exp(scores - log_total)
                grad_prob = dot_last(v_ref[span, lanes], grad)
                inner = inner + jnp.sum(prob * grad_prob, axis=0, keepdims=True)
                probs.append(prob)
                weighted.append(grad_prob)
            grad_query = jnp.zeros((BLOCK, size), F32)
            for span, prob, grad_prob in zip(spans, probs, weighted):
                low = (prob * (grad_prob - inner)).astype(BF16)
                dv_sum[span, :] += dot(prob.astype(BF16), grad)
                dk_sum[span, :] += dot(low, query)
                grad_query = grad_query + dot_first(low, k_ref[span, lanes])
            d_ref[0, rows, lanes] = (grad_query * scale).astype(BF16)
        d_ref[1, :, lanes] = dk_sum[...].astype(BF16)
        d_ref[2, :, lanes] = dv_sum[...].astype(BF16)


    @pl.when(step == steps - 1)
    def _():
        sum_ref[...] = reducer.finish(0, stages - 1)
        reducer.drain(1)


def attention_specs(length, half):
    parts = half // 128
    column = lambda which: pl.BlockSpec((length, 128), lambda i: (0, which * parts + i))
    return parts, column


def attention_forward(qkv, size):
    length, half = qkv.shape[0], qkv.shape[1] // 3
    parts, column = attention_specs(length, half)
    per = 128 // size
    return pl.pallas_call(
        functools.partial(attention_forward_kernel, size),
        grid=(parts,),
        out_shape=(
            jax.ShapeDtypeStruct((length, half), BF16),
            jax.ShapeDtypeStruct((parts, per, length), F32),
        ),
        in_specs=[column(0), column(1), column(2)],
        out_specs=(column(0), pl.BlockSpec((1, per, length), lambda i: (i, 0, 0))),
        compiler_params=pltpu.CompilerParams(vmem_limit_bytes=VMEM_LIMIT),
        cost_estimate=pl.CostEstimate(
            flops=8 * length * length * half, bytes_accessed=10 * length * half, transcendentals=0
        ),
        name="attention_forward",
    )(qkv, qkv, qkv)


def attention_backward(peers, qkv, grad, logs, terms, size):
    length, half = grad.shape
    parts, column = attention_specs(length, half)
    per = 128 // size
    rows, width = terms.shape[0] // peers, terms.shape[1]
    blocks = (peers // 2, 2, rows, width)
    shape = jax.ShapeDtypeStruct
    return pl.pallas_call(
        functools.partial(attention_backward_kernel, peers, size),
        grid=(parts,),
        out_shape=(shape((3, length, half), BF16), shape((rows, width), F32)),
        in_specs=[
            column(0),
            column(1),
            column(2),
            column(0),
            pl.BlockSpec((1, per, length), lambda i: (i, 0, 0)),
            pl.BlockSpec(blocks, lambda i: (0, 0, 0, 0)),
        ],
        out_specs=(
            pl.BlockSpec((3, length, 128), lambda i: (0, 0, i)),
            pl.BlockSpec((rows, width), lambda i: (0, 0)),
        ),
        scratch_shapes=[pltpu.VMEM((length, size), F32), pltpu.VMEM((length, size), F32)]
        + halving_buffers(peers, rows, [width], first=False),
        compiler_params=pltpu.CompilerParams(
            vmem_limit_bytes=VMEM_LIMIT, collective_id=1, has_side_effects=True
        ),
        cost_estimate=pl.CostEstimate(
            flops=20 * length * length * half, bytes_accessed=16 * length * half, transcendentals=0
        ),
        name="attention_backward",
    )(qkv, qkv, qkv, grad, logs, terms.reshape(blocks))


def stream(step, steps, pairs, buffers, sems):
    def fetch(which):
        slot = lax.rem(which, 2)
        for m, refs in enumerate(pairs):
            first = 0
            for ref in refs:
                count = ref.shape[0] // CHUNK

                @pl.when(jnp.logical_and(which >= first, which < first + count))
                def _(m=m, ref=ref, first=first):
                    row = pl.multiple_of((which - first) * CHUNK, CHUNK)
                    pltpu.make_async_copy(
                        ref.at[pl.ds(row, CHUNK)], buffers[m].at[slot], sems.at[m, slot]
                    ).start()

                first += count

    @pl.when(step == 0)
    def _():
        fetch(step)

    @pl.when(step + 1 < steps)
    def _():
        fetch(step + 1)

    slot = lax.rem(step, 2)
    for m, refs in enumerate(pairs):
        pltpu.make_async_copy(
            refs[0].at[pl.ds(0, CHUNK)], buffers[m].at[slot], sems.at[m, slot]
        ).wait()
    return slot


def gelu_parts(inner):
    cdf = 0.5 * (1.0 + lax.erf(inner * 0.7071067811865476))
    slope = cdf + inner * (jnp.exp(-0.5 * inner * inner) * 0.3989422804014327)
    return inner * cdf, slope


def forward_first_kernel(steps, *refs):
    z_ref, gain_ref, shift_ref, out_bias_ref, gain_two, shift_two, bias_ref = refs[:7]
    win, wout = refs[7:11], refs[11:15]
    first_ref, normed_ref, active_ref, slope_ref, normed_two = refs[15:20]
    in_buf, out_buf, sems = refs[20:]
    step = pl.program_id(0)

    @pl.when(step == 0)
    def _():
        z = z_ref[...].astype(F32)
        xhat, _ = normalised(z)
        normed_ref[...] = (xhat * gain_ref[...] + shift_ref[...]).astype(BF16)
        first_ref[...] = jnp.broadcast_to(out_bias_ref[...], first_ref.shape)

    slot = stream(step, steps, (win, wout), (in_buf, out_buf), sems)
    active, slope = gelu_parts(dot_last(normed_ref[...], in_buf[slot]) + bias_ref[0])
    low = active.astype(BF16)
    slope_ref[...] = slope.astype(BF16)
    first_ref[...] += dot(low, out_buf[slot])

    @pl.when(step < steps // 2)
    def _():
        active_ref[...] = low

    @pl.when(step == steps - 1)
    def _():
        xhat, _ = normalised(z_ref[...].astype(F32) + first_ref[...])
        normed_two[...] = (xhat * gain_two[...] + shift_two[...]).astype(BF16)


def forward_second_kernel(parts, steps, normed_ref, bias_ref, *refs):
    win, wout = refs[:parts], refs[parts : 2 * parts]
    part_ref, active_ref, slope_ref, total, in_buf, out_buf, sems = refs[2 * parts :]
    step = pl.program_id(0)

    @pl.when(step == 0)
    def _():
        total[...] = jnp.zeros_like(total)

    slot = stream(step, steps, (win, wout), (in_buf, out_buf), sems)
    active, slope = gelu_parts(dot_last(normed_ref[...], in_buf[slot]) + bias_ref[0])
    low = active.astype(BF16)
    active_ref[...] = low
    slope_ref[...] = slope.astype(BF16)
    total[...] += dot(low, out_buf[slot])

    @pl.when(step == steps - 1)
    def _():
        part_ref[...] = total[...].astype(part_ref.dtype)


def backward_second_kernel(parts, steps, grad_ref, slope_ref, *refs):
    win, wout = refs[:parts], refs[parts : 2 * parts]
    part_ref, inner_ref, total, in_buf, out_buf, sems = refs[2 * parts :]
    step = pl.program_id(0)

    @pl.when(step == 0)
    def _():
        total[...] = jnp.zeros_like(total)

    slot = stream(step, steps, (win, wout), (in_buf, out_buf), sems)
    inner = (slope_ref[...].astype(F32) * dot_last(grad_ref[...], out_buf[slot])).astype(BF16)
    inner_ref[...] = inner
    total[...] += dot(inner, in_buf[slot])

    @pl.when(step == steps - 1)
    def _():
        part_ref[...] = total[...].astype(part_ref.dtype)


def weights_second_kernel(parts, steps, *refs):
    inner, active, normed, grad = refs[:2], refs[2:4], refs[4:6], refs[6:8]
    bias_ref = refs[8]
    gwin, gwout = refs[9 : 9 + parts], refs[9 + parts : 9 + 2 * parts]
    step = pl.program_id(0)
    per = steps // parts
    one, two = inner[0][...], inner[1][...]
    bias_ref[0] = jnp.sum(one.astype(F32), axis=0, keepdims=True) + jnp.sum(
        two.astype(F32), axis=0, keepdims=True
    )
    grad_in = (dot_first(one, normed[0][...]) + dot_first(two, normed[1][...])).astype(BF16)
    grad_out = (
        dot_first(active[0][...], grad[0][...]) + dot_first(active[1][...], grad[1][...])
    ).astype(BF16)
    for quarter in range(parts):

        @pl.when(step // per == quarter)
        def _():
            gwin[quarter][...] = grad_in
            gwout[quarter][...] = grad_out


def backward_first_kernel(steps, *refs):
    own_ref, arrived_ref, grad_two_ref, z_ref, first_ref, cot_ref = refs[:6]
    slope_ref, gain_ref, gain_two, centre_ref = refs[6:10]
    win, wout = refs[10:14], refs[14:18]
    back_ref, grad_low, vector_ref, inner_ref = refs[18:22]
    total, in_buf, out_buf, sems = refs[22:]
    step = pl.program_id(0)
    down = lambda value: jnp.sum(value, axis=0, keepdims=True)

    @pl.when(step == 0)
    def _():
        total[...] = jnp.zeros_like(total)
        z = z_ref[...].astype(F32)
        xhat, rate = normalised(z + first_ref[...])
        grad_normed = own_ref[...] + arrived_ref[...].astype(F32)
        grad_rows = norm_back(grad_normed, xhat, rate, gain_two[...])
        back_ref[...] = grad_rows
        gate = jax.nn.sigmoid(jnp.sum(z * centre_ref[...], axis=-1, keepdims=True))
        low = (gate * cot_ref[...].astype(F32) + grad_rows).astype(BF16)
        grad_low[...] = low
        vector_ref[2:3] = down(low.astype(F32))
        vector_ref[3:4] = down(grad_normed * xhat)
        vector_ref[4:5] = down(grad_normed)
        vector_ref[5:6] = down(grad_two_ref[...].astype(F32))
        vector_ref[6:8] = jnp.zeros_like(vector_ref[6:8])

    slot = stream(step, steps, (win, wout), (in_buf, out_buf), sems)
    inner = (slope_ref[...].astype(F32) * dot_last(grad_low[...], out_buf[slot])).astype(BF16)
    total[...] += dot(inner, in_buf[slot])

    @pl.when(step < steps // 2)
    def _():
        inner_ref[...] = inner

    @pl.when(step == steps - 1)
    def _():
        xhat, rate = normalised(z_ref[...].astype(F32))
        grad_normed = total[...]
        vector_ref[0:1] = down(grad_normed * xhat)
        vector_ref[1:2] = down(grad_normed)
        back_ref[...] += norm_back(grad_normed, xhat, rate, gain_ref[...])


def weights_first_kernel(steps, *refs):
    inner_ref, active_ref, normed_ref, grad_ref, normed_far, grad_far, in_bias = refs[:7]
    win, wout = refs[7:9], refs[9:11]
    bias_ref, gwin, gwout, in_buf, out_buf, sems = refs[11], refs[12:14], refs[14:16], *refs[16:]
    step = pl.program_id(0)
    slot = stream(step, steps, (win, wout), (in_buf, out_buf), sems)
    active, slope = gelu_parts(dot_last(normed_far[...], in_buf[slot]) + in_bias[0])
    inner = (slope * dot_last(grad_far[...], out_buf[slot])).astype(BF16)
    own = inner_ref[...]
    bias_ref[0] = jnp.sum(own.astype(F32), axis=0, keepdims=True) + jnp.sum(
        inner.astype(F32), axis=0, keepdims=True
    )
    grad_in = (dot_first(own, normed_ref[...]) + dot_first(inner, normed_far[...])).astype(BF16)
    grad_out = (
        dot_first(active_ref[...], grad_ref[...]) + dot_first(active.astype(BF16), grad_far[...])
    ).astype(BF16)
    for quarter in range(2):

        @pl.when(step // (steps // 2) == quarter)
        def _():
            gwin[quarter][...] = grad_in
            gwout[quarter][...] = grad_out


def expert_call(kernel, name, steps, inputs, weights, outs, scratch, flops):
    whole = lambda shape: pl.BlockSpec(shape, lambda c: (0,) * len(shape))
    spec = lambda shape, block, at: whole(shape) if block is None else pl.BlockSpec(block, at)
    if weights:
        features = weights[0].shape[1]
        scratch = scratch + [
            pltpu.VMEM((2, CHUNK, features), BF16),
            pltpu.VMEM((2, CHUNK, features), BF16),
            pltpu.SemaphoreType.DMA((2, 2)),
        ]
    moved = sum(a.size * a.dtype.itemsize for a, _, _ in inputs + outs)
    return pl.pallas_call(
        kernel,
        grid=(steps,),
        out_shape=tuple(s for s, _, _ in outs),
        in_specs=[spec(a.shape, b, m) for a, b, m in inputs]
        + [pl.BlockSpec(memory_space=pl.ANY)] * len(weights),
        out_specs=tuple(spec(s.shape, b, m) for s, b, m in outs),
        scratch_shapes=scratch,
        compiler_params=pltpu.CompilerParams(vmem_limit_bytes=VMEM_LIMIT),
        cost_estimate=pl.CostEstimate(
            flops=2 * flops,
            bytes_accessed=moved + 2 * sum(w.size for w in weights),
            transcendentals=0,
        ),
        name=name,
    )(*[a for a, _, _ in inputs], *weights)


def expert(z, cot, vectors, biases, one, two, over):
    rows, features = z.shape
    hidden = biases.shape[1]
    steps = hidden // CHUNK
    near = steps // 2
    line = lambda i: (vectors[i : i + 1], None, None)
    flat = lambda array: (array, None, None)
    shape = jax.ShapeDtypeStruct
    low_rows, wide_rows = flat(shape((rows, features), BF16)), flat(shape((rows, features), F32))
    wide = ((rows, CHUNK), lambda c: (0, c))
    thin = ((1, 1, CHUNK), lambda c: (c, 0, 0))
    chunked = biases.reshape(2, steps, 1, CHUNK)
    matmul = 2 * rows * hidden * features

    def quarter_outs(parts, count):
        per = count // parts
        return [
            (
                shape((per * CHUNK, features), BF16),
                (CHUNK, features),
                lambda c, q=q: (jnp.clip(c - q * per, 0, per - 1), 0),
            )
            for q in range(parts)
        ]

    lines = [line(i) for i in range(7)]
    held = ((rows, CHUNK), lambda c: (0, jnp.minimum(c, near - 1)))
    half_hidden = shape((rows, hidden // 2), BF16)
    wide_z, wide_cot = z.astype(F32), cot.astype(F32)
    gate = jax.nn.sigmoid(jnp.sum(wide_z * vectors[6], axis=-1, keepdims=True))
    grad_two = (gate * wide_cot).astype(BF16)
    grad_far = over(grad_two)
    first, normed_one, active_one, slope_one, normed_two = expert_call(
        functools.partial(forward_first_kernel, steps),
        "forward_first",
        steps,
        [flat(z)] + lines[:5] + [(chunked[0], *thin)],
        one[0] + one[1],
        [wide_rows, low_rows, (half_hidden, *held), (shape((rows, hidden), BF16), *wide), low_rows],
        [],
        2 * matmul,
    )
    normed_far = over(after(normed_two, grad_far))

    def forward_second(normed, kind):
        return expert_call(
            functools.partial(forward_second_kernel, 2, near),
            "forward_second",
            near,
            [flat(normed), (chunked[1, :near], *thin)],
            two[0] + two[1],
            [flat(shape((rows, features), kind))]
            + [(shape((rows, hidden // 2), BF16), *wide)] * 2,
            [pltpu.VMEM((rows, features), F32)],
            matmul,
        )

    def backward_second(grad, slope, kind):
        return expert_call(
            functools.partial(backward_second_kernel, 2, near),
            "backward_second",
            near,
            [flat(grad), (slope, *wide)],
            two[0] + two[1],
            [flat(shape((rows, features), kind)), (shape((rows, hidden // 2), BF16), *wide)],
            [pltpu.VMEM((rows, features), F32)],
            matmul,
        )

    own_part, active_own, slope_own = forward_second(normed_two, F32)
    far_part, active_far, slope_far = forward_second(normed_far, BF16)
    normed_one_far = over(after(normed_one, normed_far))
    grad_far_part, inner_far = backward_second(grad_far, slope_far, BF16)
    grad_far_part = after(grad_far_part, normed_one_far)
    grad_own_part, inner_own = backward_second(grad_two, slope_own, F32)
    outs = expert_call(
        functools.partial(weights_second_kernel, 2, near),
        "weights_second",
        near,
        [(a, *wide) for a in (inner_own, inner_far, active_own, active_far)]
        + [flat(a) for a in (normed_two, normed_far, grad_two, grad_far)],
        [],
        [(shape((near, 1, CHUNK), F32), *thin)] + quarter_outs(2, near) + quarter_outs(2, near),
        [],
        2 * matmul,
    )
    bias_two, gwin_two, gwout_two = outs[0].reshape(hidden // 2), outs[1:3], outs[3:5]

    grad_arrived = over(grad_far_part)
    far_arrived = over(after(far_part, grad_arrived))
    back, grad_one, sums, inner_one = expert_call(
        functools.partial(backward_first_kernel, steps),
        "backward_first",
        steps,
        [
            flat(a)
            for a in (grad_own_part, after(grad_arrived, bias_two), grad_two, z, first, cot)
        ]
        + [(slope_one, *wide), line(0), line(3), line(6)],
        one[0] + one[1],
        [wide_rows, low_rows, flat(shape((8, features), F32)), (half_hidden, *held)],
        [pltpu.VMEM((rows, features), F32)],
        2 * matmul,
    )
    grad_one_far = over(grad_one)
    branch = first + (own_part + far_arrived.astype(F32) + vectors[5])
    gated = (gate * branch).astype(BF16)
    grad_gate = jnp.sum(wide_cot * branch, axis=-1, keepdims=True)
    score = grad_gate * gate * (1.0 - gate)
    grad_sent = (back + score * vectors[6]).astype(BF16)
    grad_centre = jnp.sum(score * wide_z, axis=0, keepdims=True)
    outs = expert_call(
        functools.partial(weights_first_kernel, near),
        "weights_first",
        near,
        [(inner_one, *wide), (active_one, *wide)]
        + [flat(a) for a in (normed_one, grad_one, normed_one_far, grad_one_far)]
        + [(chunked[0, :near], *thin)],
        one[0][:2] + one[1][:2],
        [(shape((near, 1, CHUNK), F32), *thin)] + quarter_outs(2, near) + quarter_outs(2, near),
        [],
        3 * matmul,
    )
    bias_one = outs[0].reshape(hidden // 2)
    sums = jnp.concatenate([sums[:6], grad_centre], axis=0)
    grads = [(outs[1], outs[2]), (outs[3], outs[4]), gwin_two, gwout_two]
    return gated, grad_sent, sums, jnp.stack([bias_one, bias_two]), grads


def project_back_kernel(peers, *refs):
    stages = bits_of(peers)
    d_ref, w_ref, normed_ref, seq_hbm, middle_hbm, gain_ref = refs[:6]
    grad_refs, tail_ref, out_ref = refs[6:9], refs[9], refs[10]
    refs = refs[11:]
    held = [refs[i * stages : (i + 1) * stages] for i in range(4)]
    landed = [refs[i * stages : (i + 1) * stages] for i in range(4, 8)]
    reducer = Halving(peers, held, landed, *refs[8 * stages : 8 * stages + 2])
    refs = refs[8 * stages + 2 :]
    rows_send, rows_recv, rows_own, shard_send, shard_recv, tail_send, tail_recv = refs[:7]
    turned, seq_ref, middle_ref, far_send, far_recv, local = refs[7:]
    seq = lax.axis_index("seq")
    tokens, features = middle_ref.shape
    half = d_ref.shape[2]
    across = {"seq": 1 - seq}
    seq_copy = pltpu.make_async_copy(seq_hbm, seq_ref, local.at[0])
    middle_copy = pltpu.make_async_copy(middle_hbm, middle_ref, local.at[1])
    seq_copy.start()
    middle_copy.start()
    greet(reducer.partner + [across])
    block = lambda which: pl.ds(pl.multiple_of(which * tokens, tokens), tokens)

    def grad_rows(which):
        total = dot_last(d_ref[0, block(which), :], w_ref[:, :half])
        total += dot_last(d_ref[1, block(which), :], w_ref[:, half : 2 * half])
        return total + dot_last(d_ref[2, block(which), :], w_ref[:, 2 * half : 3 * half])

    def norm_sums(which, grad):
        xhat, _ = normalised(seq_ref[block(which), :].astype(F32))
        return jnp.sum(grad * xhat, axis=0, keepdims=True), jnp.sum(grad, axis=0, keepdims=True)

    far = grad_rows(1 - seq)
    rows_send[...] = far.astype(BF16)
    rows_copy = remote(rows_send, rows_recv, far_send.at[0], far_recv.at[0], across)
    rows_copy.start()
    turned[...] = normed_ref[...].T
    for chunk in range(3):
        reducer.put(chunk, dot(turned[...], d_ref[chunk]))
    reducer.finish(0, 0)
    seq_copy.wait()
    far_one, far_two = norm_sums(1 - seq, far)
    reducer.finish(1, 0)
    own = grad_rows(seq)
    rows_own[...] = own
    own_one, own_two = norm_sums(seq, own)
    line = lambda value: jnp.broadcast_to(value, (64, features))
    lines = jnp.concatenate([line(far_one + own_one), line(far_two + own_two)], axis=0)
    reducer.put(3, lines.T)
    reducer.finish(2, 0)
    results = [None] * 4
    for time in range(1, stages + 3):
        for chunk in range(4):
            s = time - chunk if chunk < 3 else time - 2
            if (1 if chunk < 3 else 0) <= s < stages:
                results[chunk] = reducer.finish(chunk, s)
    for chunk in range(3):
        shard_send[chunk] = results[chunk].astype(BF16)
    tail_send[...] = results[3]
    shard_copy = remote(shard_send, shard_recv, far_send.at[1], far_recv.at[1], across)
    tail_copy = remote(tail_send, tail_recv, far_send.at[2], far_recv.at[2], across)
    shard_copy.start()
    tail_copy.start()
    rows_copy.wait_recv()
    middle_copy.wait()
    xhat, rate = normalised(seq_ref[block(seq), :].astype(F32))
    grad = rows_own[...] + rows_recv[...].astype(F32)
    out_ref[...] = middle_ref[...] + norm_back(grad, xhat, rate, gain_ref[...])
    columns = lambda which: pl.ds(pl.multiple_of(which * half, half), half)
    shard_copy.wait_recv()
    tail_copy.wait_recv()
    for chunk in range(3):
        grad_refs[chunk][:, columns(seq)] = shard_send[chunk].astype(F32)
        grad_refs[chunk][:, columns(1 - seq)] = shard_recv[chunk].astype(F32)
    tail_ref[...] = tail_send[...] + tail_recv[...]
    rows_copy.wait_send()
    shard_copy.wait_send()
    tail_copy.wait_send()
    reducer.drain(4)


def project_back(peers, grads, weight, normed, sequence, grad_middle, gain):
    tokens, features = grad_middle.shape
    half = grads.shape[2]
    rows = features // peers
    shape = jax.ShapeDtypeStruct
    return pl.pallas_call(
        functools.partial(project_back_kernel, peers),
        out_shape=[shape((rows, features), F32)] * 3
        + [shape((rows, 128), F32), shape((tokens, features), F32)],
        in_specs=[pl.BlockSpec(memory_space=pltpu.VMEM)] * 3
        + [pl.BlockSpec(memory_space=pl.ANY)] * 2
        + [pl.BlockSpec(memory_space=pltpu.VMEM)],
        out_specs=[pl.BlockSpec(memory_space=pltpu.VMEM)] * 5,
        scratch_shapes=halving_buffers(peers, rows, [half, half, half, 128])
        + [
            pltpu.VMEM((tokens, features), BF16),
            pltpu.VMEM((tokens, features), BF16),
            pltpu.VMEM((tokens, features), F32),
            pltpu.VMEM((3, rows, half), BF16),
            pltpu.VMEM((3, rows, half), BF16),
            pltpu.VMEM((rows, 128), F32),
            pltpu.VMEM((rows, 128), F32),
            pltpu.VMEM(normed.shape[::-1], BF16),
            pltpu.VMEM(sequence.shape, BF16),
            pltpu.VMEM((tokens, features), F32),
            pltpu.SemaphoreType.DMA((3,)),
            pltpu.SemaphoreType.DMA((3,)),
            pltpu.SemaphoreType.DMA((2,)),
        ],
        compiler_params=pltpu.CompilerParams(
            vmem_limit_bytes=VMEM_LIMIT, collective_id=0, has_side_effects=True
        ),
        cost_estimate=pl.CostEstimate(
            flops=60 * 10**9, bytes_accessed=40 * 10**6, transcendentals=0
        ),
        name="project_back",
    )(grads, weight, normed, sequence, grad_middle, gain)


def body(
    inputs,
    ln_gain,
    ln_shift,
    w_query,
    w_key,
    w_value,
    w_output,
    exp_gain1,
    exp_shift1,
    w_in1,
    b_in1,
    w_out1,
    b_out1,
    exp_gain2,
    exp_shift2,
    w_in2,
    b_in2,
    w_out2,
    b_out2,
    centroid,
    order,
    inverse,
    cotangent,
):
    seq, peer = lax.axis_index("seq"), lax.axis_index("fsdp")
    peers = lax.axis_size("fsdp")
    rows = inputs[0]
    tokens, features = rows.shape
    half = features // 2
    size = features // HEADS
    left, even = seq == 0, lax.rem(peer, 2) == 0
    over = lambda value: swapped(value, "seq")
    beside = lambda value: swapped(value, "fsdp")
    ordered = lambda flag, mine, other, axis: jnp.where(
        flag, jnp.concatenate([mine, other], axis), jnp.concatenate([other, mine], axis)
    )

    other_rows = over(rows)
    columns = lambda w: lax.dynamic_slice_in_dim(w, seq * half, half, 1)
    norm_vectors = jnp.pad(jnp.stack([ln_gain, ln_shift], axis=1), ((0, 0), (0, 126)))
    gathered = lax.all_gather(
        jnp.concatenate([columns(w_query), columns(w_key), columns(w_value), norm_vectors], axis=1),
        "fsdp",
        axis=0,
        tiled=True,
    )
    output_full = lax.all_gather(w_output, "fsdp", axis=0, tiled=True)
    own_vectors = jnp.concatenate(
        [exp_gain1, exp_shift1, b_out1, exp_gain2, exp_shift2, b_out2, centroid], axis=0
    )
    own_biases = jnp.concatenate([b_in1, b_in2], axis=0)
    pair = beside(jnp.concatenate([own_vectors.reshape(-1), own_biases.reshape(-1)]))
    other_vectors = pair[: own_vectors.size].reshape(own_vectors.shape)
    other_biases = pair[own_vectors.size :].reshape(own_biases.shape)
    vectors = ordered(even, own_vectors, other_vectors, 1).astype(F32)

    quarter = w_in1.shape[1]
    pick = lambda table, which: lax.dynamic_slice_in_dim(table, which * quarter, quarter, 1)
    biases = jnp.concatenate(
        [
            pick(own_biases, seq),
            pick(other_biases, seq),
            pick(own_biases, 1 - seq),
            pick(other_biases, 1 - seq),
        ],
        axis=1,
    ).astype(F32)

    def holders(mine, far):
        return [mine, beside(mine), far, beside(far)]

    far_in = over(after(w_in1[0], other_rows))
    far_out = over(after(w_out1[0], far_in))
    one = (holders(w_in1[0], far_in), holders(w_out1[0], far_out))
    two = ([w_in2[0], beside(w_in2[0])], [w_out2[0], beside(w_out2[0])])
    cot = cotangent[0]
    exchange = lambda value: lax.all_to_all(
        value.reshape(peers, tokens // peers, features),
        "fsdp",
        split_axis=0,
        concat_axis=0,
        tiled=True,
    ).reshape(tokens, features)
    cot_slots = exchange(jnp.take(cot, order[0], axis=0))

    gathered = after(gathered, cot_slots)

    sequence = ordered(left, rows, other_rows, 0)
    gain, shift = gathered[:, 3 * half].astype(F32), gathered[:, 3 * half + 1].astype(F32)
    xhat, _ = normalised(sequence.astype(F32))
    normed = (xhat * gain + shift).astype(BF16)
    qkv_weight = gathered[:, : 3 * half]
    qkv = dot(normed, qkv_weight).astype(BF16)
    qkv = after(qkv, far_in)
    mixed_heads, logs = attention_forward(qkv, size)
    block_of = lambda value, which: lax.dynamic_slice_in_dim(value, which * tokens, tokens, 0)
    other_mixed = over(block_of(mixed_heads, 1 - seq))
    mixed = ordered(left, block_of(mixed_heads, seq), other_mixed, 1)
    middle = rows.astype(F32) + dot(mixed, output_full)

    z = exchange(after(jnp.take(middle.astype(BF16), order[0], axis=0), far_out))
    gated, grad_sent, vector_grads, bias_grads, weight_grads = expert(
        z, cot_slots, vectors, biases, one, two, over
    )
    returned = exchange(grad_sent)
    home = jnp.take(exchange(after(gated, returned)), inverse[0], axis=0)
    layer_out = (middle + home.astype(F32)).astype(BF16)
    add = lambda *values: sum(value.astype(F32) for value in values)
    coming = jnp.take(returned, inverse[0], axis=0)
    grad_middle = cot.astype(F32) + coming.astype(F32)

    grad_win_one, grad_wout_one, grad_win_two, grad_wout_two = [
        add(mine, beside(near)) for mine, near in weight_grads
    ]

    own_half = lambda table, which: lax.dynamic_slice_in_dim(table, which * half, half, 1)
    core = lax.rem(peer, 2)
    bias_quarters = jnp.pad(bias_grads, ((0, 0), (0, 2 * quarter))).reshape(2, 4, quarter)
    bias_rows = lambda first: ordered(left, bias_quarters[:, first], bias_quarters[:, first + 2], 1)
    flat = lambda table, bias: jnp.concatenate([table.reshape(-1), bias.reshape(-1)])
    small = flat(own_half(vector_grads, core), bias_rows(0)) + beside(
        flat(own_half(vector_grads, 1 - core), bias_rows(1))
    )
    small = small + over(small)
    count = vector_grads.shape[0]
    vector_out = small[: count * half].reshape(count, 1, half)
    bias_out = small[count * half :].reshape(2, 1, 2 * quarter)

    grad_attn = grad_middle.astype(BF16)
    output_terms = dot_first(mixed, grad_attn).astype(BF16)
    grad_mixed = dot_last(grad_attn, output_full).astype(BF16)
    part_of = lambda value, which: lax.dynamic_slice_in_dim(value, which * half, half, 1)
    other_grad = over(part_of(grad_mixed, 1 - seq))
    grad_heads = ordered(left, part_of(grad_mixed, seq), other_grad, 0)
    parts, grad_wo = attention_backward(peers, qkv, grad_heads, logs, output_terms, size)
    grad_wo = grad_wo + over(grad_wo)
    grad_q, grad_k, grad_v, norm_grads, grad_inputs = project_back(
        peers, parts, gathered, normed, sequence, grad_middle, gain[None]
    )
    return (
        layer_out[None],
        grad_inputs[None],
        norm_grads[:, 0],
        norm_grads[:, 64],
        grad_q,
        grad_k,
        grad_v,
        grad_wo,
        vector_out[0],
        vector_out[1],
        grad_win_one[None],
        bias_out[0],
        grad_wout_one[None],
        vector_out[2],
        vector_out[3],
        vector_out[4],
        grad_win_two[None],
        bias_out[1],
        grad_wout_two[None],
        vector_out[5],
        vector_out[6],
    )


def solution(mesh):
    both, rows, vector = P("fsdp", "seq", None), P("fsdp", None), P("fsdp")
    return jax.shard_map(
        body,
        mesh=mesh,
        in_specs=(both, vector, vector, rows, rows, rows, rows)
        + (rows, rows, both, rows, both, rows) * 2
        + (rows, P("fsdp", "seq"), P("fsdp", "seq"), both),
        out_specs=(both, both, vector, vector, rows, rows, rows, rows)
        + (rows, rows, both, rows, both, rows) * 2
        + (rows,),
        check_vma=False,
    )
```

```python
import functools

import jax
import jax.numpy as jnp
from jax import lax
from jax.experimental import pallas as pl
from jax.experimental.pallas import tpu as pltpu
from jax.sharding import PartitionSpec as P

HEADS = 16
EPS = 1e-05
MASKED = -1e30
BLOCK = 256
CHUNK = 512
BF16 = jnp.bfloat16
F32 = jnp.float32
VMEM_LIMIT = 56 * 1024 * 1024
MESH = pl.DeviceIdType.MESH


def swapped(value, axis):
    pairs = [(source, source ^ 1) for source in range(lax.axis_size(axis))]
    return lax.ppermute(value, axis, pairs)


def after(value, *others):
    return lax.optimization_barrier((value, *others))[0]


def dot_last(left, right):
    return lax.dot_general(left, right, (((1,), (1,)), ((), ())), preferred_element_type=F32)


def dot_first(left, right):
    return lax.dot_general(left, right, (((0,), (0,)), ((), ())), preferred_element_type=F32)


def dot(left, right):
    return jnp.dot(left, right, preferred_element_type=F32)


def normalised(values):
    centred = values - jnp.mean(values, axis=-1, keepdims=True)
    spread = jnp.mean(centred * centred, axis=-1, keepdims=True)
    rate = lax.rsqrt(spread + EPS)
    return centred * rate, rate


def norm_back(grad, xhat, rate, gain):
    scaled = grad * gain
    inner = jnp.mean(scaled * xhat, axis=-1, keepdims=True)
    return rate * (scaled - jnp.mean(scaled, axis=-1, keepdims=True) - xhat * inner)


def bits_of(peers):
    return peers.bit_length() - 1


def greet(partners):
    barrier = pltpu.get_barrier_semaphore()
    for device in partners:
        pl.semaphore_signal(barrier, inc=1, device_id=device, device_id_type=MESH)
    pl.semaphore_wait(barrier, len(partners))


def remote(source, target, sends, recvs, device):
    return pltpu.make_async_remote_copy(
        src_ref=source,
        dst_ref=target,
        send_sem=sends,
        recv_sem=recvs,
        device_id=device,
        device_id_type=MESH,
    )


class Halving:
    def __init__(self, peers, held, landed, sends, recvs):
        peer = lax.axis_index("fsdp")
        self.stages = bits_of(peers)
        self.bit = [lax.rem(peer // (1 << s), 2) for s in range(self.stages)]
        self.partner = [
            {"fsdp": peer + (1 - 2 * self.bit[s]) * (1 << s)} for s in range(self.stages)
        ]
        self.held, self.landed, self.sends, self.recvs = held, landed, sends, recvs

    def copy(self, chunk, s):
        return remote(
            self.held[chunk][s].at[:, 1 - self.bit[s]],
            self.landed[chunk][s],
            self.sends.at[chunk, s],
            self.recvs.at[chunk, s],
            self.partner[s],
        )

    def start(self, chunk):
        self.copy(chunk, 0).start()

    def put(self, chunk, value):
        self.held[chunk][0][...] = value.astype(BF16).reshape(self.held[chunk][0].shape)
        self.start(chunk)

    def finish(self, chunk, s):
        self.copy(chunk, s).wait_recv()
        total = self.held[chunk][s][:, self.bit[s]].astype(F32)
        total = total + self.landed[chunk][s][...].astype(F32)
        if s + 1 < self.stages:
            held = self.held[chunk][s + 1]
            held[...] = total.astype(BF16).reshape(held.shape)
            self.copy(chunk, s + 1).start()
        return total[0]

    def drain(self, chunks):
        for chunk in range(chunks):
            for s in range(self.stages):
                self.copy(chunk, s).wait_send()


def halving_buffers(peers, rows, widths, first=True):
    stages = bits_of(peers)
    held = [
        pltpu.VMEM((peers >> (s + 1), 2, rows, w), BF16)
        for w in widths
        for s in range(0 if first else 1, stages)
    ]
    landed = [pltpu.VMEM((peers >> (s + 1), rows, w), BF16) for w in widths for s in range(stages)]
    return held + landed + [pltpu.SemaphoreType.DMA((len(widths), stages))] * 2


class Exchange:
    def __init__(self, peers, source, target, sends, recvs, local):
        self.peers, self.peer = peers, lax.axis_index("fsdp")
        self.source, self.target = source, target
        self.sends, self.recvs, self.local = sends, recvs, local
        ring = [lax.rem(self.peer + d, peers) for d in range(peers)]
        self.others = [{"fsdp": device} for device in ring[1:]]
        self.ring = ring

    def copy(self, d):
        return remote(
            self.source.at[self.ring[d]],
            self.target.at[self.peer],
            self.sends.at[d],
            self.recvs.at[d],
            self.others[d - 1],
        )

    def own(self):
        return pltpu.make_async_copy(
            self.source.at[self.peer], self.target.at[self.peer], self.local
        )

    def start(self):
        for d in range(1, self.peers):
            self.copy(d).start()
        self.own().start()

    def wait(self):
        for d in range(1, self.peers):
            self.copy(d).wait()
        self.own().wait()


def exchange_sems(peers):
    kind = pltpu.SemaphoreType.DMA
    return [kind((peers,)), kind((peers,)), kind]


def gather_kernel(peers, *refs):
    first_ref, second_ref, rows_ref, far_ref = refs[:4]
    first_out, second_out, rows_out, far_out = refs[4:8]
    sends, recvs, local, far_sends, far_recvs = refs[8:]
    stages = bits_of(peers)
    across = {"seq": 1 - lax.axis_index("seq")}
    peer = lax.axis_index("fsdp")
    bits = list(range(stages))[::-1]
    mixed = [1] + [b for b in bits if b > 1] + [0]
    pieces = [
        (first_ref, first_out, 0, bits, 0),
        (first_ref, first_out, 1, bits, 1),
        (second_ref, second_out, 0, mixed, 0),
    ]
    value = {b: lax.rem(peer // (1 << b), 2) for b in bits}
    partner = {b: {"fsdp": peer + (1 - 2 * value[b]) * (1 << b)} for b in bits}
    own = [
        pltpu.make_async_copy(source, target.at[pl.ds(peer, 1)], local.at[i])
        for i, (source, target) in enumerate([(first_ref, first_out), (second_ref, second_out)])
    ]
    for each in own:
        each.start()
    greet([partner[b] for b in bits] + [across])
    far = [
        remote(source, target, far_sends.at[i], far_recvs.at[i], across)
        for i, (source, target) in enumerate(
            [(rows_ref, rows_out), (far_ref.at[pl.ds(0, far_out.shape[0])], far_out)]
        )
    ]
    for each in far:
        each.start()

    def copy(which, k):
        source, target, piece, order, _ = pieces[which]
        view = target.reshape(*[2] * stages, *target.shape[1:])
        held = view.at[
            tuple(slice(None) if b in order[:k] else value[b] for b in bits) + (piece,)
        ]
        return remote(
            held if k else source.at[0, piece],
            held,
            sends.at[which, k],
            recvs.at[which, k],
            partner[order[k]],
        )

    for time in range(stages + 2):
        if time == 1:
            for each in own:
                each.wait()
        for which in range(len(pieces)):
            k = time - pieces[which][4]
            if 1 <= k <= stages:
                copy(which, k - 1).wait_recv()
            if 0 <= k < stages:
                copy(which, k).start()
    for which in range(len(pieces)):
        for k in range(stages):
            copy(which, k).wait_send()
    for each in far:
        each.wait()


def gather(peers, first, second, rows, weight):
    stages = bits_of(peers)
    shape = lambda a, pieces: (pieces, a.shape[0] // pieces, a.shape[1])
    arrays = [(first, shape(first, 2)), (second, shape(second, 1))]
    outs = pl.pallas_call(
        functools.partial(gather_kernel, peers),
        out_shape=[jax.ShapeDtypeStruct((peers, *form), BF16) for _, form in arrays]
        + [
            jax.ShapeDtypeStruct(rows.shape, BF16),
            jax.ShapeDtypeStruct((weight.shape[0] // 2, weight.shape[1]), BF16),
        ],
        in_specs=[pl.BlockSpec(memory_space=pl.ANY)] * 4,
        out_specs=[pl.BlockSpec(memory_space=pl.ANY)] * 4,
        scratch_shapes=[
            pltpu.SemaphoreType.DMA((3, stages)),
            pltpu.SemaphoreType.DMA((3, stages)),
            pltpu.SemaphoreType.DMA((2,)),
            pltpu.SemaphoreType.DMA((2,)),
            pltpu.SemaphoreType.DMA((2,)),
        ],
        compiler_params=pltpu.CompilerParams(collective_id=2, has_side_effects=True),
        cost_estimate=pl.CostEstimate(
            flops=0, bytes_accessed=40 * first.size * peers, transcendentals=0
        ),
        name="gather",
    )(*[a.reshape(1, *form) for a, form in arrays], rows, weight)
    return [out.reshape(-1, a.shape[1]) for out, (a, _) in zip(outs, arrays)] + list(outs[2:])


def causal_mask(scores):
    keys = lax.broadcasted_iota(jnp.int32, scores.shape, 0)
    queries = lax.broadcasted_iota(jnp.int32, scores.shape, 1)
    return jnp.where(keys <= queries, scores, MASKED)


def attention_forward_kernel(peers, size, *refs):
    rows_ref, other_ref, vector_ref = refs[:3]
    weights, slots_ref, weight_ref = refs[3:6], refs[6], refs[7]
    mixed_ref, log_ref, arrived_ref, far_ref, normed_ref, gain_ref = refs[8:14]
    q_ref, k_ref, v_ref = refs[14:17]
    o_all, o_far, mixed, sends, recvs, weight_sems, *exchange_refs = refs[17:]
    step, steps = pl.program_id(0), o_far.shape[0]
    length, tokens = q_ref.shape[0], o_far.shape[1]
    seq = lax.axis_index("seq")
    across = {"seq": 1 - seq}
    exchange = Exchange(peers, slots_ref, arrived_ref, *exchange_refs)
    weight = remote(
        weight_ref.at[pl.ds(far_ref.shape[0], far_ref.shape[0])],
        far_ref,
        weight_sems.at[0],
        weight_sems.at[1],
        across,
    )

    def block(which):
        column = pl.multiple_of((seq * steps + which) * 128, 128)
        return remote(
            o_far.at[which],
            mixed.at[:, pl.ds(column, 128)],
            sends.at[which],
            recvs.at[which],
            across,
        )

    @pl.when(step == 0)
    def _():
        greet(exchange.others + [across])
        exchange.start()
        weight.start()
        lines = vector_ref[...].astype(F32).T
        gain_ref[...] = jnp.broadcast_to(lines[0:1], gain_ref.shape)
        for which, source in ((seq, rows_ref), (1 - seq, other_ref)):
            xhat, _ = normalised(source[...].astype(F32))
            place = pl.ds(pl.multiple_of(which * tokens, tokens), tokens)
            normed_ref[place, :] = (xhat * lines[0:1] + lines[1:2]).astype(BF16)

    for target, matrix in zip((q_ref, k_ref, v_ref), weights):
        target[...] = dot(normed_ref[...], matrix[...]).astype(BF16)
    for head in range(q_ref.shape[1] // size):
        lanes = slice(head * size, (head + 1) * size)
        for start in range(0, length, BLOCK):
            query = q_ref[start : start + BLOCK, lanes] * BF16(size**-0.5)
            last = causal_mask(dot_last(k_ref[start : start + BLOCK, lanes], query))
            peak = jnp.max(last, axis=0, keepdims=True)
            if start:
                early = dot_last(k_ref[:start, lanes], query)
                peak = jnp.maximum(peak, jnp.max(early, axis=0, keepdims=True))
            last = jnp.exp(last - peak)
            total = jnp.sum(last, axis=0, keepdims=True)
            out = dot_first(v_ref[start : start + BLOCK, lanes], last.astype(BF16))
            if start:
                early = jnp.exp(early - peak)
                total = total + jnp.sum(early, axis=0, keepdims=True)
                out = out + dot_first(v_ref[:start, lanes], early.astype(BF16))
            at = start % tokens
            o_all[start // tokens, at : at + BLOCK, lanes] = (out / total).T.astype(BF16)
            log_ref[0, head : head + 1, start : start + BLOCK] = peak + jnp.log(total)
    column = pl.multiple_of((seq * steps + step) * 128, 128)
    mixed[:, pl.ds(column, 128)] = o_all[seq]
    o_far[step] = o_all[1 - seq]
    block(step).start()

    @pl.when(step == steps - 1)
    def _():
        for which in range(o_far.shape[0]):
            block(which).wait()
        mixed_ref[...] = mixed[...]
        weight.wait()
        exchange.wait()


def attention_backward_kernel(peers, size, *refs):
    q_ref, k_ref, v_ref, g_ref, log_ref, term_ref, d_ref, sum_ref, dk_sum, dv_sum = refs[:10]
    stages = bits_of(peers)
    held = [[term_ref, *refs[10 : 9 + stages]]]
    landed = [refs[9 + stages : 9 + 2 * stages]]
    reducer = Halving(peers, held, landed, *refs[9 + 2 * stages :])
    step, steps = pl.program_id(0), 4

    @pl.when(step == 0)
    def _():
        greet(reducer.partner)
        reducer.start(0)

    for s in range(stages - 1):

        @pl.when(step == min(1 + s, steps - 1))
        def _():
            reducer.finish(0, s)

    length = q_ref.shape[0]
    scale = size**-0.5
    for head in range(q_ref.shape[1] // size):
        lanes = slice(head * size, (head + 1) * size)
        dk_sum[...] = jnp.zeros_like(dk_sum)
        dv_sum[...] = jnp.zeros_like(dv_sum)
        for start in range(0, length, BLOCK):
            rows = slice(start, start + BLOCK)
            query = q_ref[rows, lanes] * BF16(scale)
            grad = g_ref[rows, lanes]
            log_total = log_ref[0, head : head + 1, rows]
            spans = ([slice(0, start)] if start else []) + [rows]
            probs, weighted = [], []
            inner = jnp.zeros((1, BLOCK), F32)
            for span in spans:
                scores = dot_last(k_ref[span, lanes], query)
                if span is rows:
                    scores = causal_mask(scores)
                prob = jnp.exp(scores - log_total)
                grad_prob = dot_last(v_ref[span, lanes], grad)
                inner = inner + jnp.sum(prob * grad_prob, axis=0, keepdims=True)
                probs.append(prob)
                weighted.append(grad_prob)
            grad_query = jnp.zeros((BLOCK, size), F32)
            for span, prob, grad_prob in zip(spans, probs, weighted):
                low = (prob * (grad_prob - inner)).astype(BF16)
                dv_sum[span, :] += dot(prob.astype(BF16), grad)
                dk_sum[span, :] += dot(low, query)
                grad_query = grad_query + dot_first(low, k_ref[span, lanes])
            d_ref[0, rows, lanes] = (grad_query * scale).astype(BF16)
        d_ref[1, :, lanes] = dk_sum[...].astype(BF16)
        d_ref[2, :, lanes] = dv_sum[...].astype(BF16)


    @pl.when(step == steps - 1)
    def _():
        sum_ref[...] = reducer.finish(0, stages - 1)
        reducer.drain(1)


def column(rows, first=0):
    return pl.BlockSpec((rows, 128), lambda i: (0, first + i))


def attention_forward(peers, rows, other, gathered, slots, weight, size):
    tokens, features = rows.shape
    length, half = 2 * tokens, features // 2
    parts, per = half // 128, 128 // size
    shape, kind = jax.ShapeDtypeStruct, pltpu.SemaphoreType.DMA
    anywhere = pl.BlockSpec(memory_space=pl.ANY)
    whole = lambda *form: pl.BlockSpec(form, lambda i: (0, 0))
    return pl.pallas_call(
        functools.partial(attention_forward_kernel, peers, size),
        grid=(parts,),
        out_shape=[
            shape((tokens, features), BF16),
            shape((parts, per, length), F32),
            shape(slots.shape, BF16),
            shape((weight.shape[0] // 2, weight.shape[1]), BF16),
            shape((length, features), BF16),
            shape((8, features), F32),
        ]
        + [shape((length, half), BF16)] * 3,
        in_specs=[
            whole(tokens, features),
            whole(tokens, features),
            pl.BlockSpec((features, 128), lambda i: (0, 3 * parts)),
        ]
        + [column(features, first * parts) for first in range(3)]
        + [anywhere, anywhere],
        out_specs=[
            whole(tokens, features),
            pl.BlockSpec((1, per, length), lambda i: (i, 0, 0)),
            anywhere,
            anywhere,
            whole(length, features),
            whole(8, features),
        ]
        + [column(length)] * 3,
        scratch_shapes=[
            pltpu.VMEM((2, tokens, 128), BF16),
            pltpu.VMEM((parts, tokens, 128), BF16),
            pltpu.VMEM((tokens, features), BF16),
            kind((parts,)),
            kind((parts,)),
            kind((2,)),
        ]
        + exchange_sems(peers),
        compiler_params=pltpu.CompilerParams(
            vmem_limit_bytes=VMEM_LIMIT, collective_id=3, has_side_effects=True
        ),
        cost_estimate=pl.CostEstimate(
            flops=16 * length * length * half, bytes_accessed=20 * length * half, transcendentals=0
        ),
        name="attention_forward",
    )(rows, other, gathered, gathered, gathered, gathered, slots, weight)


def dispatch_kernel(peers, *refs):
    mixed_ref, output_ref, rows_ref, order_ref, weight_ref = refs[:5]
    middle_ref, arrived_ref, far_ref, slots, weight_sems, *exchange_refs = refs[5:]
    tokens = rows_ref.shape[0]
    exchange = Exchange(peers, slots, arrived_ref, *exchange_refs)
    across = {"seq": 1 - lax.axis_index("seq")}
    rows = far_ref.shape[0]
    weight = remote(
        weight_ref.at[pl.ds(0, rows)], far_ref, weight_sems.at[0], weight_sems.at[1], across
    )
    greet(exchange.others + [across])
    weight.start()
    middle = rows_ref[...].astype(F32) + dot(mixed_ref[...], output_ref[...])
    middle_ref[...] = middle
    places = lax.broadcasted_iota(jnp.int32, (tokens, tokens), 1)
    chosen = jnp.where(places == order_ref[...], 1.0, 0.0).astype(BF16)
    slots[...] = dot(chosen, middle.astype(BF16)).astype(BF16).reshape(slots.shape)
    exchange.start()
    exchange.wait()
    weight.wait()


def dispatch(peers, mixed, output, rows, order, weight):
    tokens, features = rows.shape
    slots = (peers, tokens // peers, features)
    shape, kind = jax.ShapeDtypeStruct, pltpu.SemaphoreType.DMA
    here, anywhere = (
        pl.BlockSpec(memory_space=pltpu.VMEM),
        pl.BlockSpec(memory_space=pl.ANY),
    )
    middle, arrived, far = pl.pallas_call(
        functools.partial(dispatch_kernel, peers),
        out_shape=(
            shape((tokens, features), F32),
            shape(slots, BF16),
            shape((weight.shape[0] // 2, weight.shape[1]), BF16),
        ),
        in_specs=[here, here, here, here, anywhere],
        out_specs=(here, anywhere, anywhere),
        scratch_shapes=[pltpu.VMEM(slots, BF16), kind((2,))] + exchange_sems(peers),
        compiler_params=pltpu.CompilerParams(
            vmem_limit_bytes=VMEM_LIMIT, collective_id=4, has_side_effects=True
        ),
        cost_estimate=pl.CostEstimate(
            flops=10**9, bytes_accessed=8 * 10**7, transcendentals=0
        ),
        name="dispatch",
    )(mixed, output, rows, order.reshape(tokens, 1), weight)
    return middle, arrived.reshape(tokens, features), far


def attention_backward(peers, q, k, v, grad, logs, terms, size):
    length, half = grad.shape
    parts, per = half // 128, 128 // size
    rows, width = terms.shape[0] // peers, terms.shape[1]
    blocks = (peers // 2, 2, rows, width)
    shape = jax.ShapeDtypeStruct
    return pl.pallas_call(
        functools.partial(attention_backward_kernel, peers, size),
        grid=(parts,),
        out_shape=(shape((3, length, half), BF16), shape((rows, width), F32)),
        in_specs=[
            column(length),
            column(length),
            column(length),
            column(length),
            pl.BlockSpec((1, per, length), lambda i: (i, 0, 0)),
            pl.BlockSpec(blocks, lambda i: (0, 0, 0, 0)),
        ],
        out_specs=(
            pl.BlockSpec((3, length, 128), lambda i: (0, 0, i)),
            pl.BlockSpec((rows, width), lambda i: (0, 0)),
        ),
        scratch_shapes=[pltpu.VMEM((length, size), F32), pltpu.VMEM((length, size), F32)]
        + halving_buffers(peers, rows, [width], first=False),
        compiler_params=pltpu.CompilerParams(
            vmem_limit_bytes=VMEM_LIMIT, collective_id=1, has_side_effects=True
        ),
        cost_estimate=pl.CostEstimate(
            flops=20 * length * length * half, bytes_accessed=16 * length * half, transcendentals=0
        ),
        name="attention_backward",
    )(q, k, v, grad, logs, terms.reshape(blocks))


def stream(step, steps, pairs, buffers, sems):
    def fetch(which):
        slot = lax.rem(which, 2)
        for m, refs in enumerate(pairs):
            first = 0
            for ref in refs:
                count = ref.shape[0] // CHUNK

                @pl.when(jnp.logical_and(which >= first, which < first + count))
                def _(m=m, ref=ref, first=first):
                    row = pl.multiple_of((which - first) * CHUNK, CHUNK)
                    pltpu.make_async_copy(
                        ref.at[pl.ds(row, CHUNK)], buffers[m].at[slot], sems.at[m, slot]
                    ).start()

                first += count

    @pl.when(step == 0)
    def _():
        fetch(step)

    @pl.when(step + 1 < steps)
    def _():
        fetch(step + 1)

    slot = lax.rem(step, 2)
    for m, refs in enumerate(pairs):
        pltpu.make_async_copy(
            refs[0].at[pl.ds(0, CHUNK)], buffers[m].at[slot], sems.at[m, slot]
        ).wait()
    return slot


def gelu_parts(inner):
    cdf = 0.5 * (1.0 + lax.erf(inner * 0.7071067811865476))
    slope = cdf + inner * (jnp.exp(-0.5 * inner * inner) * 0.3989422804014327)
    return inner * cdf, slope


def forward_first_kernel(steps, *refs):
    z_ref, gain_ref, shift_ref, out_bias_ref, gain_two, shift_two, bias_ref = refs[:7]
    win, wout = refs[7:13], refs[13:19]
    first_ref, normed_ref, active_ref, slope_ref, normed_two = refs[19:24]
    in_buf, out_buf, sems = refs[24:]
    step = pl.program_id(0)

    @pl.when(step == 0)
    def _():
        z = z_ref[...].astype(F32)
        xhat, _ = normalised(z)
        normed_ref[...] = (xhat * gain_ref[...] + shift_ref[...]).astype(BF16)
        first_ref[...] = jnp.broadcast_to(out_bias_ref[...], first_ref.shape)

    slot = stream(step, steps, (win, wout), (in_buf, out_buf), sems)
    active, slope = gelu_parts(dot_last(normed_ref[...], in_buf[slot]) + bias_ref[0])
    low = active.astype(BF16)
    slope_ref[...] = slope.astype(BF16)
    first_ref[...] += dot(low, out_buf[slot])

    @pl.when(step < steps // 2)
    def _():
        active_ref[...] = low

    @pl.when(step == steps - 1)
    def _():
        xhat, _ = normalised(z_ref[...].astype(F32) + first_ref[...])
        normed_two[...] = (xhat * gain_two[...] + shift_two[...]).astype(BF16)


def forward_second_kernel(parts, steps, normed_ref, bias_ref, *refs):
    win, wout = refs[:parts], refs[parts : 2 * parts]
    part_ref, active_ref, slope_ref, total, in_buf, out_buf, sems = refs[2 * parts :]
    step = pl.program_id(0)

    @pl.when(step == 0)
    def _():
        total[...] = jnp.zeros_like(total)

    slot = stream(step, steps, (win, wout), (in_buf, out_buf), sems)
    active, slope = gelu_parts(dot_last(normed_ref[...], in_buf[slot]) + bias_ref[0])
    low = active.astype(BF16)
    active_ref[...] = low
    slope_ref[...] = slope.astype(BF16)
    total[...] += dot(low, out_buf[slot])

    @pl.when(step == steps - 1)
    def _():
        part_ref[...] = total[...].astype(part_ref.dtype)


def backward_second_kernel(parts, steps, grad_ref, slope_ref, *refs):
    win, wout = refs[:parts], refs[parts : 2 * parts]
    part_ref, inner_ref, total, in_buf, out_buf, sems = refs[2 * parts :]
    step = pl.program_id(0)

    @pl.when(step == 0)
    def _():
        total[...] = jnp.zeros_like(total)

    slot = stream(step, steps, (win, wout), (in_buf, out_buf), sems)
    inner = (slope_ref[...].astype(F32) * dot_last(grad_ref[...], out_buf[slot])).astype(BF16)
    inner_ref[...] = inner
    total[...] += dot(inner, in_buf[slot])

    @pl.when(step == steps - 1)
    def _():
        part_ref[...] = total[...].astype(part_ref.dtype)


def weights_second_kernel(parts, steps, *refs):
    inner, active, normed, grad = refs[:2], refs[2:4], refs[4:6], refs[6:8]
    bias_ref = refs[8]
    gwin, gwout = refs[9 : 9 + parts], refs[9 + parts : 9 + 2 * parts]
    step = pl.program_id(0)
    per = steps // parts
    one, two = inner[0][...], inner[1][...]
    bias_ref[0] = jnp.sum(one.astype(F32), axis=0, keepdims=True) + jnp.sum(
        two.astype(F32), axis=0, keepdims=True
    )
    grad_in = (dot_first(one, normed[0][...]) + dot_first(two, normed[1][...])).astype(BF16)
    grad_out = (
        dot_first(active[0][...], grad[0][...]) + dot_first(active[1][...], grad[1][...])
    ).astype(BF16)
    for quarter in range(parts):

        @pl.when(step // per == quarter)
        def _():
            gwin[quarter][...] = grad_in
            gwout[quarter][...] = grad_out


def backward_first_kernel(steps, *refs):
    own_ref, arrived_ref, grad_two_ref, z_ref, first_ref, cot_ref = refs[:6]
    slope_ref, gain_ref, gain_two, centre_ref, _ = refs[6:11]
    win, wout = refs[11:17], refs[17:23]
    back_ref, grad_low, vector_ref, inner_ref = refs[23:27]
    total, in_buf, out_buf, sems = refs[27:]
    step = pl.program_id(0)
    down = lambda value: jnp.sum(value, axis=0, keepdims=True)

    @pl.when(step == 0)
    def _():
        total[...] = jnp.zeros_like(total)
        z = z_ref[...].astype(F32)
        xhat, rate = normalised(z + first_ref[...])
        grad_normed = own_ref[...] + arrived_ref[...].astype(F32)
        grad_rows = norm_back(grad_normed, xhat, rate, gain_two[...])
        back_ref[...] = grad_rows
        gate = jax.nn.sigmoid(jnp.sum(z * centre_ref[...], axis=-1, keepdims=True))
        low = (gate * cot_ref[...].astype(F32) + grad_rows).astype(BF16)
        grad_low[...] = low
        vector_ref[2:3] = down(low.astype(F32))
        vector_ref[3:4] = down(grad_normed * xhat)
        vector_ref[4:5] = down(grad_normed)
        vector_ref[5:6] = down(grad_two_ref[...].astype(F32))
        vector_ref[6:8] = jnp.zeros_like(vector_ref[6:8])

    slot = stream(step, steps, (win, wout), (in_buf, out_buf), sems)
    inner = (slope_ref[...].astype(F32) * dot_last(grad_low[...], out_buf[slot])).astype(BF16)
    total[...] += dot(inner, in_buf[slot])

    @pl.when(step < steps // 2)
    def _():
        inner_ref[...] = inner

    @pl.when(step == steps - 1)
    def _():
        xhat, rate = normalised(z_ref[...].astype(F32))
        grad_normed = total[...]
        vector_ref[0:1] = down(grad_normed * xhat)
        vector_ref[1:2] = down(grad_normed)
        back_ref[...] += norm_back(grad_normed, xhat, rate, gain_ref[...])


def weights_first_kernel(steps, *refs):
    inner_ref, active_ref, normed_ref, grad_ref, normed_far, grad_far, in_bias = refs[:7]
    win, wout = refs[7:9], refs[9:11]
    bias_ref, gwin, gwout, in_buf, out_buf, sems = refs[11], refs[12:14], refs[14:16], *refs[16:]
    step = pl.program_id(0)
    slot = stream(step, steps, (win, wout), (in_buf, out_buf), sems)
    active, slope = gelu_parts(dot_last(normed_far[...], in_buf[slot]) + in_bias[0])
    inner = (slope * dot_last(grad_far[...], out_buf[slot])).astype(BF16)
    own = inner_ref[...]
    bias_ref[0] = jnp.sum(own.astype(F32), axis=0, keepdims=True) + jnp.sum(
        inner.astype(F32), axis=0, keepdims=True
    )
    grad_in = (dot_first(own, normed_ref[...]) + dot_first(inner, normed_far[...])).astype(BF16)
    grad_out = (
        dot_first(active_ref[...], grad_ref[...]) + dot_first(active.astype(BF16), grad_far[...])
    ).astype(BF16)
    for quarter in range(2):

        @pl.when(step // (steps // 2) == quarter)
        def _():
            gwin[quarter][...] = grad_in
            gwout[quarter][...] = grad_out


def expert_call(kernel, name, steps, inputs, weights, outs, scratch, flops):
    whole = lambda shape: pl.BlockSpec(shape, lambda c: (0,) * len(shape))
    spec = lambda shape, block, at: whole(shape) if block is None else pl.BlockSpec(block, at)
    if weights:
        features = weights[0].shape[-1]
        scratch = scratch + [
            pltpu.VMEM((2, CHUNK, features), BF16),
            pltpu.VMEM((2, CHUNK, features), BF16),
            pltpu.SemaphoreType.DMA((2, 2)),
        ]
    moved = sum(a.size * a.dtype.itemsize for a, _, _ in inputs + outs)
    return pl.pallas_call(
        kernel,
        grid=(steps,),
        out_shape=tuple(s for s, _, _ in outs),
        in_specs=[spec(a.shape, b, m) for a, b, m in inputs]
        + [pl.BlockSpec(memory_space=pl.ANY)] * len(weights),
        out_specs=tuple(spec(s.shape, b, m) for s, b, m in outs),
        scratch_shapes=scratch,
        compiler_params=pltpu.CompilerParams(vmem_limit_bytes=VMEM_LIMIT),
        cost_estimate=pl.CostEstimate(
            flops=2 * flops,
            bytes_accessed=moved + 2 * sum(w.size for w in weights),
            transcendentals=0,
        ),
        name=name,
    )(*[a for a, _, _ in inputs], *weights)


def expert(z, cot, vectors, biases, one, two, over):
    rows, features = z.shape
    hidden = biases.shape[1]
    steps = hidden // CHUNK
    near = steps // 2
    line = lambda i: (vectors[i : i + 1], None, None)
    flat = lambda array: (array, None, None)
    shape = jax.ShapeDtypeStruct
    low_rows, wide_rows = flat(shape((rows, features), BF16)), flat(shape((rows, features), F32))
    wide = ((rows, CHUNK), lambda c: (0, c))
    thin = ((1, 1, CHUNK), lambda c: (c, 0, 0))
    chunked = biases.reshape(2, steps, 1, CHUNK)
    matmul = 2 * rows * hidden * features

    def quarter_outs(parts, count):
        per = count // parts
        return [
            (
                shape((per * CHUNK, features), BF16),
                (CHUNK, features),
                lambda c, q=q: (jnp.clip(c - q * per, 0, per - 1), 0),
            )
            for q in range(parts)
        ]

    lines = [line(i) for i in range(7)]
    held = ((rows, CHUNK), lambda c: (0, jnp.minimum(c, near - 1)))
    half_hidden = shape((rows, hidden // 2), BF16)
    wide_z, wide_cot = z.astype(F32), cot.astype(F32)
    gate = jax.nn.sigmoid(jnp.sum(wide_z * vectors[6], axis=-1, keepdims=True))
    grad_two = (gate * wide_cot).astype(BF16)
    grad_far = over(grad_two)
    first, normed_one, active_one, slope_one, normed_two = expert_call(
        functools.partial(forward_first_kernel, steps),
        "forward_first",
        steps,
        [flat(z)] + lines[:5] + [(chunked[0], *thin)],
        one[0] + one[1],
        [wide_rows, low_rows, (half_hidden, *held), (shape((rows, hidden), BF16), *wide), low_rows],
        [],
        2 * matmul,
    )
    normed_far = over(after(normed_two, grad_far))

    def forward_second(normed, kind):
        return expert_call(
            functools.partial(forward_second_kernel, 2, near),
            "forward_second",
            near,
            [flat(normed), (chunked[1, :near], *thin)],
            two[0] + two[1],
            [flat(shape((rows, features), kind))]
            + [(shape((rows, hidden // 2), BF16), *wide)] * 2,
            [pltpu.VMEM((rows, features), F32)],
            matmul,
        )

    def backward_second(grad, slope, kind):
        return expert_call(
            functools.partial(backward_second_kernel, 2, near),
            "backward_second",
            near,
            [flat(grad), (slope, *wide)],
            two[0] + two[1],
            [flat(shape((rows, features), kind)), (shape((rows, hidden // 2), BF16), *wide)],
            [pltpu.VMEM((rows, features), F32)],
            matmul,
        )

    own_part, active_own, slope_own = forward_second(normed_two, F32)
    grad_own_part, inner_own = backward_second(grad_two, slope_own, F32)
    normed_one_far = over(after(normed_one, normed_far))
    far_part, active_far, slope_far = forward_second(after(normed_far, inner_own), BF16)
    grad_far_part, inner_far = backward_second(grad_far, slope_far, BF16)
    grad_far_part = after(grad_far_part, normed_one_far)
    outs = expert_call(
        functools.partial(weights_second_kernel, 2, near),
        "weights_second",
        near,
        [(a, *wide) for a in (inner_own, inner_far, active_own, active_far)]
        + [flat(a) for a in (normed_two, normed_far, grad_two, grad_far)],
        [],
        [(shape((near, 1, CHUNK), F32), *thin)] + quarter_outs(2, near) + quarter_outs(2, near),
        [],
        2 * matmul,
    )
    bias_two, gwin_two, gwout_two = outs[0].reshape(hidden // 2), outs[1:3], outs[3:5]

    grad_arrived = over(grad_far_part)
    far_arrived = over(after(far_part, grad_arrived))
    back, grad_one, sums, inner_one = expert_call(
        functools.partial(backward_first_kernel, steps),
        "backward_first",
        steps,
        [flat(a) for a in (grad_own_part, grad_arrived, grad_two, z, first, cot)]
        + [(slope_one, *wide), line(0), line(3), line(6), flat(outs[0])],
        one[0] + one[1],
        [wide_rows, low_rows, flat(shape((8, features), F32)), (half_hidden, *held)],
        [pltpu.VMEM((rows, features), F32)],
        2 * matmul,
    )
    grad_one_far = over(grad_one)
    branch = first + (own_part + far_arrived.astype(F32) + vectors[5])
    gated = (gate * branch).astype(BF16)
    grad_gate = jnp.sum(wide_cot * branch, axis=-1, keepdims=True)
    score = grad_gate * gate * (1.0 - gate)
    grad_sent = (back + score * vectors[6]).astype(BF16)
    grad_centre = jnp.sum(score * wide_z, axis=0, keepdims=True)
    outs = expert_call(
        functools.partial(weights_first_kernel, near),
        "weights_first",
        near,
        [(inner_one, *wide), (active_one, *wide)]
        + [flat(a) for a in (normed_one, grad_one, normed_one_far, grad_one_far)]
        + [(chunked[0, :near], *thin)],
        one[0][:2] + one[1][:2],
        [(shape((near, 1, CHUNK), F32), *thin)] + quarter_outs(2, near) + quarter_outs(2, near),
        [],
        3 * matmul,
    )
    bias_one = outs[0].reshape(hidden // 2)
    sums = jnp.concatenate([sums[:6], grad_centre], axis=0)
    grads = [(outs[1], outs[2]), (outs[3], outs[4]), gwin_two, gwout_two]
    return gated, grad_sent, sums, jnp.stack([bias_one, bias_two]), grads


def project_back_kernel(peers, *refs):
    stages = bits_of(peers)
    d_ref, w_ref, normed_ref, own_hbm, other_hbm, middle_hbm, gain_ref = refs[:7]
    ours, theirs = refs[7:11], refs[11:15]
    grad_refs, tail_ref, out_ref, pair_refs = refs[15:18], refs[18], refs[19], refs[20:24]
    refs = refs[24:]
    held = [refs[i * stages : (i + 1) * stages] for i in range(4)]
    landed = [refs[i * stages : (i + 1) * stages] for i in range(4, 8)]
    reducer = Halving(peers, held, landed, *refs[8 * stages : 8 * stages + 2])
    refs = refs[8 * stages + 2 :]
    rows_send, rows_recv, rows_own, shard_send, shard_recv, tail_send, tail_recv = refs[:7]
    turned, seq_ref, middle_ref, far_send, far_recv, local = refs[7:13]
    pair_in, pair_out, in_sems, out_sems = refs[13:]
    seq = lax.axis_index("seq")
    tokens, features = middle_ref.shape
    half = d_ref.shape[2]
    across = {"seq": 1 - seq}
    own_copy = pltpu.make_async_copy(own_hbm, seq_ref.at[0], local.at[0])
    other_copy = pltpu.make_async_copy(other_hbm, seq_ref.at[1], local.at[2])
    middle_copy = pltpu.make_async_copy(middle_hbm, middle_ref, local.at[1])
    own_copy.start()
    other_copy.start()
    middle_copy.start()

    piece = pair_in.shape[2]
    pieces = [(m, at) for m in range(4) for at in range(0, ours[0].shape[0], piece)]
    place = lambda ref, at: ref.at[pl.ds(at, piece)]

    def pair_inputs(i):
        m, at = pieces[i]
        return [
            pltpu.make_async_copy(
                place(ref[m], at), pair_in.at[i % 2, side], in_sems.at[i % 2, side]
            )
            for side, ref in enumerate((ours, theirs))
        ]

    def pair_output(i):
        m, at = pieces[i]
        return pltpu.make_async_copy(
            pair_out.at[i % 2], place(pair_refs[m], at), out_sems.at[i % 2]
        )

    def pair_add(count):
        for i in range(added[0], min(added[0] + count, len(pieces))):
            for copy in pair_inputs(i):
                copy.wait()
            if i >= 2:
                pair_output(i - 2).wait()
            pair_out[i % 2] = pair_in[i % 2, 0].astype(F32) + pair_in[i % 2, 1].astype(F32)
            pair_output(i).start()
            if i + 2 < len(pieces):
                for copy in pair_inputs(i + 2):
                    copy.start()
        added[0] = min(added[0] + count, len(pieces))

    added = [0]
    for i in range(2):
        for copy in pair_inputs(i):
            copy.start()
    greet(reducer.partner + [across])
    block = lambda which: pl.ds(pl.multiple_of(which * tokens, tokens), tokens)

    def grad_rows(which):
        total = dot_last(d_ref[0, block(which), :], w_ref[:, :half])
        total += dot_last(d_ref[1, block(which), :], w_ref[:, half : 2 * half])
        return total + dot_last(d_ref[2, block(which), :], w_ref[:, 2 * half : 3 * half])

    def norm_sums(which, grad):
        xhat, _ = normalised(seq_ref[which].astype(F32))
        return jnp.sum(grad * xhat, axis=0, keepdims=True), jnp.sum(grad, axis=0, keepdims=True)

    far = grad_rows(1 - seq)
    rows_send[...] = far.astype(BF16)
    rows_copy = remote(rows_send, rows_recv, far_send.at[0], far_recv.at[0], across)
    rows_copy.start()
    turned[...] = normed_ref[...].T
    for chunk in range(3):
        reducer.put(chunk, dot(turned[...], d_ref[chunk]))
    reducer.finish(0, 0)
    own_copy.wait()
    other_copy.wait()
    far_one, far_two = norm_sums(1, far)
    reducer.finish(1, 0)
    own = grad_rows(seq)
    rows_own[...] = own
    own_one, own_two = norm_sums(0, own)
    line = lambda value: jnp.broadcast_to(value, (64, features))
    lines = jnp.concatenate([line(far_one + own_one), line(far_two + own_two)], axis=0)
    reducer.put(3, lines.T)
    reducer.finish(2, 0)
    results = [None] * 4
    for time in range(1, stages + 3):
        pair_add(2)
        for chunk in range(4):
            s = time - chunk if chunk < 3 else time - 2
            if (1 if chunk < 3 else 0) <= s < stages:
                results[chunk] = reducer.finish(chunk, s)
    for chunk in range(3):
        shard_send[chunk] = results[chunk].astype(BF16)
    tail_send[...] = results[3]
    shard_copy = remote(shard_send, shard_recv, far_send.at[1], far_recv.at[1], across)
    tail_copy = remote(tail_send, tail_recv, far_send.at[2], far_recv.at[2], across)
    shard_copy.start()
    tail_copy.start()
    pair_add(len(pieces))
    for i in range(len(pieces) - 2, len(pieces)):
        pair_output(i).wait()
    rows_copy.wait_recv()
    middle_copy.wait()
    xhat, rate = normalised(seq_ref[0].astype(F32))
    grad = rows_own[...] + rows_recv[...].astype(F32)
    out_ref[...] = middle_ref[...] + norm_back(grad, xhat, rate, gain_ref[...])
    columns = lambda which: pl.ds(pl.multiple_of(which * half, half), half)
    shard_copy.wait_recv()
    tail_copy.wait_recv()
    for chunk in range(3):
        grad_refs[chunk][:, columns(seq)] = shard_send[chunk].astype(F32)
        grad_refs[chunk][:, columns(1 - seq)] = shard_recv[chunk].astype(F32)
    tail_ref[...] = tail_send[...] + tail_recv[...]
    rows_copy.wait_send()
    shard_copy.wait_send()
    tail_copy.wait_send()
    reducer.drain(4)


def project_back(peers, grads, weight, normed, rows_own, rows_far, grad_middle, gain, ours, theirs):
    tokens, features = grad_middle.shape
    half = grads.shape[2]
    rows = features // peers
    shape = jax.ShapeDtypeStruct
    return pl.pallas_call(
        functools.partial(project_back_kernel, peers),
        out_shape=[shape((rows, features), F32)] * 3
        + [shape((rows, 128), F32), shape((tokens, features), F32)]
        + [shape(array.shape, F32) for array in ours],
        in_specs=[pl.BlockSpec(memory_space=pltpu.VMEM)] * 3
        + [pl.BlockSpec(memory_space=pl.ANY)] * 3
        + [pl.BlockSpec(memory_space=pltpu.VMEM)]
        + [pl.BlockSpec(memory_space=pl.ANY)] * 8,
        out_specs=[pl.BlockSpec(memory_space=pltpu.VMEM)] * 5
        + [pl.BlockSpec(memory_space=pl.ANY)] * 4,
        scratch_shapes=halving_buffers(peers, rows, [half, half, half, 128])
        + [
            pltpu.VMEM((tokens, features), BF16),
            pltpu.VMEM((tokens, features), BF16),
            pltpu.VMEM((tokens, features), F32),
            pltpu.VMEM((3, rows, half), BF16),
            pltpu.VMEM((3, rows, half), BF16),
            pltpu.VMEM((rows, 128), F32),
            pltpu.VMEM((rows, 128), F32),
            pltpu.VMEM(normed.shape[::-1], BF16),
            pltpu.VMEM((2, tokens, features), BF16),
            pltpu.VMEM((tokens, features), F32),
            pltpu.SemaphoreType.DMA((3,)),
            pltpu.SemaphoreType.DMA((3,)),
            pltpu.SemaphoreType.DMA((3,)),
            pltpu.VMEM((2, 2, 256, features), BF16),
            pltpu.VMEM((2, 256, features), F32),
            pltpu.SemaphoreType.DMA((2, 2)),
            pltpu.SemaphoreType.DMA((2,)),
        ],
        compiler_params=pltpu.CompilerParams(
            vmem_limit_bytes=VMEM_LIMIT, collective_id=0, has_side_effects=True
        ),
        cost_estimate=pl.CostEstimate(
            flops=60 * 10**9, bytes_accessed=40 * 10**6, transcendentals=0
        ),
        name="project_back",
    )(grads, weight, normed, rows_own, rows_far, grad_middle, gain, *ours, *theirs)


def body(
    inputs,
    ln_gain,
    ln_shift,
    w_query,
    w_key,
    w_value,
    w_output,
    exp_gain1,
    exp_shift1,
    w_in1,
    b_in1,
    w_out1,
    b_out1,
    exp_gain2,
    exp_shift2,
    w_in2,
    b_in2,
    w_out2,
    b_out2,
    centroid,
    order,
    inverse,
    cotangent,
):
    seq, peer = lax.axis_index("seq"), lax.axis_index("fsdp")
    peers = lax.axis_size("fsdp")
    rows = inputs[0]
    tokens, features = rows.shape
    half = features // 2
    size = features // HEADS
    left, even = seq == 0, lax.rem(peer, 2) == 0
    over = lambda value: swapped(value, "seq")
    beside = lambda value: swapped(value, "fsdp")
    ordered = lambda flag, mine, other, axis: jnp.where(
        flag, jnp.concatenate([mine, other], axis), jnp.concatenate([other, mine], axis)
    )

    columns = lambda w: lax.dynamic_slice_in_dim(w, seq * half, half, 1)
    norm_vectors = jnp.pad(jnp.stack([ln_gain, ln_shift], axis=1), ((0, 0), (0, 126)))
    gathered, output_full, other_rows, far_in_a = gather(
        peers,
        jnp.concatenate([columns(w_query), columns(w_key), columns(w_value), norm_vectors], axis=1),
        w_output,
        rows,
        w_in1[0],
    )
    own_vectors = jnp.concatenate(
        [exp_gain1, exp_shift1, b_out1, exp_gain2, exp_shift2, b_out2, centroid], axis=0
    )
    own_biases = jnp.concatenate([b_in1, b_in2], axis=0)
    pair = beside(jnp.concatenate([own_vectors.reshape(-1), own_biases.reshape(-1)]))
    other_vectors = pair[: own_vectors.size].reshape(own_vectors.shape)
    other_biases = pair[own_vectors.size :].reshape(own_biases.shape)
    vectors = ordered(even, own_vectors, other_vectors, 1).astype(F32)

    quarter = w_in1.shape[1]
    pick = lambda table, which: lax.dynamic_slice_in_dim(table, which * quarter, quarter, 1)
    biases = jnp.concatenate(
        [
            pick(own_biases, seq),
            pick(other_biases, seq),
            pick(own_biases, 1 - seq),
            pick(other_biases, 1 - seq),
        ],
        axis=1,
    ).astype(F32)

    two = ([w_in2[0], beside(w_in2[0])], [w_out2[0], beside(w_out2[0])])
    cot = cotangent[0]
    exchange = lambda value: lax.all_to_all(
        value.reshape(peers, tokens // peers, features),
        "fsdp",
        split_axis=0,
        concat_axis=0,
        tiled=True,
    ).reshape(tokens, features)


    slots = lambda value: jnp.take(value, order[0], axis=0).reshape(peers, -1, features)
    outs = attention_forward(peers, rows, other_rows, gathered, slots(cot), w_in1[0], size)
    mixed, logs, cot_slots, far_in_b, normed, gain, query, keys, values = outs
    cot_slots = cot_slots.reshape(tokens, features)
    far_out_b = over(w_out1[0, quarter // 2 :])
    middle, z, far_out_a = dispatch(peers, mixed, output_full, rows, order, w_out1[0])
    holders = lambda own, *far: [own, beside(own), *far, *[beside(f) for f in far]]
    one = (holders(w_in1[0], far_in_a, far_in_b), holders(w_out1[0], far_out_a, far_out_b))

    gated, grad_sent, vector_grads, bias_grads, weight_grads = expert(
        z, cot_slots, vectors, biases, one, two, over
    )
    returned = exchange(grad_sent)
    coming = jnp.take(returned, inverse[0], axis=0)
    grad_middle = cot.astype(F32) + coming.astype(F32)

    own_half = lambda table, which: lax.dynamic_slice_in_dim(table, which * half, half, 1)
    core = lax.rem(peer, 2)
    bias_quarters = jnp.pad(bias_grads, ((0, 0), (0, 2 * quarter))).reshape(2, 4, quarter)
    bias_rows = lambda first: ordered(left, bias_quarters[:, first], bias_quarters[:, first + 2], 1)
    flat = lambda table, bias: jnp.concatenate([table.reshape(-1), bias.reshape(-1)])
    small = flat(own_half(vector_grads, core), bias_rows(0)) + beside(
        flat(own_half(vector_grads, 1 - core), bias_rows(1))
    )
    small = small + over(small)
    count = vector_grads.shape[0]
    vector_out = small[: count * half].reshape(count, 1, half)
    bias_out = small[count * half :].reshape(2, 1, 2 * quarter)

    grad_attn = grad_middle.astype(BF16)
    output_terms = dot_first(mixed, grad_attn).astype(BF16)
    grad_mixed = dot_last(grad_attn, output_full).astype(BF16)
    part_of = lambda value, which: lax.dynamic_slice_in_dim(value, which * half, half, 1)
    other_grad = over(part_of(grad_mixed, 1 - seq))
    grad_heads = ordered(left, part_of(grad_mixed, seq), other_grad, 0)
    home = jnp.take(after(exchange(after(gated, returned)), grad_heads), inverse[0], axis=0)
    layer_out = (middle + home.astype(F32)).astype(BF16)
    parts, grad_wo = attention_backward(peers, query, keys, values, grad_heads, logs, output_terms, size)
    grad_wo = grad_wo + over(grad_wo)
    ours = [mine for mine, _ in weight_grads]
    theirs = [beside(near) for _, near in weight_grads]
    outs = project_back(
        peers, parts, gathered, normed, rows, other_rows, grad_middle, gain[:1], ours, theirs
    )
    grad_q, grad_k, grad_v, norm_grads, grad_inputs = outs[:5]
    grad_win_one, grad_wout_one, grad_win_two, grad_wout_two = outs[5:]
    return (
        layer_out[None],
        grad_inputs[None],
        norm_grads[:, 0],
        norm_grads[:, 64],
        grad_q,
        grad_k,
        grad_v,
        grad_wo,
        vector_out[0],
        vector_out[1],
        grad_win_one[None],
        bias_out[0],
        grad_wout_one[None],
        vector_out[2],
        vector_out[3],
        vector_out[4],
        grad_win_two[None],
        bias_out[1],
        grad_wout_two[None],
        vector_out[5],
        vector_out[6],
    )


def solution(mesh):
    both, rows, vector = P("fsdp", "seq", None), P("fsdp", None), P("fsdp")
    return jax.shard_map(
        body,
        mesh=mesh,
        in_specs=(both, vector, vector, rows, rows, rows, rows)
        + (rows, rows, both, rows, both, rows) * 2
        + (rows, P("fsdp", "seq"), P("fsdp", "seq"), both),
        out_specs=(both, both, vector, vector, rows, rows, rows, rows)
        + (rows, rows, both, rows, both, rows) * 2
        + (rows,),
        check_vma=False,
    )
```

```python
import functools

import jax
import jax.numpy as jnp
from jax import lax
from jax.experimental import pallas as pl
from jax.experimental.pallas import tpu as pltpu
from jax.sharding import PartitionSpec as P

HEADS = 16
EPS = 1e-05
MASKED = -1e30
BLOCK = 256
CHUNK = 512
BF16 = jnp.bfloat16
F32 = jnp.float32
VMEM_LIMIT = 56 * 1024 * 1024
MESH = pl.DeviceIdType.MESH


def swapped(value, axis):
    pairs = [(source, source ^ 1) for source in range(lax.axis_size(axis))]
    return lax.ppermute(value, axis, pairs)


def after(value, *others):
    return lax.optimization_barrier((value, *others))[0]


def dot_last(left, right):
    return lax.dot_general(left, right, (((1,), (1,)), ((), ())), preferred_element_type=F32)


def dot_first(left, right):
    return lax.dot_general(left, right, (((0,), (0,)), ((), ())), preferred_element_type=F32)


def dot(left, right):
    return jnp.dot(left, right, preferred_element_type=F32)


def normalised(values):
    centred = values - jnp.mean(values, axis=-1, keepdims=True)
    spread = jnp.mean(centred * centred, axis=-1, keepdims=True)
    rate = lax.rsqrt(spread + EPS)
    return centred * rate, rate


def norm_back(grad, xhat, rate, gain):
    scaled = grad * gain
    inner = jnp.mean(scaled * xhat, axis=-1, keepdims=True)
    return rate * (scaled - jnp.mean(scaled, axis=-1, keepdims=True) - xhat * inner)


def bits_of(peers):
    return peers.bit_length() - 1


def greet(partners):
    barrier = pltpu.get_barrier_semaphore()
    for device in partners:
        pl.semaphore_signal(barrier, inc=1, device_id=device, device_id_type=MESH)
    pl.semaphore_wait(barrier, len(partners))


def remote(source, target, sends, recvs, device):
    return pltpu.make_async_remote_copy(
        src_ref=source,
        dst_ref=target,
        send_sem=sends,
        recv_sem=recvs,
        device_id=device,
        device_id_type=MESH,
    )


class Halving:
    def __init__(self, peers, held, landed, sends, recvs):
        peer = lax.axis_index("fsdp")
        self.stages = bits_of(peers)
        self.bit = [lax.rem(peer // (1 << s), 2) for s in range(self.stages)]
        self.partner = [
            {"fsdp": peer + (1 - 2 * self.bit[s]) * (1 << s)} for s in range(self.stages)
        ]
        self.held, self.landed, self.sends, self.recvs = held, landed, sends, recvs

    def copy(self, chunk, s):
        return remote(
            self.held[chunk][s].at[:, 1 - self.bit[s]],
            self.landed[chunk][s],
            self.sends.at[chunk, s],
            self.recvs.at[chunk, s],
            self.partner[s],
        )

    def start(self, chunk):
        self.copy(chunk, 0).start()

    def put(self, chunk, value):
        self.held[chunk][0][...] = value.astype(BF16).reshape(self.held[chunk][0].shape)
        self.start(chunk)

    def finish(self, chunk, s):
        self.copy(chunk, s).wait_recv()
        total = self.held[chunk][s][:, self.bit[s]].astype(F32)
        total = total + self.landed[chunk][s][...].astype(F32)
        if s + 1 < self.stages:
            held = self.held[chunk][s + 1]
            held[...] = total.astype(BF16).reshape(held.shape)
            self.copy(chunk, s + 1).start()
        return total[0]

    def drain(self, chunks):
        for chunk in range(chunks):
            for s in range(self.stages):
                self.copy(chunk, s).wait_send()


def halving_buffers(peers, rows, widths, first=True):
    stages = bits_of(peers)
    held = [
        pltpu.VMEM((peers >> (s + 1), 2, rows, w), BF16)
        for w in widths
        for s in range(0 if first else 1, stages)
    ]
    landed = [pltpu.VMEM((peers >> (s + 1), rows, w), BF16) for w in widths for s in range(stages)]
    return held + landed + [pltpu.SemaphoreType.DMA((len(widths), stages))] * 2


class Exchange:
    def __init__(self, peers, source, target, sends, recvs, local):
        self.peers, self.peer = peers, lax.axis_index("fsdp")
        self.source, self.target = source, target
        self.sends, self.recvs, self.local = sends, recvs, local
        ring = [lax.rem(self.peer + d, peers) for d in range(peers)]
        self.others = [{"fsdp": device} for device in ring[1:]]
        self.ring = ring

    def copy(self, d):
        return remote(
            self.source.at[self.ring[d]],
            self.target.at[self.peer],
            self.sends.at[d],
            self.recvs.at[d],
            self.others[d - 1],
        )

    def own(self):
        return pltpu.make_async_copy(
            self.source.at[self.peer], self.target.at[self.peer], self.local
        )

    def start(self):
        for d in range(1, self.peers):
            self.copy(d).start()
        self.own().start()

    def wait(self):
        for d in range(1, self.peers):
            self.copy(d).wait()
        self.own().wait()


def exchange_sems(peers):
    kind = pltpu.SemaphoreType.DMA
    return [kind((peers,)), kind((peers,)), kind]


def gather_kernel(peers, *refs):
    first_ref, second_ref, rows_ref, far_ref, pair_ref, other_ref = refs[:6]
    first_out, second_out, rows_out, far_out, pair_out, near_in, near_out = refs[6:13]
    sends, recvs, local, far_sends, far_recvs = refs[13:]
    stages = bits_of(peers)
    across = {"seq": 1 - lax.axis_index("seq")}
    peer = lax.axis_index("fsdp")
    bits = list(range(stages))[::-1]
    mixed = [1] + [b for b in bits if b > 1] + [0]
    pieces = [
        (first_ref, first_out, 0, bits, 0),
        (first_ref, first_out, 1, bits, 1),
        (second_ref, second_out, 0, mixed, 0),
    ]
    value = {b: lax.rem(peer // (1 << b), 2) for b in bits}
    partner = {b: {"fsdp": peer + (1 - 2 * value[b]) * (1 << b)} for b in bits}
    own = [
        pltpu.make_async_copy(source, target.at[pl.ds(peer, 1)], local.at[i])
        for i, (source, target) in enumerate([(first_ref, first_out), (second_ref, second_out)])
    ]
    for each in own:
        each.start()
    greet([partner[b] for b in bits] + [across])
    far = [
        remote(source, target, far_sends.at[i], far_recvs.at[i], device)
        for i, (source, target, device) in enumerate(
            [
                (rows_ref, rows_out, across),
                (far_ref, far_out, across),
                (pair_ref, pair_out, partner[0]),
                (far_ref, near_in, partner[0]),
                (other_ref, near_out, partner[0]),
            ]
        )
    ]
    for each in far:
        each.start()

    def copy(which, k):
        source, target, piece, order, _ = pieces[which]
        view = target.reshape(*[2] * stages, *target.shape[1:])
        held = view.at[
            tuple(slice(None) if b in order[:k] else value[b] for b in bits) + (piece,)
        ]
        return remote(
            held if k else source.at[0, piece],
            held,
            sends.at[which, k],
            recvs.at[which, k],
            partner[order[k]],
        )

    for time in range(stages + 2):
        if time == 1:
            for each in own:
                each.wait()
        for which in range(len(pieces)):
            k = time - pieces[which][4]
            if 1 <= k <= stages:
                copy(which, k - 1).wait_recv()
            if 0 <= k < stages:
                copy(which, k).start()
    for which in range(len(pieces)):
        for k in range(stages):
            copy(which, k).wait_send()
    for each in far:
        each.wait()


def gather(peers, first, second, rows, weight, lent, other):
    stages = bits_of(peers)
    shape = lambda a, pieces: (pieces, a.shape[0] // pieces, a.shape[1])
    arrays = [(first, shape(first, 2)), (second, shape(second, 1))]
    outs = pl.pallas_call(
        functools.partial(gather_kernel, peers),
        out_shape=[jax.ShapeDtypeStruct((peers, *form), BF16) for _, form in arrays]
        + [
            jax.ShapeDtypeStruct(rows.shape, BF16),
            *[jax.ShapeDtypeStruct(a.shape, BF16) for a in (weight, lent, weight, other)],
        ],
        in_specs=[pl.BlockSpec(memory_space=pl.ANY)] * 6,
        out_specs=[pl.BlockSpec(memory_space=pl.ANY)] * 7,
        scratch_shapes=[
            pltpu.SemaphoreType.DMA((3, stages)),
            pltpu.SemaphoreType.DMA((3, stages)),
            pltpu.SemaphoreType.DMA((2,)),
            pltpu.SemaphoreType.DMA((5,)),
            pltpu.SemaphoreType.DMA((5,)),
        ],
        compiler_params=pltpu.CompilerParams(collective_id=2, has_side_effects=True),
        cost_estimate=pl.CostEstimate(
            flops=0, bytes_accessed=40 * first.size * peers, transcendentals=0
        ),
        name="gather",
    )(*[a.reshape(1, *form) for a, form in arrays], rows, weight, lent, other)
    return [out.reshape(-1, a.shape[1]) for out, (a, _) in zip(outs, arrays)] + list(outs[2:])


def causal_mask(scores):
    keys = lax.broadcasted_iota(jnp.int32, scores.shape, 0)
    queries = lax.broadcasted_iota(jnp.int32, scores.shape, 1)
    return jnp.where(keys <= queries, scores, MASKED)


def attention_forward_kernel(peers, size, *refs):
    rows_ref, other_ref, vector_ref = refs[:3]
    weights, cot_ref, order_ref, halves = refs[3:6], refs[6], refs[7], refs[8:10]
    mixed_ref, log_ref, arrived_ref, far_refs = refs[10], refs[11], refs[12], refs[13:15]
    normed_ref, gain_ref, q_ref, k_ref, v_ref = refs[15:20]
    o_all, o_far, mixed, slots_ref, sends, recvs, weight_sems, *exchange_refs = refs[20:]
    step, steps = pl.program_id(0), o_far.shape[0]
    length, tokens = q_ref.shape[0], o_far.shape[1]
    seq = lax.axis_index("seq")
    across = {"seq": 1 - seq}
    exchange = Exchange(peers, slots_ref, arrived_ref, *exchange_refs)
    beside = {"fsdp": exchange.peer + 1 - 2 * lax.rem(exchange.peer, 2)}
    copies = [
        remote(
            source.at[pl.ds(0, target.shape[0])],
            target,
            weight_sems.at[0, i],
            weight_sems.at[1, i],
            device,
        )
        for i, (source, target, device) in enumerate(zip(halves, far_refs, (across, beside)))
    ]

    def block(which):
        column = pl.multiple_of((seq * steps + which) * 128, 128)
        return remote(
            o_far.at[which],
            mixed.at[:, pl.ds(column, 128)],
            sends.at[which],
            recvs.at[which],
            across,
        )

    @pl.when(step == 0)
    def _():
        slots_ref[...] = placed(order_ref, cot_ref[...]).astype(BF16).reshape(slots_ref.shape)
        greet(exchange.others + [across])
        for each in copies:
            each.start()
        exchange.start()
        lines = vector_ref[...].astype(F32).T
        gain_ref[...] = jnp.broadcast_to(lines[0:1], gain_ref.shape)
        for which, source in ((seq, rows_ref), (1 - seq, other_ref)):
            xhat, _ = normalised(source[...].astype(F32))
            place = pl.ds(pl.multiple_of(which * tokens, tokens), tokens)
            normed_ref[place, :] = (xhat * lines[0:1] + lines[1:2]).astype(BF16)

    for target, matrix in zip((q_ref, k_ref, v_ref), weights):
        target[...] = dot(normed_ref[...], matrix[...]).astype(BF16)
    for head in range(q_ref.shape[1] // size):
        lanes = slice(head * size, (head + 1) * size)
        for start in range(0, length, BLOCK):
            query = q_ref[start : start + BLOCK, lanes] * BF16(size**-0.5)
            last = causal_mask(dot_last(k_ref[start : start + BLOCK, lanes], query))
            peak = jnp.max(last, axis=0, keepdims=True)
            if start:
                early = dot_last(k_ref[:start, lanes], query)
                peak = jnp.maximum(peak, jnp.max(early, axis=0, keepdims=True))
            last = jnp.exp(last - peak)
            total = jnp.sum(last, axis=0, keepdims=True)
            out = dot_first(v_ref[start : start + BLOCK, lanes], last.astype(BF16))
            if start:
                early = jnp.exp(early - peak)
                total = total + jnp.sum(early, axis=0, keepdims=True)
                out = out + dot_first(v_ref[:start, lanes], early.astype(BF16))
            at = start % tokens
            o_all[start // tokens, at : at + BLOCK, lanes] = (out / total).T.astype(BF16)
            log_ref[0, head : head + 1, start : start + BLOCK] = peak + jnp.log(total)
    column = pl.multiple_of((seq * steps + step) * 128, 128)
    mixed[:, pl.ds(column, 128)] = o_all[seq]
    o_far[step] = o_all[1 - seq]
    block(step).start()

    @pl.when(step == steps - 1)
    def _():
        for which in range(o_far.shape[0]):
            block(which).wait()
        mixed_ref[...] = mixed[...]
        for each in copies:
            each.wait()
        exchange.wait()


def placed(places_ref, rows):
    tokens = places_ref.shape[0]
    columns = lax.broadcasted_iota(jnp.int32, (tokens, tokens), 1)
    return dot(jnp.where(columns == places_ref[...], 1.0, 0.0).astype(BF16), rows)


def attention_backward_kernel(peers, size, *refs):
    q_ref, k_ref, v_ref, log_ref, arrived_ref, place_ref, cot_ref, w_ref, mixed_ref = refs[:9]
    gated_ref = refs[9]
    d_ref, sum_ref, middle_ref, home_ref = refs[10:14]
    dk_sum, dv_sum, grads, grad_all, far_sends, far_recvs = refs[14:20]
    exchange = Exchange(peers, gated_ref, home_ref, *refs[20:23])
    refs = refs[23:]
    stages = bits_of(peers)
    reducer = Halving(
        peers, [refs[:stages]], [refs[stages : 2 * stages]], *refs[2 * stages :]
    )
    step, steps = pl.program_id(0), 4
    parts, tokens = grads.shape[1], grads.shape[2]
    seq = lax.axis_index("seq")
    across = {"seq": 1 - seq}
    columns = lambda side, which: pl.ds(
        pl.multiple_of((side * parts + which) * 128, 128), 128
    )

    def block(which):
        return remote(
            grad_all.at[:, columns(1 - seq, which)],
            grads.at[seq, which],
            far_sends.at[which],
            far_recvs.at[which],
            across,
        )

    @pl.when(step == 0)
    def _():
        greet(exchange.others + [across])
        middle = cot_ref[...].astype(F32) + placed(place_ref, arrived_ref[...])
        middle_ref[...] = middle
        low = middle.astype(BF16)
        grad_all[...] = dot_last(low, w_ref[...]).astype(BF16)
        for which in range(parts):
            block(which).start()
        for which in range(parts):
            grads[seq, which] = grad_all[:, columns(seq, which)]
        reducer.put(0, dot_first(mixed_ref[...], low))

    block(step).wait()

    @pl.when(step == 1)
    def _():
        reducer.finish(0, 0)
        exchange.start()

    @pl.when(step == steps - 1)
    def _():
        reducer.finish(0, 1)

    length = q_ref.shape[0]
    scale = size**-0.5
    for head in range(q_ref.shape[1] // size):
        lanes = slice(head * size, (head + 1) * size)
        dk_sum[...] = jnp.zeros_like(dk_sum)
        dv_sum[...] = jnp.zeros_like(dv_sum)
        for start in range(0, length, BLOCK):
            rows = slice(start, start + BLOCK)
            query = q_ref[rows, lanes] * BF16(scale)
            grad = grads[start // tokens, step, start % tokens : start % tokens + BLOCK, lanes]
            log_total = log_ref[0, head : head + 1, rows]
            spans = ([slice(0, start)] if start else []) + [rows]
            probs, weighted = [], []
            inner = jnp.zeros((1, BLOCK), F32)
            for span in spans:
                scores = dot_last(k_ref[span, lanes], query)
                if span is rows:
                    scores = causal_mask(scores)
                prob = jnp.exp(scores - log_total)
                grad_prob = dot_last(v_ref[span, lanes], grad)
                inner = inner + jnp.sum(prob * grad_prob, axis=0, keepdims=True)
                probs.append(prob)
                weighted.append(grad_prob)
            grad_query = jnp.zeros((BLOCK, size), F32)
            for span, prob, grad_prob in zip(spans, probs, weighted):
                low = (prob * (grad_prob - inner)).astype(BF16)
                dv_sum[span, :] += dot(prob.astype(BF16), grad)
                dk_sum[span, :] += dot(low, query)
                grad_query = grad_query + dot_first(low, k_ref[span, lanes])
            d_ref[0, rows, lanes] = (grad_query * scale).astype(BF16)
        d_ref[1, :, lanes] = dk_sum[...].astype(BF16)
        d_ref[2, :, lanes] = dv_sum[...].astype(BF16)


    @pl.when(step == steps - 1)
    def _():
        for s in range(2, stages):
            total = reducer.finish(0, s)
        sum_ref[...] = total
        reducer.drain(1)
        exchange.wait()


def column(rows, first=0):
    return pl.BlockSpec((rows, 128), lambda i: (0, first + i))


def placed(places_ref, rows):
    tokens = places_ref.shape[0]
    columns = lax.broadcasted_iota(jnp.int32, (tokens, tokens), 1)
    return dot(jnp.where(columns == places_ref[...], 1.0, 0.0).astype(BF16), rows)


def attention_backward_kernel(peers, size, *refs):
    q_ref, k_ref, v_ref, log_ref, arrived_ref, place_ref, cot_ref, w_ref, mixed_ref = refs[:9]
    gated_ref = refs[9]
    d_ref, sum_ref, middle_ref, home_ref = refs[10:14]
    dk_sum, dv_sum, grads, grad_all, far_sends, far_recvs = refs[14:20]
    exchange = Exchange(peers, gated_ref, home_ref, *refs[20:23])
    refs = refs[23:]
    stages = bits_of(peers)
    reducer = Halving(
        peers, [refs[:stages]], [refs[stages : 2 * stages]], *refs[2 * stages :]
    )
    step, steps = pl.program_id(0), 4
    parts, tokens = grads.shape[1], grads.shape[2]
    seq = lax.axis_index("seq")
    across = {"seq": 1 - seq}
    columns = lambda side, which: pl.ds(
        pl.multiple_of((side * parts + which) * 128, 128), 128
    )

    def block(which):
        return remote(
            grad_all.at[:, columns(1 - seq, which)],
            grads.at[seq, which],
            far_sends.at[which],
            far_recvs.at[which],
            across,
        )

    @pl.when(step == 0)
    def _():
        greet(exchange.others + [across])
        middle = cot_ref[...].astype(F32) + placed(place_ref, arrived_ref[...])
        middle_ref[...] = middle
        low = middle.astype(BF16)
        grad_all[...] = dot_last(low, w_ref[...]).astype(BF16)
        for which in range(parts):
            block(which).start()
        for which in range(parts):
            grads[seq, which] = grad_all[:, columns(seq, which)]
        reducer.put(0, dot_first(mixed_ref[...], low))
        exchange.start()

    block(step).wait()

    for s in range(stages - 1):

        @pl.when(step == min(1 + s, steps - 1))
        def _():
            reducer.finish(0, s)

    length = q_ref.shape[0]
    scale = size**-0.5
    for head in range(q_ref.shape[1] // size):
        lanes = slice(head * size, (head + 1) * size)
        dk_sum[...] = jnp.zeros_like(dk_sum)
        dv_sum[...] = jnp.zeros_like(dv_sum)
        for start in range(0, length, BLOCK):
            rows = slice(start, start + BLOCK)
            query = q_ref[rows, lanes] * BF16(scale)
            grad = grads[start // tokens, step, start % tokens : start % tokens + BLOCK, lanes]
            log_total = log_ref[0, head : head + 1, rows]
            spans = ([slice(0, start)] if start else []) + [rows]
            probs, weighted = [], []
            inner = jnp.zeros((1, BLOCK), F32)
            for span in spans:
                scores = dot_last(k_ref[span, lanes], query)
                if span is rows:
                    scores = causal_mask(scores)
                prob = jnp.exp(scores - log_total)
                grad_prob = dot_last(v_ref[span, lanes], grad)
                inner = inner + jnp.sum(prob * grad_prob, axis=0, keepdims=True)
                probs.append(prob)
                weighted.append(grad_prob)
            grad_query = jnp.zeros((BLOCK, size), F32)
            for span, prob, grad_prob in zip(spans, probs, weighted):
                low = (prob * (grad_prob - inner)).astype(BF16)
                dv_sum[span, :] += dot(prob.astype(BF16), grad)
                dk_sum[span, :] += dot(low, query)
                grad_query = grad_query + dot_first(low, k_ref[span, lanes])
            d_ref[0, rows, lanes] = (grad_query * scale).astype(BF16)
        d_ref[1, :, lanes] = dk_sum[...].astype(BF16)
        d_ref[2, :, lanes] = dv_sum[...].astype(BF16)


    @pl.when(step == steps - 1)
    def _():
        sum_ref[...] = reducer.finish(0, stages - 1)
        reducer.drain(1)
        exchange.wait()


def column(rows, first=0):
    return pl.BlockSpec((rows, 128), lambda i: (0, first + i))


def attention_forward(peers, rows, other, gathered, cot, order, weight, far, size):
    tokens, features = rows.shape
    length, half = 2 * tokens, features // 2
    parts, per = half // 128, 128 // size
    slots = (peers, tokens // peers, features)
    shape, kind = jax.ShapeDtypeStruct, pltpu.SemaphoreType.DMA
    anywhere = pl.BlockSpec(memory_space=pl.ANY)
    whole = lambda *form: pl.BlockSpec(form, lambda i: (0, 0))
    return pl.pallas_call(
        functools.partial(attention_forward_kernel, peers, size),
        grid=(parts,),
        out_shape=[
            shape((tokens, features), BF16),
            shape((parts, per, length), F32),
            shape(slots, BF16),
            shape((weight.shape[0] // 2, weight.shape[1]), BF16),
            shape(far.shape, BF16),
            shape((length, features), BF16),
            shape((8, features), F32),
        ]
        + [shape((length, half), BF16)] * 3,
        in_specs=[
            whole(tokens, features),
            whole(tokens, features),
            pl.BlockSpec((features, 128), lambda i: (0, 3 * parts)),
        ]
        + [column(features, first * parts) for first in range(3)]
        + [whole(tokens, features), whole(tokens, 1), anywhere, anywhere],
        out_specs=[
            whole(tokens, features),
            pl.BlockSpec((1, per, length), lambda i: (i, 0, 0)),
            anywhere,
            anywhere,
            anywhere,
            whole(length, features),
            whole(8, features),
        ]
        + [column(length)] * 3,
        scratch_shapes=[
            pltpu.VMEM((2, tokens, 128), BF16),
            pltpu.VMEM((parts, tokens, 128), BF16),
            pltpu.VMEM((tokens, features), BF16),
            pltpu.VMEM(slots, BF16),
            kind((parts,)),
            kind((parts,)),
            kind((2, 2)),
        ]
        + exchange_sems(peers),
        compiler_params=pltpu.CompilerParams(
            vmem_limit_bytes=VMEM_LIMIT, collective_id=3, has_side_effects=True
        ),
        cost_estimate=pl.CostEstimate(
            flops=16 * length * length * half, bytes_accessed=20 * length * half, transcendentals=0
        ),
        name="attention_forward",
    )(rows, other, gathered, gathered, gathered, gathered, cot, order.reshape(tokens, 1), weight, far)


def dispatch_kernel(peers, *refs):
    mixed_ref, output_ref, rows_ref, order_ref, weight_ref, lent_ref = refs[:6]
    middle_ref, arrived_ref, far_ref, near_ref, slots, weight_sems, *exchange_refs = refs[6:]
    exchange = Exchange(peers, slots, arrived_ref, *exchange_refs)
    across = {"seq": 1 - lax.axis_index("seq")}
    rows = far_ref.shape[0]
    beside = {"fsdp": exchange.peer + 1 - 2 * lax.rem(exchange.peer, 2)}
    copies = [
        remote(
            weight_ref.at[pl.ds(rows, rows)], far_ref, weight_sems.at[0], weight_sems.at[1], across
        ),
        remote(lent_ref, near_ref, weight_sems.at[2], weight_sems.at[3], beside),
    ]
    greet(exchange.others + [across])
    for each in copies:
        each.start()
    middle = rows_ref[...].astype(F32) + dot(mixed_ref[...], output_ref[...])
    middle_ref[...] = middle
    slots[...] = placed(order_ref, middle.astype(BF16)).astype(BF16).reshape(slots.shape)
    exchange.start()
    exchange.wait()
    for each in copies:
        each.wait()


def dispatch(peers, mixed, output, rows, order, weight, lent):
    tokens, features = rows.shape
    slots = (peers, tokens // peers, features)
    shape, kind = jax.ShapeDtypeStruct, pltpu.SemaphoreType.DMA
    here, anywhere = (
        pl.BlockSpec(memory_space=pltpu.VMEM),
        pl.BlockSpec(memory_space=pl.ANY),
    )
    middle, arrived, far, near = pl.pallas_call(
        functools.partial(dispatch_kernel, peers),
        out_shape=(
            shape((tokens, features), F32),
            shape(slots, BF16),
            shape((weight.shape[0] // 2, weight.shape[1]), BF16),
            shape(lent.shape, BF16),
        ),
        in_specs=[here, here, here, here, anywhere, anywhere],
        out_specs=(here, anywhere, anywhere, anywhere),
        scratch_shapes=[pltpu.VMEM(slots, BF16), kind((4,))] + exchange_sems(peers),
        compiler_params=pltpu.CompilerParams(
            vmem_limit_bytes=VMEM_LIMIT, collective_id=4, has_side_effects=True
        ),
        cost_estimate=pl.CostEstimate(
            flops=10**9, bytes_accessed=8 * 10**7, transcendentals=0
        ),
        name="dispatch",
    )(mixed, output, rows, order.reshape(tokens, 1), weight, lent)
    return middle, arrived.reshape(tokens, features), far, near


def attention_backward(peers, saved, arrived, inverse, cot, output, gated, size):
    query, keys, values, logs, mixed = saved
    length, half = query.shape
    tokens, features = cot.shape
    parts, per, rows = half // 128, 128 // size, features // peers
    shape, kind = jax.ShapeDtypeStruct, pltpu.SemaphoreType.DMA
    whole = lambda *form: pl.BlockSpec(form, lambda i: (0, 0), pipeline_mode=pl.Buffered(1))
    return pl.pallas_call(
        functools.partial(attention_backward_kernel, peers, size),
        grid=(parts,),
        out_shape=(
            shape((3, length, half), BF16),
            shape((rows, features), F32),
            shape((tokens, features), F32),
            shape((peers, tokens // peers, features), BF16),
        ),
        in_specs=[column(length)] * 3
        + [
            pl.BlockSpec((1, per, length), lambda i: (i, 0, 0)),
            whole(tokens, features),
            whole(tokens, 1),
            whole(tokens, features),
            whole(features, features),
            whole(tokens, features),
            pl.BlockSpec(memory_space=pl.ANY),
        ],
        out_specs=(
            pl.BlockSpec((3, length, 128), lambda i: (0, 0, i)),
            pl.BlockSpec((rows, features), lambda i: (0, 0)),
            pl.BlockSpec((tokens, features), lambda i: (0, 0)),
            pl.BlockSpec(memory_space=pl.ANY),
        ),
        scratch_shapes=[
            pltpu.VMEM((length, size), F32),
            pltpu.VMEM((length, size), F32),
            pltpu.VMEM((2, parts, tokens, 128), BF16),
            pltpu.VMEM((tokens, features), BF16),
            kind((parts,)),
            kind((parts,)),
        ]
        + exchange_sems(peers)
        + halving_buffers(peers, rows, [features]),
        compiler_params=pltpu.CompilerParams(
            vmem_limit_bytes=VMEM_LIMIT, collective_id=1, has_side_effects=True
        ),
        cost_estimate=pl.CostEstimate(
            flops=20 * length * length * half, bytes_accessed=16 * length * half, transcendentals=0
        ),
        name="attention_backward",
    )(
        query,
        keys,
        values,
        logs,
        arrived,
        inverse.reshape(tokens, 1),
        cot,
        output,
        mixed,
        gated.reshape(peers, tokens // peers, features),
    )


def stream(step, steps, pairs, buffers, sems):
    def fetch(which):
        slot = lax.rem(which, 2)
        for m, refs in enumerate(pairs):
            first = 0
            for ref in refs:
                count = ref.shape[0] // CHUNK

                @pl.when(jnp.logical_and(which >= first, which < first + count))
                def _(m=m, ref=ref, first=first):
                    row = pl.multiple_of((which - first) * CHUNK, CHUNK)
                    pltpu.make_async_copy(
                        ref.at[pl.ds(row, CHUNK)], buffers[m].at[slot], sems.at[m, slot]
                    ).start()

                first += count

    @pl.when(step == 0)
    def _():
        fetch(step)

    @pl.when(step + 1 < steps)
    def _():
        fetch(step + 1)

    slot = lax.rem(step, 2)
    for m, refs in enumerate(pairs):
        pltpu.make_async_copy(
            refs[0].at[pl.ds(0, CHUNK)], buffers[m].at[slot], sems.at[m, slot]
        ).wait()
    return slot


def gelu_parts(inner):
    cdf = 0.5 * (1.0 + lax.erf(inner * 0.7071067811865476))
    slope = cdf + inner * (jnp.exp(-0.5 * inner * inner) * 0.3989422804014327)
    return inner * cdf, slope


def forward_first_kernel(steps, *refs):
    z_ref, gain_ref, shift_ref, out_bias_ref, gain_two, shift_two, bias_ref = refs[:7]
    win, wout = refs[7:11], refs[11:17]
    first_ref, normed_ref, active_ref, slope_ref, normed_two = refs[17:22]
    in_buf, out_buf, sems = refs[22:]
    step = pl.program_id(0)

    @pl.when(step == 0)
    def _():
        z = z_ref[...].astype(F32)
        xhat, _ = normalised(z)
        normed_ref[...] = (xhat * gain_ref[...] + shift_ref[...]).astype(BF16)
        first_ref[...] = jnp.broadcast_to(out_bias_ref[...], first_ref.shape)

    slot = stream(step, steps, (win, wout), (in_buf, out_buf), sems)
    active, slope = gelu_parts(dot_last(normed_ref[...], in_buf[slot]) + bias_ref[0])
    low = active.astype(BF16)
    slope_ref[...] = slope.astype(BF16)
    first_ref[...] += dot(low, out_buf[slot])

    @pl.when(step < steps // 2)
    def _():
        active_ref[...] = low

    @pl.when(step == steps - 1)
    def _():
        xhat, _ = normalised(z_ref[...].astype(F32) + first_ref[...])
        normed_two[...] = (xhat * gain_two[...] + shift_two[...]).astype(BF16)


def second_kernel(parts, steps, normed_ref, grad_ref, bias_ref, *refs):
    win, wout = refs[:parts], refs[parts : 2 * parts]
    part_ref, back_ref, active_ref, inner_ref = refs[2 * parts : 2 * parts + 4]
    total, back, in_buf, out_buf, sems = refs[2 * parts + 4 :]
    step = pl.program_id(0)

    @pl.when(step == 0)
    def _():
        total[...] = jnp.zeros_like(total)
        back[...] = jnp.zeros_like(back)

    slot = stream(step, steps, (win, wout), (in_buf, out_buf), sems)
    grad_active = dot_last(grad_ref[...], out_buf[slot])
    active, slope = gelu_parts(dot_last(normed_ref[...], in_buf[slot]) + bias_ref[0])
    low, inner = active.astype(BF16), (slope * grad_active).astype(BF16)
    active_ref[...] = low
    inner_ref[...] = inner
    total[...] += dot(low, out_buf[slot])
    back[...] += dot(inner, in_buf[slot])

    @pl.when(step == steps - 1)
    def _():
        part_ref[...] = total[...].astype(part_ref.dtype)
        back_ref[...] = back[...].astype(back_ref.dtype)


def weights_second_kernel(parts, steps, *refs):
    inner, active, normed, grad = refs[:2], refs[2:4], refs[4:6], refs[6:8]
    bias_ref = refs[8]
    gwin, gwout = refs[9 : 9 + parts], refs[9 + parts : 9 + 2 * parts]
    step = pl.program_id(0)
    per = steps // parts
    one, two = inner[0][...], inner[1][...]
    bias_ref[0] = jnp.sum(one.astype(F32), axis=0, keepdims=True) + jnp.sum(
        two.astype(F32), axis=0, keepdims=True
    )
    grad_in = (dot_first(one, normed[0][...]) + dot_first(two, normed[1][...])).astype(BF16)
    grad_out = (
        dot_first(active[0][...], grad[0][...]) + dot_first(active[1][...], grad[1][...])
    ).astype(BF16)
    for quarter in range(parts):

        @pl.when(step // per == quarter)
        def _():
            gwin[quarter][...] = grad_in
            gwout[quarter][...] = grad_out


def backward_first_kernel(steps, *refs):
    own_ref, arrived_ref, grad_two_ref, z_ref, first_ref, cot_ref = refs[:6]
    slope_ref, gain_ref, gain_two, centre_ref, _ = refs[6:11]
    win, wout = refs[11:15], refs[15:21]
    back_ref, grad_low, vector_ref, inner_ref = refs[21:25]
    total, in_buf, out_buf, sems = refs[25:]
    step = pl.program_id(0)
    down = lambda value: jnp.sum(value, axis=0, keepdims=True)

    @pl.when(step == 0)
    def _():
        total[...] = jnp.zeros_like(total)
        z = z_ref[...].astype(F32)
        xhat, rate = normalised(z + first_ref[...])
        grad_normed = own_ref[...] + arrived_ref[...].astype(F32)
        grad_rows = norm_back(grad_normed, xhat, rate, gain_two[...])
        back_ref[...] = grad_rows
        gate = jax.nn.sigmoid(jnp.sum(z * centre_ref[...], axis=-1, keepdims=True))
        low = (gate * cot_ref[...].astype(F32) + grad_rows).astype(BF16)
        grad_low[...] = low
        vector_ref[2:3] = down(low.astype(F32))
        vector_ref[3:4] = down(grad_normed * xhat)
        vector_ref[4:5] = down(grad_normed)
        vector_ref[5:6] = down(grad_two_ref[...].astype(F32))
        vector_ref[6:8] = jnp.zeros_like(vector_ref[6:8])

    slot = stream(step, steps, (win, wout), (in_buf, out_buf), sems)
    inner = (slope_ref[...].astype(F32) * dot_last(grad_low[...], out_buf[slot])).astype(BF16)
    total[...] += dot(inner, in_buf[slot])

    @pl.when(step < steps // 2)
    def _():
        inner_ref[...] = inner

    @pl.when(step == steps - 1)
    def _():
        xhat, rate = normalised(z_ref[...].astype(F32))
        grad_normed = total[...]
        vector_ref[0:1] = down(grad_normed * xhat)
        vector_ref[1:2] = down(grad_normed)
        back_ref[...] += norm_back(grad_normed, xhat, rate, gain_ref[...])


def weights_first_kernel(steps, *refs):
    inner_ref, active_ref, normed_ref, grad_ref, normed_far, grad_far, in_bias = refs[:7]
    pairs = refs[7:11]
    win, wout = refs[11:13], refs[13:15]
    bias_ref, gwin, gwout, sums = refs[15], refs[16:18], refs[18:20], refs[20:22]
    in_buf, out_buf, sems = refs[22:]
    step = pl.program_id(0)
    for m in range(2):
        sums[m][...] = pairs[2 * m][...].astype(F32) + pairs[2 * m + 1][...].astype(F32)
    slot = stream(step, steps, (win, wout), (in_buf, out_buf), sems)
    active, slope = gelu_parts(dot_last(normed_far[...], in_buf[slot]) + in_bias[0])
    inner = (slope * dot_last(grad_far[...], out_buf[slot])).astype(BF16)
    own = inner_ref[...]
    bias_ref[0] = jnp.sum(own.astype(F32), axis=0, keepdims=True) + jnp.sum(
        inner.astype(F32), axis=0, keepdims=True
    )
    grad_in = (dot_first(own, normed_ref[...]) + dot_first(inner, normed_far[...])).astype(BF16)
    grad_out = (
        dot_first(active_ref[...], grad_ref[...]) + dot_first(active.astype(BF16), grad_far[...])
    ).astype(BF16)
    for quarter in range(2):

        @pl.when(step // (steps // 2) == quarter)
        def _():
            gwin[quarter][...] = grad_in
            gwout[quarter][...] = grad_out


def expert_call(kernel, name, steps, inputs, weights, outs, scratch, flops):
    whole = lambda shape: pl.BlockSpec(shape, lambda c: (0,) * len(shape))
    spec = lambda shape, block, at: whole(shape) if block is None else pl.BlockSpec(block, at)
    if weights:
        features = weights[0].shape[-1]
        scratch = scratch + [
            pltpu.VMEM((2, CHUNK, features), BF16),
            pltpu.VMEM((2, CHUNK, features), BF16),
            pltpu.SemaphoreType.DMA((2, 2)),
        ]
    moved = sum(a.size * a.dtype.itemsize for a, _, _ in inputs + outs)
    return pl.pallas_call(
        kernel,
        grid=(steps,),
        out_shape=tuple(s for s, _, _ in outs),
        in_specs=[spec(a.shape, b, m) for a, b, m in inputs]
        + [pl.BlockSpec(memory_space=pl.ANY)] * len(weights),
        out_specs=tuple(spec(s.shape, b, m) for s, b, m in outs),
        scratch_shapes=scratch,
        compiler_params=pltpu.CompilerParams(vmem_limit_bytes=VMEM_LIMIT),
        cost_estimate=pl.CostEstimate(
            flops=2 * flops,
            bytes_accessed=moved + 2 * sum(w.size for w in weights),
            transcendentals=0,
        ),
        name=name,
    )(*[a for a, _, _ in inputs], *weights)


def expert(z, cot, vectors, biases, one, two, over, beside):
    rows, features = z.shape
    hidden = biases.shape[1]
    steps = hidden // CHUNK
    near = steps // 2
    line = lambda i: (vectors[i : i + 1], None, None)
    flat = lambda array: (array, None, None)
    shape = jax.ShapeDtypeStruct
    low_rows, wide_rows = flat(shape((rows, features), BF16)), flat(shape((rows, features), F32))
    wide = ((rows, CHUNK), lambda c: (0, c))
    thin = ((1, 1, CHUNK), lambda c: (c, 0, 0))
    chunked = biases.reshape(2, steps, 1, CHUNK)
    matmul = 2 * rows * hidden * features

    def quarter_outs(parts, count):
        per = count // parts
        return [
            (
                shape((per * CHUNK, features), BF16),
                (CHUNK, features),
                lambda c, q=q: (jnp.clip(c - q * per, 0, per - 1), 0),
            )
            for q in range(parts)
        ]

    lines = [line(i) for i in range(7)]
    held = ((rows, CHUNK), lambda c: (0, jnp.minimum(c, near - 1)))
    half_hidden = shape((rows, hidden // 2), BF16)
    wide_z, wide_cot = z.astype(F32), cot.astype(F32)
    gate = jax.nn.sigmoid(jnp.sum(wide_z * vectors[6], axis=-1, keepdims=True))
    grad_two = (gate * wide_cot).astype(BF16)
    grad_far = over(grad_two)
    first, normed_one, active_one, slope_one, normed_two = expert_call(
        functools.partial(forward_first_kernel, steps),
        "forward_first",
        steps,
        [flat(z)] + lines[:5] + [(chunked[0], *thin)],
        one[0] + one[1],
        [wide_rows, low_rows, (half_hidden, *held), (shape((rows, hidden), BF16), *wide), low_rows],
        [],
        2 * matmul,
    )
    normed_far = over(after(normed_two, grad_far))

    def second(normed, grad, kind):
        return expert_call(
            functools.partial(second_kernel, 2, near),
            "second",
            near,
            [flat(normed), flat(grad), (chunked[1, :near], *thin)],
            two[0] + two[1],
            [flat(shape((rows, features), kind))] * 2 + [(half_hidden, *wide)] * 2,
            [pltpu.VMEM((rows, features), F32)] * 2,
            2 * matmul,
        )

    own_part, grad_own_part, active_own, inner_own = second(normed_two, grad_two, F32)
    normed_one_far = over(after(normed_one, normed_far))
    normed_far = after(normed_far, inner_own)
    far_part, grad_far_part, active_far, inner_far = second(normed_far, grad_far, BF16)
    grad_far_part = after(grad_far_part, normed_one_far)
    outs = expert_call(
        functools.partial(weights_second_kernel, 2, near),
        "weights_second",
        near,
        [(a, *wide) for a in (inner_own, inner_far, active_own, active_far)]
        + [flat(a) for a in (normed_two, normed_far, grad_two, grad_far)],
        [],
        [(shape((near, 1, CHUNK), F32), *thin)] + quarter_outs(2, near) + quarter_outs(2, near),
        [],
        2 * matmul,
    )
    bias_two, gwin_two, gwout_two = outs[0].reshape(hidden // 2), outs[1:3], outs[3:5]

    grad_arrived = over(grad_far_part)
    far_arrived = over(after(far_part, grad_arrived))
    back, grad_one, sums, inner_one = expert_call(
        functools.partial(backward_first_kernel, steps),
        "backward_first",
        steps,
        [flat(a) for a in (grad_own_part, grad_arrived, grad_two, z, first, cot)]
        + [(slope_one, *wide), line(0), line(3), line(6), flat(outs[0])],
        one[0] + one[1],
        [wide_rows, low_rows, flat(shape((8, features), F32)), (half_hidden, *held)],
        [pltpu.VMEM((rows, features), F32)],
        2 * matmul,
    )
    grad_one_far = over(grad_one)
    branch = first + (own_part + far_arrived.astype(F32) + vectors[5])
    gated = (gate * branch).astype(BF16)
    grad_gate = jnp.sum(wide_cot * branch, axis=-1, keepdims=True)
    score = grad_gate * gate * (1.0 - gate)
    grad_sent = (back + score * vectors[6]).astype(BF16)
    grad_centre = jnp.sum(score * wide_z, axis=0, keepdims=True)
    strip_rows = gwin_two[0].shape[0] // near
    strip = ((strip_rows, features), lambda c: (c, 0))
    outs = expert_call(
        functools.partial(weights_first_kernel, near),
        "weights_first",
        near,
        [(inner_one, *wide), (active_one, *wide)]
        + [flat(a) for a in (normed_one, grad_one, normed_one_far, grad_one_far)]
        + [(chunked[0, :near], *thin)]
        + [
            (array, *strip)
            for mine, other in (gwin_two, gwout_two)
            for array in (mine, beside(other))
        ],
        one[0][:2] + one[1][:2],
        [(shape((near, 1, CHUNK), F32), *thin)]
        + quarter_outs(2, near)
        + quarter_outs(2, near)
        + [(shape(gwin_two[0].shape, F32), *strip)] * 2,
        [],
        3 * matmul,
    )
    bias_one = outs[0].reshape(hidden // 2)
    sums = jnp.concatenate([sums[:6], grad_centre], axis=0)
    grads = [(outs[1], outs[2]), (outs[3], outs[4])]
    return gated, grad_sent, sums, jnp.stack([bias_one, bias_two]), grads, outs[5:]


def project_back_kernel(peers, *refs):
    stages = bits_of(peers)
    d_ref, w_ref, normed_ref, own_hbm, other_hbm, middle_hbm, gain_ref = refs[:7]
    ours, theirs = refs[7:9], refs[9:11]
    place_ref, gated_ref, start_hbm = refs[11:14]
    term_ref, small_ref, lent_ref = refs[14:17]
    grad_refs, tail_ref, out_ref, pair_refs = refs[17:20], refs[20], refs[21], refs[22:24]
    layer_ref, term_out, small_out = refs[24:27]
    refs = refs[27:]
    held = [refs[i * stages : (i + 1) * stages] for i in range(4)]
    landed = [refs[i * stages : (i + 1) * stages] for i in range(4, 8)]
    reducer = Halving(peers, held, landed, *refs[8 * stages : 8 * stages + 2])
    refs = refs[8 * stages + 2 :]
    rows_send, rows_recv, rows_own, shard_send, shard_recv, tail_send, tail_recv = refs[:7]
    turned, seq_ref, middle_ref, far_send, far_recv, local = refs[7:13]
    pair_in, pair_out, in_sems, out_sems, start_ref = refs[13:18]
    term_recv, small_near, small_sum, small_far, side_sends, side_recvs = refs[18:]
    start_copy = pltpu.make_async_copy(start_hbm, start_ref, local.at[3])
    start_copy.start()
    seq = lax.axis_index("seq")
    tokens, features = middle_ref.shape
    half = d_ref.shape[2]
    across = {"seq": 1 - seq}
    own_copy = pltpu.make_async_copy(own_hbm, seq_ref.at[0], local.at[0])
    other_copy = pltpu.make_async_copy(other_hbm, seq_ref.at[1], local.at[2])
    middle_copy = pltpu.make_async_copy(middle_hbm, middle_ref, local.at[1])
    own_copy.start()
    other_copy.start()
    middle_copy.start()

    piece = pair_in.shape[2]
    pieces = [(m, at) for m in range(2) for at in range(0, ours[0].shape[0], piece)]
    place = lambda ref, at: ref.at[pl.ds(at, piece)]

    def pair_inputs(i):
        m, at = pieces[i]
        return [
            pltpu.make_async_copy(
                place(ref[m], at), pair_in.at[i % 2, side], in_sems.at[i % 2, side]
            )
            for side, ref in enumerate((ours, theirs))
        ]

    def pair_output(i):
        m, at = pieces[i]
        return pltpu.make_async_copy(
            pair_out.at[i % 2], place(pair_refs[m], at), out_sems.at[i % 2]
        )

    def pair_add(count):
        for i in range(added[0], min(added[0] + count, len(pieces))):
            for copy in pair_inputs(i):
                copy.wait()
            if i >= 2:
                pair_output(i - 2).wait()
            pair_out[i % 2] = pair_in[i % 2, 0].astype(F32) + pair_in[i % 2, 1].astype(F32)
            pair_output(i).start()
            if i + 2 < len(pieces):
                for copy in pair_inputs(i + 2):
                    copy.start()
        added[0] = min(added[0] + count, len(pieces))

    added = [0]
    for i in range(2):
        for copy in pair_inputs(i):
            copy.start()
    turned[...] = normed_ref[...].T
    terms = dot(turned[...], d_ref[0])
    greet(reducer.partner + [across])
    reducer.put(0, terms)
    term_copy = remote(term_ref, term_recv, side_sends.at[0], side_recvs.at[0], across)
    near_copy = remote(
        lent_ref, small_near, side_sends.at[1], side_recvs.at[1], reducer.partner[0]
    )
    far_copy = remote(small_sum, small_far, side_sends.at[2], side_recvs.at[2], across)
    term_copy.start()
    near_copy.start()
    block = lambda which: pl.ds(pl.multiple_of(which * tokens, tokens), tokens)

    def grad_rows(which):
        total = dot_last(d_ref[0, block(which), :], w_ref[:, :half])
        total += dot_last(d_ref[1, block(which), :], w_ref[:, half : 2 * half])
        return total + dot_last(d_ref[2, block(which), :], w_ref[:, 2 * half : 3 * half])

    def norm_sums(which, grad):
        xhat, _ = normalised(seq_ref[which].astype(F32))
        return jnp.sum(grad * xhat, axis=0, keepdims=True), jnp.sum(grad, axis=0, keepdims=True)

    far = grad_rows(1 - seq)
    rows_send[...] = far.astype(BF16)
    rows_copy = remote(rows_send, rows_recv, far_send.at[0], far_recv.at[0], across)
    rows_copy.start()
    for chunk in range(1, 3):
        reducer.put(chunk, dot(turned[...], d_ref[chunk]))
    reducer.finish(0, 0)
    near_copy.wait()
    small_sum[...] = small_ref[...] + small_near[...]
    far_copy.start()
    own_copy.wait()
    other_copy.wait()
    far_one, far_two = norm_sums(1, far)
    reducer.finish(1, 0)
    own = grad_rows(seq)
    rows_own[...] = own
    own_one, own_two = norm_sums(0, own)
    line = lambda value: jnp.broadcast_to(value, (64, features))
    lines = jnp.concatenate([line(far_one + own_one), line(far_two + own_two)], axis=0)
    reducer.put(3, lines.T)
    reducer.finish(2, 0)
    results = [None] * 4
    for time in range(1, stages + 3):
        pair_add(1)
        if time == 2:
            start_copy.wait()
            layer_ref[...] = (start_ref[...] + placed(place_ref, gated_ref[...])).astype(BF16)
        for chunk in range(4):
            s = time - chunk if chunk < 3 else time - 2
            if (1 if chunk < 3 else 0) <= s < stages:
                results[chunk] = reducer.finish(chunk, s)
    for chunk in range(3):
        shard_send[chunk] = results[chunk].astype(BF16)
    tail_send[...] = results[3]
    shard_copy = remote(shard_send, shard_recv, far_send.at[1], far_recv.at[1], across)
    tail_copy = remote(tail_send, tail_recv, far_send.at[2], far_recv.at[2], across)
    shard_copy.start()
    tail_copy.start()
    pair_add(len(pieces))
    for i in range(len(pieces) - 2, len(pieces)):
        pair_output(i).wait()
    rows_copy.wait_recv()
    middle_copy.wait()
    xhat, rate = normalised(seq_ref[0].astype(F32))
    grad = rows_own[...] + rows_recv[...].astype(F32)
    out_ref[...] = middle_ref[...] + norm_back(grad, xhat, rate, gain_ref[...])
    columns = lambda which: pl.ds(pl.multiple_of(which * half, half), half)
    shard_copy.wait_recv()
    tail_copy.wait_recv()
    for chunk in range(3):
        grad_refs[chunk][:, columns(seq)] = shard_send[chunk].astype(F32)
        grad_refs[chunk][:, columns(1 - seq)] = shard_recv[chunk].astype(F32)
    tail_ref[...] = tail_send[...] + tail_recv[...]
    term_copy.wait()
    term_out[...] = term_ref[...] + term_recv[...]
    far_copy.wait()
    small_out[...] = small_sum[...] + small_far[...]
    rows_copy.wait_send()
    shard_copy.wait_send()
    tail_copy.wait_send()
    reducer.drain(4)


def project_back(peers, grads, weight, normed, rows_own, rows_far, grad_middle, gain, pairs, forward, terms):
    tokens, features = grad_middle.shape
    half = grads.shape[2]
    rows = features // peers
    shape = jax.ShapeDtypeStruct
    return pl.pallas_call(
        functools.partial(project_back_kernel, peers),
        out_shape=[shape((rows, features), F32)] * 3
        + [shape((rows, 128), F32), shape((tokens, features), F32)]
        + [shape(array.shape, F32) for array, _ in pairs]
        + [shape((tokens, features), BF16)]
        + [shape(array.shape, F32) for array in terms[:2]],
        in_specs=[pl.BlockSpec(memory_space=pltpu.VMEM)] * 3
        + [pl.BlockSpec(memory_space=pl.ANY)] * 3
        + [pl.BlockSpec(memory_space=pltpu.VMEM)]
        + [pl.BlockSpec(memory_space=pl.ANY)] * 4
        + [pl.BlockSpec(memory_space=pltpu.VMEM)] * 2
        + [pl.BlockSpec(memory_space=pl.ANY)]
        + [pl.BlockSpec(memory_space=pltpu.VMEM)] * 3,
        out_specs=[pl.BlockSpec(memory_space=pltpu.VMEM)] * 5
        + [pl.BlockSpec(memory_space=pl.ANY)] * 2
        + [pl.BlockSpec(memory_space=pltpu.VMEM)] * 3,
        scratch_shapes=halving_buffers(peers, rows, [half, half, half, 128])
        + [
            pltpu.VMEM((tokens, features), BF16),
            pltpu.VMEM((tokens, features), BF16),
            pltpu.VMEM((tokens, features), F32),
            pltpu.VMEM((3, rows, half), BF16),
            pltpu.VMEM((3, rows, half), BF16),
            pltpu.VMEM((rows, 128), F32),
            pltpu.VMEM((rows, 128), F32),
            pltpu.VMEM(normed.shape[::-1], BF16),
            pltpu.VMEM((2, tokens, features), BF16),
            pltpu.VMEM((tokens, features), F32),
            pltpu.SemaphoreType.DMA((3,)),
            pltpu.SemaphoreType.DMA((3,)),
            pltpu.SemaphoreType.DMA((4,)),
            pltpu.VMEM((2, 2, 256, features), BF16),
            pltpu.VMEM((2, 256, features), F32),
            pltpu.SemaphoreType.DMA((2, 2)),
            pltpu.SemaphoreType.DMA((2,)),
            pltpu.VMEM((tokens, features), F32),
            pltpu.VMEM(terms[0].shape, F32),
        ]
        + [pltpu.VMEM(terms[1].shape, F32)] * 3
        + [pltpu.SemaphoreType.DMA((3,))] * 2,
        compiler_params=pltpu.CompilerParams(
            vmem_limit_bytes=VMEM_LIMIT, collective_id=0, has_side_effects=True
        ),
        cost_estimate=pl.CostEstimate(
            flops=60 * 10**9, bytes_accessed=40 * 10**6, transcendentals=0
        ),
        name="project_back",
    )(
        grads,
        weight,
        normed,
        rows_own,
        rows_far,
        grad_middle,
        gain,
        *[mine for mine, _ in pairs],
        *[other for _, other in pairs],
        *forward,
        *terms,
    )


def body(
    inputs,
    ln_gain,
    ln_shift,
    w_query,
    w_key,
    w_value,
    w_output,
    exp_gain1,
    exp_shift1,
    w_in1,
    b_in1,
    w_out1,
    b_out1,
    exp_gain2,
    exp_shift2,
    w_in2,
    b_in2,
    w_out2,
    b_out2,
    centroid,
    order,
    inverse,
    cotangent,
):
    seq, peer = lax.axis_index("seq"), lax.axis_index("fsdp")
    peers = lax.axis_size("fsdp")
    rows = inputs[0]
    tokens, features = rows.shape
    half = features // 2
    size = features // HEADS
    left, even = seq == 0, lax.rem(peer, 2) == 0
    over = lambda value: swapped(value, "seq")
    beside = lambda value: swapped(value, "fsdp")
    ordered = lambda flag, mine, other, axis: jnp.where(
        flag, jnp.concatenate([mine, other], axis), jnp.concatenate([other, mine], axis)
    )

    columns = lambda w: lax.dynamic_slice_in_dim(w, seq * half, half, 1)
    norm_vectors = jnp.pad(jnp.stack([ln_gain, ln_shift], axis=1), ((0, 0), (0, 126)))
    own_vectors = jnp.concatenate(
        [exp_gain1, exp_shift1, b_out1, exp_gain2, exp_shift2, b_out2, centroid], axis=0
    )
    own_biases = jnp.concatenate([b_in1, b_in2], axis=0)
    gathered, output_full, other_rows, far_in, pair, near_in, near_out = gather(
        peers,
        jnp.concatenate([columns(w_query), columns(w_key), columns(w_value), norm_vectors], axis=1),
        w_output,
        rows,
        w_in1[0],
        jnp.concatenate([own_vectors.reshape(-1), own_biases.reshape(-1)]).reshape(-1, 128),
        w_out1[0],
    )
    pair = pair.reshape(-1)
    other_vectors = pair[: own_vectors.size].reshape(own_vectors.shape)
    other_biases = pair[own_vectors.size :].reshape(own_biases.shape)
    vectors = ordered(even, own_vectors, other_vectors, 1).astype(F32)

    quarter = w_in1.shape[1]
    pick = lambda table, which: lax.dynamic_slice_in_dim(table, which * quarter, quarter, 1)
    biases = jnp.concatenate(
        [
            pick(own_biases, seq),
            pick(other_biases, seq),
            pick(own_biases, 1 - seq),
            pick(other_biases, 1 - seq),
        ],
        axis=1,
    ).astype(F32)

    two = ([w_in2[0], beside(w_in2[0])], [w_out2[0], beside(w_out2[0])])
    cot = cotangent[0]
    exchange = lambda value: lax.all_to_all(
        value.reshape(peers, tokens // peers, features),
        "fsdp",
        split_axis=0,
        concat_axis=0,
        tiled=True,
    ).reshape(tokens, features)


    outs = attention_forward(peers, rows, other_rows, gathered, cot, order, w_out1[0], far_in, size)
    mixed, logs, cot_slots, far_out_a, cross_in, normed, gain, query, keys, values = outs
    cot_slots = cot_slots.reshape(tokens, features)
    middle, z, far_out_b, cross_out_a = dispatch(
        peers, mixed, output_full, rows, order, w_out1[0], far_out_a
    )
    one = (
        [w_in1[0], near_in, far_in, cross_in],
        [w_out1[0], near_out, far_out_a, far_out_b, cross_out_a, beside(far_out_b)],
    )

    gated, grad_sent, vector_grads, bias_grads, grads_one, grads_two = expert(
        z, cot_slots, vectors, biases, one, two, over, beside
    )
    returned = exchange(grad_sent)

    own_half = lambda table, which: lax.dynamic_slice_in_dim(table, which * half, half, 1)
    core = lax.rem(peer, 2)
    bias_quarters = jnp.pad(bias_grads, ((0, 0), (0, 2 * quarter))).reshape(2, 4, quarter)
    bias_rows = lambda first: ordered(left, bias_quarters[:, first], bias_quarters[:, first + 2], 1)
    flat = lambda table, bias: jnp.concatenate([table.reshape(-1), bias.reshape(-1)])
    small = flat(own_half(vector_grads, core), bias_rows(0)).reshape(-1, 128)
    lent = flat(own_half(vector_grads, 1 - core), bias_rows(1)).reshape(-1, 128)

    parts, wo_terms, grad_middle, home = attention_backward(
        peers, (query, keys, values, logs, mixed), returned, inverse, cot, output_full, gated, size
    )
    home = home.reshape(tokens, features)
    outs = project_back(
        peers,
        parts,
        gathered,
        normed,
        rows,
        other_rows,
        grad_middle,
        gain[:1],
        [(mine, beside(near)) for mine, near in grads_one],
        (inverse.reshape(tokens, 1), home, middle),
        (wo_terms, small, lent),
    )
    grad_q, grad_k, grad_v, norm_grads, grad_inputs = outs[:5]
    grad_win_one, grad_wout_one, layer_out, grad_wo, small = outs[5:]
    small = small.reshape(-1)
    count = vector_grads.shape[0]
    vector_out = small[: count * half].reshape(count, 1, half)
    bias_out = small[count * half :].reshape(2, 1, 2 * quarter)
    grad_win_two, grad_wout_two = grads_two
    return (
        layer_out[None],
        grad_inputs[None],
        norm_grads[:, 0],
        norm_grads[:, 64],
        grad_q,
        grad_k,
        grad_v,
        grad_wo,
        vector_out[0],
        vector_out[1],
        grad_win_one[None],
        bias_out[0],
        grad_wout_one[None],
        vector_out[2],
        vector_out[3],
        vector_out[4],
        grad_win_two[None],
        bias_out[1],
        grad_wout_two[None],
        vector_out[5],
        vector_out[6],
    )


def solution(mesh):
    both, rows, vector = P("fsdp", "seq", None), P("fsdp", None), P("fsdp")
    return jax.shard_map(
        body,
        mesh=mesh,
        in_specs=(both, vector, vector, rows, rows, rows, rows)
        + (rows, rows, both, rows, both, rows) * 2
        + (rows, P("fsdp", "seq"), P("fsdp", "seq"), both),
        out_specs=(both, both, vector, vector, rows, rows, rows, rows)
        + (rows, rows, both, rows, both, rows) * 2
        + (rows,),
        check_vma=False,
    )
```

```python
import functools

import jax
import jax.numpy as jnp
from jax import lax
from jax.experimental import pallas as pl
from jax.experimental.pallas import tpu as pltpu
from jax.sharding import PartitionSpec as P

HEADS = 16
EPS = 1e-05
MASKED = -1e30
BLOCK = 256
CHUNK = 512
BF16 = jnp.bfloat16
F32 = jnp.float32
VMEM_LIMIT = 56 * 1024 * 1024
MESH = pl.DeviceIdType.MESH


def swapped(value, axis):
    pairs = [(source, source ^ 1) for source in range(lax.axis_size(axis))]
    return lax.ppermute(value, axis, pairs)


def after(value, *others):
    return lax.optimization_barrier((value, *others))[0]


def dot_last(left, right):
    return lax.dot_general(left, right, (((1,), (1,)), ((), ())), preferred_element_type=F32)


def dot_first(left, right):
    return lax.dot_general(left, right, (((0,), (0,)), ((), ())), preferred_element_type=F32)


def dot(left, right):
    return jnp.dot(left, right, preferred_element_type=F32)


def normalised(values):
    centred = values - jnp.mean(values, axis=-1, keepdims=True)
    spread = jnp.mean(centred * centred, axis=-1, keepdims=True)
    rate = lax.rsqrt(spread + EPS)
    return centred * rate, rate


def norm_back(grad, xhat, rate, gain):
    scaled = grad * gain
    inner = jnp.mean(scaled * xhat, axis=-1, keepdims=True)
    return rate * (scaled - jnp.mean(scaled, axis=-1, keepdims=True) - xhat * inner)


def bits_of(peers):
    return peers.bit_length() - 1


def greet(partners):
    barrier = pltpu.get_barrier_semaphore()
    for device in partners:
        pl.semaphore_signal(barrier, inc=1, device_id=device, device_id_type=MESH)
    pl.semaphore_wait(barrier, len(partners))


def remote(source, target, sends, recvs, device):
    return pltpu.make_async_remote_copy(
        src_ref=source,
        dst_ref=target,
        send_sem=sends,
        recv_sem=recvs,
        device_id=device,
        device_id_type=MESH,
    )


class Halving:
    def __init__(self, peers, held, landed, sends, recvs):
        peer = lax.axis_index("fsdp")
        self.stages = bits_of(peers)
        self.bit = [lax.rem(peer // (1 << s), 2) for s in range(self.stages)]
        self.partner = [
            {"fsdp": peer + (1 - 2 * self.bit[s]) * (1 << s)} for s in range(self.stages)
        ]
        self.held, self.landed, self.sends, self.recvs = held, landed, sends, recvs

    def copy(self, chunk, s):
        return remote(
            self.held[chunk][s].at[:, 1 - self.bit[s]],
            self.landed[chunk][s],
            self.sends.at[chunk, s],
            self.recvs.at[chunk, s],
            self.partner[s],
        )

    def start(self, chunk):
        self.copy(chunk, 0).start()

    def put(self, chunk, value):
        self.held[chunk][0][...] = value.astype(BF16).reshape(self.held[chunk][0].shape)
        self.start(chunk)

    def total(self, chunk, s):
        self.copy(chunk, s).wait_recv()
        mine = self.held[chunk][s][:, self.bit[s]].astype(F32)
        return mine + self.landed[chunk][s][...].astype(F32)

    def finish(self, chunk, s):
        total = self.total(chunk, s)
        if s + 1 < self.stages:
            held = self.held[chunk][s + 1]
            held[...] = total.astype(BF16).reshape(held.shape)
            self.copy(chunk, s + 1).start()
        return total[0]

    def drain(self, chunks, stages):
        for chunk in range(chunks):
            for s in stages:
                self.copy(chunk, s).wait_send()


def halving_buffers(peers, rows, widths, first=True):
    stages = bits_of(peers)
    held = [
        pltpu.VMEM((peers >> (s + 1), 2, rows, w), BF16)
        for w in widths
        for s in range(0 if first else 1, stages)
    ]
    landed = [pltpu.VMEM((peers >> (s + 1), rows, w), BF16) for w in widths for s in range(stages)]
    return held + landed + [pltpu.SemaphoreType.DMA((len(widths), stages))] * 2


class Exchange:
    def __init__(self, peers, source, target, sends, recvs, local):
        self.peers, self.peer = peers, lax.axis_index("fsdp")
        self.source, self.target = source, target
        self.sends, self.recvs, self.local = sends, recvs, local
        ring = [lax.rem(self.peer + d, peers) for d in range(peers)]
        self.others = [{"fsdp": device} for device in ring[1:]]
        self.ring = ring

    def copy(self, d):
        return remote(
            self.source.at[self.ring[d]],
            self.target.at[self.peer],
            self.sends.at[d],
            self.recvs.at[d],
            self.others[d - 1],
        )

    def own(self):
        return pltpu.make_async_copy(
            self.source.at[self.peer], self.target.at[self.peer], self.local
        )

    def start(self):
        for d in range(1, self.peers):
            self.copy(d).start()
        self.own().start()

    def wait(self):
        for d in range(1, self.peers):
            self.copy(d).wait()
        self.own().wait()


def exchange_sems(peers):
    kind = pltpu.SemaphoreType.DMA
    return [kind((peers,)), kind((peers,)), kind]


def gather_kernel(peers, *refs):
    first_ref, second_ref, rows_ref, far_ref, pair_ref, other_ref = refs[:6]
    first_out, second_out, rows_out, far_out, pair_out, near_in, near_out = refs[6:13]
    sends, recvs, local, far_sends, far_recvs = refs[13:]
    stages = bits_of(peers)
    across = {"seq": 1 - lax.axis_index("seq")}
    peer = lax.axis_index("fsdp")
    bits = list(range(stages))[::-1]
    mixed = [1] + [b for b in bits if b > 1] + [0]
    pieces = [
        (first_ref, first_out, 0, bits, 0),
        (first_ref, first_out, 1, bits, 1),
        (second_ref, second_out, 0, mixed, 0),
    ]
    value = {b: lax.rem(peer // (1 << b), 2) for b in bits}
    partner = {b: {"fsdp": peer + (1 - 2 * value[b]) * (1 << b)} for b in bits}
    own = [
        pltpu.make_async_copy(source, target.at[pl.ds(peer, 1)], local.at[i])
        for i, (source, target) in enumerate([(first_ref, first_out), (second_ref, second_out)])
    ]
    for each in own:
        each.start()
    greet([partner[b] for b in bits] + [across])
    far = [
        remote(source, target, far_sends.at[i], far_recvs.at[i], device)
        for i, (source, target, device) in enumerate(
            [
                (rows_ref, rows_out, across),
                (far_ref, far_out, across),
                (pair_ref, pair_out, partner[0]),
                (far_ref, near_in, partner[0]),
                (other_ref, near_out, partner[0]),
            ]
        )
    ]
    for each in far:
        each.start()

    def copy(which, k):
        source, target, piece, order, _ = pieces[which]
        view = target.reshape(*[2] * stages, *target.shape[1:])
        held = view.at[
            tuple(slice(None) if b in order[:k] else value[b] for b in bits) + (piece,)
        ]
        return remote(
            held if k else source.at[0, piece],
            held,
            sends.at[which, k],
            recvs.at[which, k],
            partner[order[k]],
        )

    for time in range(stages + 2):
        if time == 1:
            for each in own:
                each.wait()
        for which in range(len(pieces)):
            k = time - pieces[which][4]
            if 1 <= k <= stages:
                copy(which, k - 1).wait_recv()
            if 0 <= k < stages:
                copy(which, k).start()
    for which in range(len(pieces)):
        for k in range(stages):
            copy(which, k).wait_send()
    for each in far:
        each.wait()


def gather(peers, first, second, rows, weight, lent, other):
    stages = bits_of(peers)
    shape = lambda a, pieces: (pieces, a.shape[0] // pieces, a.shape[1])
    arrays = [(first, shape(first, 2)), (second, shape(second, 1))]
    outs = pl.pallas_call(
        functools.partial(gather_kernel, peers),
        out_shape=[jax.ShapeDtypeStruct((peers, *form), BF16) for _, form in arrays]
        + [
            jax.ShapeDtypeStruct(rows.shape, BF16),
            *[jax.ShapeDtypeStruct(a.shape, BF16) for a in (weight, lent, weight, other)],
        ],
        in_specs=[pl.BlockSpec(memory_space=pl.ANY)] * 6,
        out_specs=[pl.BlockSpec(memory_space=pl.ANY)] * 7,
        scratch_shapes=[
            pltpu.SemaphoreType.DMA((3, stages)),
            pltpu.SemaphoreType.DMA((3, stages)),
            pltpu.SemaphoreType.DMA((2,)),
            pltpu.SemaphoreType.DMA((5,)),
            pltpu.SemaphoreType.DMA((5,)),
        ],
        compiler_params=pltpu.CompilerParams(collective_id=2, has_side_effects=True),
        cost_estimate=pl.CostEstimate(
            flops=0, bytes_accessed=40 * first.size * peers, transcendentals=0
        ),
        name="gather",
    )(*[a.reshape(1, *form) for a, form in arrays], rows, weight, lent, other)
    return [out.reshape(-1, a.shape[1]) for out, (a, _) in zip(outs, arrays)] + list(outs[2:])


def causal_mask(scores):
    keys = lax.broadcasted_iota(jnp.int32, scores.shape, 0)
    queries = lax.broadcasted_iota(jnp.int32, scores.shape, 1)
    return jnp.where(keys <= queries, scores, MASKED)


def attention_forward_kernel(peers, size, *refs):
    rows_ref, other_ref, vector_ref = refs[:3]
    weights, cot_ref, order_ref, halves = refs[3:6], refs[6], refs[7], refs[8:10]
    mixed_ref, log_ref, arrived_ref, far_refs = refs[10], refs[11], refs[12], refs[13:15]
    normed_ref, gain_ref, q_ref, k_ref, v_ref = refs[15:20]
    o_all, o_far, mixed, slots_ref, sends, recvs, weight_sems, *exchange_refs = refs[20:]
    step, steps = pl.program_id(0), o_far.shape[0]
    length, tokens = q_ref.shape[0], o_far.shape[1]
    seq = lax.axis_index("seq")
    across = {"seq": 1 - seq}
    exchange = Exchange(peers, slots_ref, arrived_ref, *exchange_refs)
    beside = {"fsdp": exchange.peer + 1 - 2 * lax.rem(exchange.peer, 2)}
    copies = [
        remote(
            source.at[pl.ds(0, target.shape[0])],
            target,
            weight_sems.at[0, i],
            weight_sems.at[1, i],
            device,
        )
        for i, (source, target, device) in enumerate(zip(halves, far_refs, (across, beside)))
    ]

    def block(which):
        column = pl.multiple_of((seq * steps + which) * 128, 128)
        return remote(
            o_far.at[which],
            mixed.at[:, pl.ds(column, 128)],
            sends.at[which],
            recvs.at[which],
            across,
        )

    @pl.when(step == 0)
    def _():
        slots_ref[...] = placed(order_ref, cot_ref[...]).astype(BF16).reshape(slots_ref.shape)
        greet(exchange.others + [across])
        for each in copies:
            each.start()
        exchange.start()
        lines = vector_ref[...].astype(F32).T
        gain_ref[...] = jnp.broadcast_to(lines[0:1], gain_ref.shape)
        for which, source in ((seq, rows_ref), (1 - seq, other_ref)):
            xhat, _ = normalised(source[...].astype(F32))
            place = pl.ds(pl.multiple_of(which * tokens, tokens), tokens)
            normed_ref[place, :] = (xhat * lines[0:1] + lines[1:2]).astype(BF16)

    for target, matrix in zip((q_ref, k_ref, v_ref), weights):
        target[...] = dot(normed_ref[...], matrix[...]).astype(BF16)
    for head in range(q_ref.shape[1] // size):
        lanes = slice(head * size, (head + 1) * size)
        for start in range(0, length, BLOCK):
            query = q_ref[start : start + BLOCK, lanes] * BF16(size**-0.5)
            last = causal_mask(dot_last(k_ref[start : start + BLOCK, lanes], query))
            peak = jnp.max(last, axis=0, keepdims=True)
            if start:
                early = dot_last(k_ref[:start, lanes], query)
                peak = jnp.maximum(peak, jnp.max(early, axis=0, keepdims=True))
            last = jnp.exp(last - peak)
            total = jnp.sum(last, axis=0, keepdims=True)
            out = dot_first(v_ref[start : start + BLOCK, lanes], last.astype(BF16))
            if start:
                early = jnp.exp(early - peak)
                total = total + jnp.sum(early, axis=0, keepdims=True)
                out = out + dot_first(v_ref[:start, lanes], early.astype(BF16))
            at = start % tokens
            o_all[start // tokens, at : at + BLOCK, lanes] = (out / total).T.astype(BF16)
            log_ref[0, head : head + 1, start : start + BLOCK] = peak + jnp.log(total)
    column = pl.multiple_of((seq * steps + step) * 128, 128)
    mixed[:, pl.ds(column, 128)] = o_all[seq]
    o_far[step] = o_all[1 - seq]
    block(step).start()

    @pl.when(step == steps - 1)
    def _():
        for which in range(o_far.shape[0]):
            block(which).wait()
        mixed_ref[...] = mixed[...]
        for each in copies:
            each.wait()
        exchange.wait()


def placed(places_ref, rows):
    tokens = places_ref.shape[0]
    columns = lax.broadcasted_iota(jnp.int32, (tokens, tokens), 1)
    return dot(jnp.where(columns == places_ref[...], 1.0, 0.0).astype(BF16), rows)


def attention_backward_kernel(peers, size, *refs):
    q_ref, k_ref, v_ref, log_ref, arrived_ref, place_ref, cot_ref, w_ref, mixed_ref = refs[:9]
    gated_ref = refs[9]
    d_ref, sum_ref, middle_ref, home_ref = refs[10:14]
    dk_sum, dv_sum, grads, grad_all, far_sends, far_recvs = refs[14:20]
    exchange = Exchange(peers, gated_ref, home_ref, *refs[20:23])
    refs = refs[23:]
    stages = bits_of(peers)
    reducer = Halving(
        peers, [refs[:stages]], [refs[stages : 2 * stages]], *refs[2 * stages :]
    )
    step, steps = pl.program_id(0), 4
    parts, tokens = grads.shape[1], grads.shape[2]
    seq = lax.axis_index("seq")
    across = {"seq": 1 - seq}
    columns = lambda side, which: pl.ds(
        pl.multiple_of((side * parts + which) * 128, 128), 128
    )

    def block(which):
        return remote(
            grad_all.at[:, columns(1 - seq, which)],
            grads.at[seq, which],
            far_sends.at[which],
            far_recvs.at[which],
            across,
        )

    @pl.when(step == 0)
    def _():
        greet(exchange.others + [across])
        middle = cot_ref[...].astype(F32) + placed(place_ref, arrived_ref[...])
        middle_ref[...] = middle
        low = middle.astype(BF16)
        grad_all[...] = dot_last(low, w_ref[...]).astype(BF16)
        for which in range(parts):
            block(which).start()
        for which in range(parts):
            grads[seq, which] = grad_all[:, columns(seq, which)]
        reducer.put(0, dot_first(mixed_ref[...], low))
        exchange.start()

    block(step).wait()

    @pl.when(step == 1)
    def _():
        reducer.finish(0, 0)

    length = q_ref.shape[0]
    scale = size**-0.5
    for head in range(q_ref.shape[1] // size):
        lanes = slice(head * size, (head + 1) * size)
        dk_sum[...] = jnp.zeros_like(dk_sum)
        dv_sum[...] = jnp.zeros_like(dv_sum)
        for start in range(0, length, BLOCK):
            rows = slice(start, start + BLOCK)
            query = q_ref[rows, lanes] * BF16(scale)
            grad = grads[start // tokens, step, start % tokens : start % tokens + BLOCK, lanes]
            log_total = log_ref[0, head : head + 1, rows]
            spans = ([slice(0, start)] if start else []) + [rows]
            probs, weighted = [], []
            inner = jnp.zeros((1, BLOCK), F32)
            for span in spans:
                scores = dot_last(k_ref[span, lanes], query)
                if span is rows:
                    scores = causal_mask(scores)
                prob = jnp.exp(scores - log_total)
                grad_prob = dot_last(v_ref[span, lanes], grad)
                inner = inner + jnp.sum(prob * grad_prob, axis=0, keepdims=True)
                probs.append(prob)
                weighted.append(grad_prob)
            grad_query = jnp.zeros((BLOCK, size), F32)
            for span, prob, grad_prob in zip(spans, probs, weighted):
                low = (prob * (grad_prob - inner)).astype(BF16)
                dv_sum[span, :] += dot(prob.astype(BF16), grad)
                dk_sum[span, :] += dot(low, query)
                grad_query = grad_query + dot_first(low, k_ref[span, lanes])
            d_ref[0, rows, lanes] = (grad_query * scale).astype(BF16)
        d_ref[1, :, lanes] = dk_sum[...].astype(BF16)
        d_ref[2, :, lanes] = dv_sum[...].astype(BF16)

    @pl.when(step == steps - 1)
    def _():
        sum_ref[...] = reducer.total(0, 1).astype(BF16).reshape(sum_ref.shape)
        reducer.drain(1, range(2))
        exchange.wait()


def column(rows, first=0):
    return pl.BlockSpec((rows, 128), lambda i: (0, first + i))


def attention_forward(peers, rows, other, gathered, cot, order, weight, far, size):
    tokens, features = rows.shape
    length, half = 2 * tokens, features // 2
    parts, per = half // 128, 128 // size
    slots = (peers, tokens // peers, features)
    shape, kind = jax.ShapeDtypeStruct, pltpu.SemaphoreType.DMA
    anywhere = pl.BlockSpec(memory_space=pl.ANY)
    whole = lambda *form: pl.BlockSpec(form, lambda i: (0, 0))
    return pl.pallas_call(
        functools.partial(attention_forward_kernel, peers, size),
        grid=(parts,),
        out_shape=[
            shape((tokens, features), BF16),
            shape((parts, per, length), F32),
            shape(slots, BF16),
            shape((weight.shape[0] // 2, weight.shape[1]), BF16),
            shape(far.shape, BF16),
            shape((length, features), BF16),
            shape((8, features), F32),
        ]
        + [shape((length, half), BF16)] * 3,
        in_specs=[
            whole(tokens, features),
            whole(tokens, features),
            pl.BlockSpec((features, 128), lambda i: (0, 3 * parts)),
        ]
        + [column(features, first * parts) for first in range(3)]
        + [whole(tokens, features), whole(tokens, 1), anywhere, anywhere],
        out_specs=[
            whole(tokens, features),
            pl.BlockSpec((1, per, length), lambda i: (i, 0, 0)),
            anywhere,
            anywhere,
            anywhere,
            whole(length, features),
            whole(8, features),
        ]
        + [column(length)] * 3,
        scratch_shapes=[
            pltpu.VMEM((2, tokens, 128), BF16),
            pltpu.VMEM((parts, tokens, 128), BF16),
            pltpu.VMEM((tokens, features), BF16),
            pltpu.VMEM(slots, BF16),
            kind((parts,)),
            kind((parts,)),
            kind((2, 2)),
        ]
        + exchange_sems(peers),
        compiler_params=pltpu.CompilerParams(
            vmem_limit_bytes=VMEM_LIMIT, collective_id=3, has_side_effects=True
        ),
        cost_estimate=pl.CostEstimate(
            flops=16 * length * length * half, bytes_accessed=20 * length * half, transcendentals=0
        ),
        name="attention_forward",
    )(rows, other, gathered, gathered, gathered, gathered, cot, order.reshape(tokens, 1), weight, far)


def dispatch_kernel(peers, *refs):
    mixed_ref, output_ref, rows_ref, order_ref, weight_ref, lent_ref = refs[:6]
    middle_ref, arrived_ref, far_ref, near_ref, slots, weight_sems, *exchange_refs = refs[6:]
    exchange = Exchange(peers, slots, arrived_ref, *exchange_refs)
    across = {"seq": 1 - lax.axis_index("seq")}
    rows = far_ref.shape[0]
    beside = {"fsdp": exchange.peer + 1 - 2 * lax.rem(exchange.peer, 2)}
    copies = [
        remote(
            weight_ref.at[pl.ds(rows, rows)], far_ref, weight_sems.at[0], weight_sems.at[1], across
        ),
        remote(lent_ref, near_ref, weight_sems.at[2], weight_sems.at[3], beside),
    ]
    greet(exchange.others + [across])
    for each in copies:
        each.start()
    middle = rows_ref[...].astype(F32) + dot(mixed_ref[...], output_ref[...])
    middle_ref[...] = middle
    slots[...] = placed(order_ref, middle.astype(BF16)).astype(BF16).reshape(slots.shape)
    exchange.start()
    exchange.wait()
    for each in copies:
        each.wait()


def dispatch(peers, mixed, output, rows, order, weight, lent):
    tokens, features = rows.shape
    slots = (peers, tokens // peers, features)
    shape, kind = jax.ShapeDtypeStruct, pltpu.SemaphoreType.DMA
    here, anywhere = (
        pl.BlockSpec(memory_space=pltpu.VMEM),
        pl.BlockSpec(memory_space=pl.ANY),
    )
    middle, arrived, far, near = pl.pallas_call(
        functools.partial(dispatch_kernel, peers),
        out_shape=(
            shape((tokens, features), F32),
            shape(slots, BF16),
            shape((weight.shape[0] // 2, weight.shape[1]), BF16),
            shape(lent.shape, BF16),
        ),
        in_specs=[here, here, here, here, anywhere, anywhere],
        out_specs=(here, anywhere, anywhere, anywhere),
        scratch_shapes=[pltpu.VMEM(slots, BF16), kind((4,))] + exchange_sems(peers),
        compiler_params=pltpu.CompilerParams(
            vmem_limit_bytes=VMEM_LIMIT, collective_id=4, has_side_effects=True
        ),
        cost_estimate=pl.CostEstimate(
            flops=10**9, bytes_accessed=8 * 10**7, transcendentals=0
        ),
        name="dispatch",
    )(mixed, output, rows, order.reshape(tokens, 1), weight, lent)
    return middle, arrived.reshape(tokens, features), far, near


def attention_backward(peers, saved, arrived, inverse, cot, output, gated, size):
    query, keys, values, logs, mixed = saved
    length, half = query.shape
    tokens, features = cot.shape
    parts, per, rows = half // 128, 128 // size, features // peers
    carried = (peers >> 3, 2, rows, features)
    shape, kind = jax.ShapeDtypeStruct, pltpu.SemaphoreType.DMA
    whole = lambda *form: pl.BlockSpec(form, lambda i: (0, 0), pipeline_mode=pl.Buffered(1))
    return pl.pallas_call(
        functools.partial(attention_backward_kernel, peers, size),
        grid=(parts,),
        out_shape=(
            shape((3, length, half), BF16),
            shape(carried, BF16),
            shape((tokens, features), F32),
            shape((peers, tokens // peers, features), BF16),
        ),
        in_specs=[column(length)] * 3
        + [
            pl.BlockSpec((1, per, length), lambda i: (i, 0, 0)),
            whole(tokens, features),
            whole(tokens, 1),
            whole(tokens, features),
            whole(features, features),
            whole(tokens, features),
            pl.BlockSpec(memory_space=pl.ANY),
        ],
        out_specs=(
            pl.BlockSpec((3, length, 128), lambda i: (0, 0, i)),
            pl.BlockSpec(carried, lambda i: (0, 0, 0, 0)),
            pl.BlockSpec((tokens, features), lambda i: (0, 0)),
            pl.BlockSpec(memory_space=pl.ANY),
        ),
        scratch_shapes=[
            pltpu.VMEM((length, size), F32),
            pltpu.VMEM((length, size), F32),
            pltpu.VMEM((2, parts, tokens, 128), BF16),
            pltpu.VMEM((tokens, features), BF16),
            kind((parts,)),
            kind((parts,)),
        ]
        + exchange_sems(peers)
        + halving_buffers(peers, rows, [features]),
        compiler_params=pltpu.CompilerParams(
            vmem_limit_bytes=VMEM_LIMIT, collective_id=1, has_side_effects=True
        ),
        cost_estimate=pl.CostEstimate(
            flops=20 * length * length * half, bytes_accessed=16 * length * half, transcendentals=0
        ),
        name="attention_backward",
    )(
        query,
        keys,
        values,
        logs,
        arrived,
        inverse.reshape(tokens, 1),
        cot,
        output,
        mixed,
        gated.reshape(peers, tokens // peers, features),
    )


def stream(step, steps, pairs, buffers, sems):
    def fetch(which):
        slot = lax.rem(which, 2)
        for m, refs in enumerate(pairs):
            first = 0
            for ref in refs:
                count = ref.shape[0] // CHUNK

                @pl.when(jnp.logical_and(which >= first, which < first + count))
                def _(m=m, ref=ref, first=first):
                    row = pl.multiple_of((which - first) * CHUNK, CHUNK)
                    pltpu.make_async_copy(
                        ref.at[pl.ds(row, CHUNK)], buffers[m].at[slot], sems.at[m, slot]
                    ).start()

                first += count

    @pl.when(step == 0)
    def _():
        fetch(step)

    @pl.when(step + 1 < steps)
    def _():
        fetch(step + 1)

    slot = lax.rem(step, 2)
    for m, refs in enumerate(pairs):
        pltpu.make_async_copy(
            refs[0].at[pl.ds(0, CHUNK)], buffers[m].at[slot], sems.at[m, slot]
        ).wait()
    return slot


def gelu_parts(inner):
    cdf = 0.5 * (1.0 + lax.erf(inner * 0.7071067811865476))
    slope = cdf + inner * (jnp.exp(-0.5 * inner * inner) * 0.3989422804014327)
    return inner * cdf, slope


def forward_first_kernel(steps, *refs):
    z_ref, gain_ref, shift_ref, out_bias_ref, gain_two, shift_two, bias_ref = refs[:7]
    win, wout = refs[7:11], refs[11:17]
    first_ref, normed_ref, active_ref, slope_ref, normed_two = refs[17:22]
    in_buf, out_buf, sems = refs[22:]
    step = pl.program_id(0)

    @pl.when(step == 0)
    def _():
        z = z_ref[...].astype(F32)
        xhat, _ = normalised(z)
        normed_ref[...] = (xhat * gain_ref[...] + shift_ref[...]).astype(BF16)
        first_ref[...] = jnp.broadcast_to(out_bias_ref[...], first_ref.shape)

    slot = stream(step, steps, (win, wout), (in_buf, out_buf), sems)
    active, slope = gelu_parts(dot_last(normed_ref[...], in_buf[slot]) + bias_ref[0])
    low = active.astype(BF16)
    slope_ref[...] = slope.astype(BF16)
    first_ref[...] += dot(low, out_buf[slot])

    @pl.when(step < steps // 2)
    def _():
        active_ref[...] = low

    @pl.when(step == steps - 1)
    def _():
        xhat, _ = normalised(z_ref[...].astype(F32) + first_ref[...])
        normed_two[...] = (xhat * gain_two[...] + shift_two[...]).astype(BF16)


def second_kernel(parts, steps, normed_ref, grad_ref, bias_ref, *refs):
    win, wout = refs[:parts], refs[parts : 2 * parts]
    part_ref, back_ref, active_ref, inner_ref = refs[2 * parts : 2 * parts + 4]
    total, back, in_buf, out_buf, sems = refs[2 * parts + 4 :]
    step = pl.program_id(0)

    @pl.when(step == 0)
    def _():
        total[...] = jnp.zeros_like(total)
        back[...] = jnp.zeros_like(back)

    slot = stream(step, steps, (win, wout), (in_buf, out_buf), sems)
    grad_active = dot_last(grad_ref[...], out_buf[slot])
    active, slope = gelu_parts(dot_last(normed_ref[...], in_buf[slot]) + bias_ref[0])
    low, inner = active.astype(BF16), (slope * grad_active).astype(BF16)
    active_ref[...] = low
    inner_ref[...] = inner
    total[...] += dot(low, out_buf[slot])
    back[...] += dot(inner, in_buf[slot])

    @pl.when(step == steps - 1)
    def _():
        part_ref[...] = total[...].astype(part_ref.dtype)
        back_ref[...] = back[...].astype(back_ref.dtype)


def weights_second_kernel(parts, steps, *refs):
    inner, active, normed, grad = refs[:2], refs[2:4], refs[4:6], refs[6:8]
    bias_ref = refs[8]
    gwin, gwout = refs[9 : 9 + parts], refs[9 + parts : 9 + 2 * parts]
    step = pl.program_id(0)
    per = steps // parts
    one, two = inner[0][...], inner[1][...]
    bias_ref[0] = jnp.sum(one.astype(F32), axis=0, keepdims=True) + jnp.sum(
        two.astype(F32), axis=0, keepdims=True
    )
    grad_in = (dot_first(one, normed[0][...]) + dot_first(two, normed[1][...])).astype(BF16)
    grad_out = (
        dot_first(active[0][...], grad[0][...]) + dot_first(active[1][...], grad[1][...])
    ).astype(BF16)
    for quarter in range(parts):

        @pl.when(step // per == quarter)
        def _():
            gwin[quarter][...] = grad_in
            gwout[quarter][...] = grad_out


def backward_first_kernel(steps, *refs):
    own_ref, arrived_ref, grad_two_ref, z_ref, first_ref, cot_ref = refs[:6]
    slope_ref, gain_ref, gain_two, centre_ref, _ = refs[6:11]
    win, wout = refs[11:15], refs[15:21]
    back_ref, grad_low, vector_ref, inner_ref = refs[21:25]
    total, in_buf, out_buf, sems = refs[25:]
    step = pl.program_id(0)
    down = lambda value: jnp.sum(value, axis=0, keepdims=True)

    @pl.when(step == 0)
    def _():
        total[...] = jnp.zeros_like(total)
        z = z_ref[...].astype(F32)
        xhat, rate = normalised(z + first_ref[...])
        grad_normed = own_ref[...] + arrived_ref[...].astype(F32)
        grad_rows = norm_back(grad_normed, xhat, rate, gain_two[...])
        back_ref[...] = grad_rows
        gate = jax.nn.sigmoid(jnp.sum(z * centre_ref[...], axis=-1, keepdims=True))
        low = (gate * cot_ref[...].astype(F32) + grad_rows).astype(BF16)
        grad_low[...] = low
        vector_ref[2:3] = down(low.astype(F32))
        vector_ref[3:4] = down(grad_normed * xhat)
        vector_ref[4:5] = down(grad_normed)
        vector_ref[5:6] = down(grad_two_ref[...].astype(F32))
        vector_ref[6:8] = jnp.zeros_like(vector_ref[6:8])

    slot = stream(step, steps, (win, wout), (in_buf, out_buf), sems)
    inner = (slope_ref[...].astype(F32) * dot_last(grad_low[...], out_buf[slot])).astype(BF16)
    total[...] += dot(inner, in_buf[slot])

    @pl.when(step < steps // 2)
    def _():
        inner_ref[...] = inner

    @pl.when(step == steps - 1)
    def _():
        xhat, rate = normalised(z_ref[...].astype(F32))
        grad_normed = total[...]
        vector_ref[0:1] = down(grad_normed * xhat)
        vector_ref[1:2] = down(grad_normed)
        back_ref[...] += norm_back(grad_normed, xhat, rate, gain_ref[...])


def weights_first_kernel(steps, *refs):
    inner_ref, active_ref, normed_ref, grad_ref, normed_far, grad_far, in_bias = refs[:7]
    pairs = refs[7:11]
    win, wout = refs[11:13], refs[13:15]
    bias_ref, gwin, gwout, sums = refs[15], refs[16:18], refs[18:20], refs[20:22]
    in_buf, out_buf, sems = refs[22:]
    step = pl.program_id(0)
    for m in range(2):
        sums[m][...] = pairs[2 * m][...].astype(F32) + pairs[2 * m + 1][...].astype(F32)
    slot = stream(step, steps, (win, wout), (in_buf, out_buf), sems)
    active, slope = gelu_parts(dot_last(normed_far[...], in_buf[slot]) + in_bias[0])
    inner = (slope * dot_last(grad_far[...], out_buf[slot])).astype(BF16)
    own = inner_ref[...]
    bias_ref[0] = jnp.sum(own.astype(F32), axis=0, keepdims=True) + jnp.sum(
        inner.astype(F32), axis=0, keepdims=True
    )
    grad_in = (dot_first(own, normed_ref[...]) + dot_first(inner, normed_far[...])).astype(BF16)
    grad_out = (
        dot_first(active_ref[...], grad_ref[...]) + dot_first(active.astype(BF16), grad_far[...])
    ).astype(BF16)
    for quarter in range(2):

        @pl.when(step // (steps // 2) == quarter)
        def _():
            gwin[quarter][...] = grad_in
            gwout[quarter][...] = grad_out


def expert_call(kernel, name, steps, inputs, weights, outs, scratch, flops):
    whole = lambda shape: pl.BlockSpec(shape, lambda c: (0,) * len(shape))
    spec = lambda shape, block, at: whole(shape) if block is None else pl.BlockSpec(block, at)
    if weights:
        features = weights[0].shape[-1]
        scratch = scratch + [
            pltpu.VMEM((2, CHUNK, features), BF16),
            pltpu.VMEM((2, CHUNK, features), BF16),
            pltpu.SemaphoreType.DMA((2, 2)),
        ]
    moved = sum(a.size * a.dtype.itemsize for a, _, _ in inputs + outs)
    return pl.pallas_call(
        kernel,
        grid=(steps,),
        out_shape=tuple(s for s, _, _ in outs),
        in_specs=[spec(a.shape, b, m) for a, b, m in inputs]
        + [pl.BlockSpec(memory_space=pl.ANY)] * len(weights),
        out_specs=tuple(spec(s.shape, b, m) for s, b, m in outs),
        scratch_shapes=scratch,
        compiler_params=pltpu.CompilerParams(vmem_limit_bytes=VMEM_LIMIT),
        cost_estimate=pl.CostEstimate(
            flops=2 * flops,
            bytes_accessed=moved + 2 * sum(w.size for w in weights),
            transcendentals=0,
        ),
        name=name,
    )(*[a for a, _, _ in inputs], *weights)


def expert(z, cot, vectors, biases, one, two, over, beside):
    rows, features = z.shape
    hidden = biases.shape[1]
    steps = hidden // CHUNK
    near = steps // 2
    line = lambda i: (vectors[i : i + 1], None, None)
    flat = lambda array: (array, None, None)
    shape = jax.ShapeDtypeStruct
    low_rows, wide_rows = flat(shape((rows, features), BF16)), flat(shape((rows, features), F32))
    wide = ((rows, CHUNK), lambda c: (0, c))
    thin = ((1, 1, CHUNK), lambda c: (c, 0, 0))
    chunked = biases.reshape(2, steps, 1, CHUNK)
    matmul = 2 * rows * hidden * features

    def quarter_outs(parts, count):
        per = count // parts
        return [
            (
                shape((per * CHUNK, features), BF16),
                (CHUNK, features),
                lambda c, q=q: (jnp.clip(c - q * per, 0, per - 1), 0),
            )
            for q in range(parts)
        ]

    lines = [line(i) for i in range(7)]
    held = ((rows, CHUNK), lambda c: (0, jnp.minimum(c, near - 1)))
    half_hidden = shape((rows, hidden // 2), BF16)
    wide_z, wide_cot = z.astype(F32), cot.astype(F32)
    gate = jax.nn.sigmoid(jnp.sum(wide_z * vectors[6], axis=-1, keepdims=True))
    grad_two = (gate * wide_cot).astype(BF16)
    grad_far = over(grad_two)
    first, normed_one, active_one, slope_one, normed_two = expert_call(
        functools.partial(forward_first_kernel, steps),
        "forward_first",
        steps,
        [flat(z)] + lines[:5] + [(chunked[0], *thin)],
        one[0] + one[1],
        [wide_rows, low_rows, (half_hidden, *held), (shape((rows, hidden), BF16), *wide), low_rows],
        [],
        2 * matmul,
    )
    normed_far = over(after(normed_two, grad_far))

    def second(normed, grad, kind):
        return expert_call(
            functools.partial(second_kernel, 2, near),
            "second",
            near,
            [flat(normed), flat(grad), (chunked[1, :near], *thin)],
            two[0] + two[1],
            [flat(shape((rows, features), kind))] * 2 + [(half_hidden, *wide)] * 2,
            [pltpu.VMEM((rows, features), F32)] * 2,
            2 * matmul,
        )

    own_part, grad_own_part, active_own, inner_own = second(normed_two, grad_two, F32)
    normed_one_far = over(after(normed_one, normed_far))
    normed_far = after(normed_far, inner_own)
    far_part, grad_far_part, active_far, inner_far = second(normed_far, grad_far, BF16)
    grad_far_part = after(grad_far_part, normed_one_far)
    outs = expert_call(
        functools.partial(weights_second_kernel, 2, near),
        "weights_second",
        near,
        [(a, *wide) for a in (inner_own, inner_far, active_own, active_far)]
        + [flat(a) for a in (normed_two, normed_far, grad_two, grad_far)],
        [],
        [(shape((near, 1, CHUNK), F32), *thin)] + quarter_outs(2, near) + quarter_outs(2, near),
        [],
        2 * matmul,
    )
    bias_two, gwin_two, gwout_two = outs[0].reshape(hidden // 2), outs[1:3], outs[3:5]

    grad_arrived = over(grad_far_part)
    far_arrived = over(after(far_part, grad_arrived))
    back, grad_one, sums, inner_one = expert_call(
        functools.partial(backward_first_kernel, steps),
        "backward_first",
        steps,
        [flat(a) for a in (grad_own_part, grad_arrived, grad_two, z, first, cot)]
        + [(slope_one, *wide), line(0), line(3), line(6), flat(outs[0])],
        one[0] + one[1],
        [wide_rows, low_rows, flat(shape((8, features), F32)), (half_hidden, *held)],
        [pltpu.VMEM((rows, features), F32)],
        2 * matmul,
    )
    grad_one_far = over(grad_one)
    branch = first + (own_part + far_arrived.astype(F32) + vectors[5])
    gated = (gate * branch).astype(BF16)
    grad_gate = jnp.sum(wide_cot * branch, axis=-1, keepdims=True)
    score = grad_gate * gate * (1.0 - gate)
    grad_sent = (back + score * vectors[6]).astype(BF16)
    grad_centre = jnp.sum(score * wide_z, axis=0, keepdims=True)
    strip_rows = gwin_two[0].shape[0] // near
    strip = ((strip_rows, features), lambda c: (c, 0))
    outs = expert_call(
        functools.partial(weights_first_kernel, near),
        "weights_first",
        near,
        [(inner_one, *wide), (active_one, *wide)]
        + [flat(a) for a in (normed_one, grad_one, normed_one_far, grad_one_far)]
        + [(chunked[0, :near], *thin)]
        + [
            (array, *strip)
            for mine, other in (gwin_two, gwout_two)
            for array in (mine, beside(other))
        ],
        one[0][:2] + one[1][:2],
        [(shape((near, 1, CHUNK), F32), *thin)]
        + quarter_outs(2, near)
        + quarter_outs(2, near)
        + [(shape(gwin_two[0].shape, F32), *strip)] * 2,
        [],
        3 * matmul,
    )
    bias_one = outs[0].reshape(hidden // 2)
    sums = jnp.concatenate([sums[:6], grad_centre], axis=0)
    grads = [(outs[1], outs[2]), (outs[3], outs[4])]
    return gated, grad_sent, sums, jnp.stack([bias_one, bias_two]), grads, outs[5:]


def project_back_kernel(peers, *refs):
    stages = bits_of(peers)
    d_ref, w_ref, normed_ref, own_hbm, other_hbm, middle_hbm, gain_ref = refs[:7]
    ours, theirs = refs[7:9], refs[9:11]
    place_ref, gated_ref, start_hbm = refs[11:14]
    term_ref, small_ref, lent_ref = refs[14:17]
    grad_refs, tail_ref, out_ref, pair_refs = refs[17:20], refs[20], refs[21], refs[22:24]
    layer_ref, term_out, small_out = refs[24:27]
    refs = refs[27:]
    held = [refs[i * stages : (i + 1) * stages] for i in range(4)]
    landed = [refs[i * stages : (i + 1) * stages] for i in range(4, 8)]
    reducer = Halving(peers, held, landed, *refs[8 * stages : 8 * stages + 2])
    refs = refs[8 * stages + 2 :]
    rows_send, rows_recv, rows_own, shard_send, shard_recv, tail_send, tail_recv = refs[:7]
    turned, seq_ref, middle_ref, far_send, far_recv, local = refs[7:13]
    pair_in, pair_out, in_sems, out_sems, start_ref = refs[13:18]
    term_recv, small_near, small_sum, small_far, side_sends, side_recvs = refs[18:24]
    term_send, term_sends, term_recvs = refs[24:27]
    later = stages - 2
    term_held = [None, None, term_ref, *refs[27 : 26 + later]]
    term_landed = [None, None, *refs[26 + later :]]
    output_terms = Halving(peers, [term_held], [term_landed], term_sends, term_recvs)
    start_copy = pltpu.make_async_copy(start_hbm, start_ref, local.at[3])
    start_copy.start()
    seq = lax.axis_index("seq")
    tokens, features = middle_ref.shape
    half = d_ref.shape[2]
    across = {"seq": 1 - seq}
    own_copy = pltpu.make_async_copy(own_hbm, seq_ref.at[0], local.at[0])
    other_copy = pltpu.make_async_copy(other_hbm, seq_ref.at[1], local.at[2])
    middle_copy = pltpu.make_async_copy(middle_hbm, middle_ref, local.at[1])
    own_copy.start()
    other_copy.start()
    middle_copy.start()

    piece = pair_in.shape[2]
    pieces = [(m, at) for m in range(2) for at in range(0, ours[0].shape[0], piece)]
    place = lambda ref, at: ref.at[pl.ds(at, piece)]

    def pair_inputs(i):
        m, at = pieces[i]
        return [
            pltpu.make_async_copy(
                place(ref[m], at), pair_in.at[i % 2, side], in_sems.at[i % 2, side]
            )
            for side, ref in enumerate((ours, theirs))
        ]

    def pair_output(i):
        m, at = pieces[i]
        return pltpu.make_async_copy(
            pair_out.at[i % 2], place(pair_refs[m], at), out_sems.at[i % 2]
        )

    def pair_add(count):
        for i in range(added[0], min(added[0] + count, len(pieces))):
            for copy in pair_inputs(i):
                copy.wait()
            if i >= 2:
                pair_output(i - 2).wait()
            pair_out[i % 2] = pair_in[i % 2, 0].astype(F32) + pair_in[i % 2, 1].astype(F32)
            pair_output(i).start()
            if i + 2 < len(pieces):
                for copy in pair_inputs(i + 2):
                    copy.start()
        added[0] = min(added[0] + count, len(pieces))

    added = [0]
    for i in range(2):
        for copy in pair_inputs(i):
            copy.start()
    turned[...] = normed_ref[...].T
    terms = dot(turned[...], d_ref[0])
    greet(reducer.partner + [across])
    reducer.put(0, terms)
    output_terms.copy(0, 2).start()
    term_copy = remote(term_send, term_recv, side_sends.at[0], side_recvs.at[0], across)
    near_copy = remote(
        lent_ref, small_near, side_sends.at[1], side_recvs.at[1], reducer.partner[0]
    )
    far_copy = remote(small_sum, small_far, side_sends.at[2], side_recvs.at[2], across)
    near_copy.start()
    block = lambda which: pl.ds(pl.multiple_of(which * tokens, tokens), tokens)

    def grad_rows(which):
        total = dot_last(d_ref[0, block(which), :], w_ref[:, :half])
        total += dot_last(d_ref[1, block(which), :], w_ref[:, half : 2 * half])
        return total + dot_last(d_ref[2, block(which), :], w_ref[:, 2 * half : 3 * half])

    def norm_sums(which, grad):
        xhat, _ = normalised(seq_ref[which].astype(F32))
        return jnp.sum(grad * xhat, axis=0, keepdims=True), jnp.sum(grad, axis=0, keepdims=True)

    far = grad_rows(1 - seq)
    rows_send[...] = far.astype(BF16)
    rows_copy = remote(rows_send, rows_recv, far_send.at[0], far_recv.at[0], across)
    rows_copy.start()
    for chunk in range(1, 3):
        reducer.put(chunk, dot(turned[...], d_ref[chunk]))
        reducer.finish(chunk - 1, 0)
    reducer.finish(2, 0)
    near_copy.wait()
    small_sum[...] = small_ref[...] + small_near[...]
    far_copy.start()
    own_copy.wait()
    other_copy.wait()
    far_one, far_two = norm_sums(1, far)
    own = grad_rows(seq)
    rows_own[...] = own
    own_one, own_two = norm_sums(0, own)
    line = lambda value: jnp.broadcast_to(value, (64, features))
    lines = jnp.concatenate([line(far_one + own_one), line(far_two + own_two)], axis=0)
    reducer.put(3, lines.T)
    results = [None] * 4
    for time in range(1, stages + 3):
        pair_add(1)
        if time == 2:
            start_copy.wait()
            layer_ref[...] = (start_ref[...] + placed(place_ref, gated_ref[...])).astype(BF16)
        if time + 1 < stages:
            total = output_terms.finish(0, time + 1)
            if time + 2 == stages:
                term_send[...] = total
                term_copy.start()
        for chunk in range(4):
            s = time - chunk if chunk < 3 else time - 2
            if (1 if chunk < 3 else 0) <= s < stages:
                results[chunk] = reducer.finish(chunk, s)
    for chunk in range(3):
        shard_send[chunk] = results[chunk].astype(BF16)
    tail_send[...] = results[3]
    shard_copy = remote(shard_send, shard_recv, far_send.at[1], far_recv.at[1], across)
    tail_copy = remote(tail_send, tail_recv, far_send.at[2], far_recv.at[2], across)
    shard_copy.start()
    tail_copy.start()
    pair_add(len(pieces))
    for i in range(len(pieces) - 2, len(pieces)):
        pair_output(i).wait()
    rows_copy.wait_recv()
    middle_copy.wait()
    xhat, rate = normalised(seq_ref[0].astype(F32))
    grad = rows_own[...] + rows_recv[...].astype(F32)
    out_ref[...] = middle_ref[...] + norm_back(grad, xhat, rate, gain_ref[...])
    columns = lambda which: pl.ds(pl.multiple_of(which * half, half), half)
    shard_copy.wait_recv()
    tail_copy.wait_recv()
    for chunk in range(3):
        grad_refs[chunk][:, columns(seq)] = shard_send[chunk].astype(F32)
        grad_refs[chunk][:, columns(1 - seq)] = shard_recv[chunk].astype(F32)
    tail_ref[...] = tail_send[...] + tail_recv[...]
    term_copy.wait()
    term_out[...] = term_send[...] + term_recv[...]
    far_copy.wait()
    small_out[...] = small_sum[...] + small_far[...]
    rows_copy.wait_send()
    shard_copy.wait_send()
    tail_copy.wait_send()
    reducer.drain(4, range(stages))
    output_terms.drain(1, range(2, stages))


def project_back(peers, grads, weight, normed, rows_own, rows_far, grad_middle, gain, pairs, forward, terms):
    tokens, features = grad_middle.shape
    half = grads.shape[2]
    rows, stages = features // peers, bits_of(peers)
    shape = jax.ShapeDtypeStruct
    return pl.pallas_call(
        functools.partial(project_back_kernel, peers),
        out_shape=[shape((rows, features), F32)] * 3
        + [shape((rows, 128), F32), shape((tokens, features), F32)]
        + [shape(array.shape, F32) for array, _ in pairs]
        + [shape((tokens, features), BF16)]
        + [shape((rows, features), F32), shape(terms[1].shape, F32)],
        in_specs=[pl.BlockSpec(memory_space=pltpu.VMEM)] * 3
        + [pl.BlockSpec(memory_space=pl.ANY)] * 3
        + [pl.BlockSpec(memory_space=pltpu.VMEM)]
        + [pl.BlockSpec(memory_space=pl.ANY)] * 4
        + [pl.BlockSpec(memory_space=pltpu.VMEM)] * 2
        + [pl.BlockSpec(memory_space=pl.ANY)]
        + [pl.BlockSpec(memory_space=pltpu.VMEM)] * 3,
        out_specs=[pl.BlockSpec(memory_space=pltpu.VMEM)] * 5
        + [pl.BlockSpec(memory_space=pl.ANY)] * 2
        + [pl.BlockSpec(memory_space=pltpu.VMEM)] * 3,
        scratch_shapes=halving_buffers(peers, rows, [half, half, half, 128])
        + [
            pltpu.VMEM((tokens, features), BF16),
            pltpu.VMEM((tokens, features), BF16),
            pltpu.VMEM((tokens, features), F32),
            pltpu.VMEM((3, rows, half), BF16),
            pltpu.VMEM((3, rows, half), BF16),
            pltpu.VMEM((rows, 128), F32),
            pltpu.VMEM((rows, 128), F32),
            pltpu.VMEM(normed.shape[::-1], BF16),
            pltpu.VMEM((2, tokens, features), BF16),
            pltpu.VMEM((tokens, features), F32),
            pltpu.SemaphoreType.DMA((3,)),
            pltpu.SemaphoreType.DMA((3,)),
            pltpu.SemaphoreType.DMA((4,)),
            pltpu.VMEM((2, 2, 256, features), BF16),
            pltpu.VMEM((2, 256, features), F32),
            pltpu.SemaphoreType.DMA((2, 2)),
            pltpu.SemaphoreType.DMA((2,)),
            pltpu.VMEM((tokens, features), F32),
            pltpu.VMEM((rows, features), F32),
        ]
        + [pltpu.VMEM(terms[1].shape, F32)] * 3
        + [pltpu.SemaphoreType.DMA((3,))] * 2
        + [pltpu.VMEM((rows, features), F32)]
        + [pltpu.SemaphoreType.DMA((1, stages))] * 2
        + [pltpu.VMEM((peers >> (s + 1), 2, rows, features), BF16) for s in range(3, stages)]
        + [pltpu.VMEM((peers >> (s + 1), rows, features), BF16) for s in range(2, stages)],
        compiler_params=pltpu.CompilerParams(
            vmem_limit_bytes=VMEM_LIMIT, collective_id=0, has_side_effects=True
        ),
        cost_estimate=pl.CostEstimate(
            flops=60 * 10**9, bytes_accessed=40 * 10**6, transcendentals=0
        ),
        name="project_back",
    )(
        grads,
        weight,
        normed,
        rows_own,
        rows_far,
        grad_middle,
        gain,
        *[mine for mine, _ in pairs],
        *[other for _, other in pairs],
        *forward,
        *terms,
    )


def body(
    inputs,
    ln_gain,
    ln_shift,
    w_query,
    w_key,
    w_value,
    w_output,
    exp_gain1,
    exp_shift1,
    w_in1,
    b_in1,
    w_out1,
    b_out1,
    exp_gain2,
    exp_shift2,
    w_in2,
    b_in2,
    w_out2,
    b_out2,
    centroid,
    order,
    inverse,
    cotangent,
):
    seq, peer = lax.axis_index("seq"), lax.axis_index("fsdp")
    peers = lax.axis_size("fsdp")
    rows = inputs[0]
    tokens, features = rows.shape
    half = features // 2
    size = features // HEADS
    left, even = seq == 0, lax.rem(peer, 2) == 0
    over = lambda value: swapped(value, "seq")
    beside = lambda value: swapped(value, "fsdp")
    ordered = lambda flag, mine, other, axis: jnp.where(
        flag, jnp.concatenate([mine, other], axis), jnp.concatenate([other, mine], axis)
    )

    columns = lambda w: lax.dynamic_slice_in_dim(w, seq * half, half, 1)
    norm_vectors = jnp.pad(jnp.stack([ln_gain, ln_shift], axis=1), ((0, 0), (0, 126)))
    own_vectors = jnp.concatenate(
        [exp_gain1, exp_shift1, b_out1, exp_gain2, exp_shift2, b_out2, centroid], axis=0
    )
    own_biases = jnp.concatenate([b_in1, b_in2], axis=0)
    gathered, output_full, other_rows, far_in, pair, near_in, near_out = gather(
        peers,
        jnp.concatenate([columns(w_query), columns(w_key), columns(w_value), norm_vectors], axis=1),
        w_output,
        rows,
        w_in1[0],
        jnp.concatenate([own_vectors.reshape(-1), own_biases.reshape(-1)]).reshape(-1, 128),
        w_out1[0],
    )
    pair = pair.reshape(-1)
    other_vectors = pair[: own_vectors.size].reshape(own_vectors.shape)
    other_biases = pair[own_vectors.size :].reshape(own_biases.shape)
    vectors = ordered(even, own_vectors, other_vectors, 1).astype(F32)

    quarter = w_in1.shape[1]
    pick = lambda table, which: lax.dynamic_slice_in_dim(table, which * quarter, quarter, 1)
    biases = jnp.concatenate(
        [
            pick(own_biases, seq),
            pick(other_biases, seq),
            pick(own_biases, 1 - seq),
            pick(other_biases, 1 - seq),
        ],
        axis=1,
    ).astype(F32)

    two = ([w_in2[0], beside(w_in2[0])], [w_out2[0], beside(w_out2[0])])
    cot = cotangent[0]
    exchange = lambda value: lax.all_to_all(
        value.reshape(peers, tokens // peers, features),
        "fsdp",
        split_axis=0,
        concat_axis=0,
        tiled=True,
    ).reshape(tokens, features)


    outs = attention_forward(peers, rows, other_rows, gathered, cot, order, w_out1[0], far_in, size)
    mixed, logs, cot_slots, far_out_a, cross_in, normed, gain, query, keys, values = outs
    cot_slots = cot_slots.reshape(tokens, features)
    middle, z, far_out_b, cross_out_a = dispatch(
        peers, mixed, output_full, rows, order, w_out1[0], far_out_a
    )
    one = (
        [w_in1[0], near_in, far_in, cross_in],
        [w_out1[0], near_out, far_out_a, far_out_b, cross_out_a, beside(far_out_b)],
    )

    gated, grad_sent, vector_grads, bias_grads, grads_one, grads_two = expert(
        z, cot_slots, vectors, biases, one, two, over, beside
    )
    returned = exchange(grad_sent)

    own_half = lambda table, which: lax.dynamic_slice_in_dim(table, which * half, half, 1)
    core = lax.rem(peer, 2)
    bias_quarters = jnp.pad(bias_grads, ((0, 0), (0, 2 * quarter))).reshape(2, 4, quarter)
    bias_rows = lambda first: ordered(left, bias_quarters[:, first], bias_quarters[:, first + 2], 1)
    flat = lambda table, bias: jnp.concatenate([table.reshape(-1), bias.reshape(-1)])
    small = flat(own_half(vector_grads, core), bias_rows(0)).reshape(-1, 128)
    lent = flat(own_half(vector_grads, 1 - core), bias_rows(1)).reshape(-1, 128)

    parts, wo_terms, grad_middle, home = attention_backward(
        peers, (query, keys, values, logs, mixed), returned, inverse, cot, output_full, gated, size
    )
    home = home.reshape(tokens, features)
    outs = project_back(
        peers,
        parts,
        gathered,
        normed,
        rows,
        other_rows,
        grad_middle,
        gain[:1],
        [(mine, beside(near)) for mine, near in grads_one],
        (inverse.reshape(tokens, 1), home, middle),
        (wo_terms, small, lent),
    )
    grad_q, grad_k, grad_v, norm_grads, grad_inputs = outs[:5]
    grad_win_one, grad_wout_one, layer_out, grad_wo, small = outs[5:]
    small = small.reshape(-1)
    count = vector_grads.shape[0]
    vector_out = small[: count * half].reshape(count, 1, half)
    bias_out = small[count * half :].reshape(2, 1, 2 * quarter)
    grad_win_two, grad_wout_two = grads_two
    return (
        layer_out[None],
        grad_inputs[None],
        norm_grads[:, 0],
        norm_grads[:, 64],
        grad_q,
        grad_k,
        grad_v,
        grad_wo,
        vector_out[0],
        vector_out[1],
        grad_win_one[None],
        bias_out[0],
        grad_wout_one[None],
        vector_out[2],
        vector_out[3],
        vector_out[4],
        grad_win_two[None],
        bias_out[1],
        grad_wout_two[None],
        vector_out[5],
        vector_out[6],
    )


def solution(mesh):
    both, rows, vector = P("fsdp", "seq", None), P("fsdp", None), P("fsdp")
    return jax.shard_map(
        body,
        mesh=mesh,
        in_specs=(both, vector, vector, rows, rows, rows, rows)
        + (rows, rows, both, rows, both, rows) * 2
        + (rows, P("fsdp", "seq"), P("fsdp", "seq"), both),
        out_specs=(both, both, vector, vector, rows, rows, rows, rows)
        + (rows, rows, both, rows, both, rows) * 2
        + (rows,),
        check_vma=False,
    )
```

```python
import functools

import jax
import jax.numpy as jnp
from jax import lax
from jax.experimental import pallas as pl
from jax.experimental.pallas import tpu as pltpu
from jax.sharding import PartitionSpec as P

HEADS = 16
EPS = 1e-05
MASKED = -1e30
BLOCK = 256
CHUNK = 512
BF16 = jnp.bfloat16
F32 = jnp.float32
VMEM_LIMIT = 56 * 1024 * 1024
MESH = pl.DeviceIdType.MESH


def swapped(value, axis):
    pairs = [(source, source ^ 1) for source in range(lax.axis_size(axis))]
    return lax.ppermute(value, axis, pairs)


def after(value, *others):
    return lax.optimization_barrier((value, *others))[0]


def dot_last(left, right):
    return lax.dot_general(left, right, (((1,), (1,)), ((), ())), preferred_element_type=F32)


def dot_first(left, right):
    return lax.dot_general(left, right, (((0,), (0,)), ((), ())), preferred_element_type=F32)


def dot(left, right):
    return jnp.dot(left, right, preferred_element_type=F32)


def normalised(values):
    centred = values - jnp.mean(values, axis=-1, keepdims=True)
    spread = jnp.mean(centred * centred, axis=-1, keepdims=True)
    rate = lax.rsqrt(spread + EPS)
    return centred * rate, rate


def norm_back(grad, xhat, rate, gain):
    scaled = grad * gain
    inner = jnp.mean(scaled * xhat, axis=-1, keepdims=True)
    return rate * (scaled - jnp.mean(scaled, axis=-1, keepdims=True) - xhat * inner)


def bits_of(peers):
    return peers.bit_length() - 1


def greet(partners):
    barrier = pltpu.get_barrier_semaphore()
    for device in partners:
        pl.semaphore_signal(barrier, inc=1, device_id=device, device_id_type=MESH)
    pl.semaphore_wait(barrier, len(partners))


def remote(source, target, sends, recvs, device):
    return pltpu.make_async_remote_copy(
        src_ref=source,
        dst_ref=target,
        send_sem=sends,
        recv_sem=recvs,
        device_id=device,
        device_id_type=MESH,
    )


class Halving:
    def __init__(self, peers, held, landed, sends, recvs):
        peer = lax.axis_index("fsdp")
        self.stages = bits_of(peers)
        self.bit = [lax.rem(peer // (1 << s), 2) for s in range(self.stages)]
        self.partner = [
            {"fsdp": peer + (1 - 2 * self.bit[s]) * (1 << s)} for s in range(self.stages)
        ]
        self.held, self.landed, self.sends, self.recvs = held, landed, sends, recvs

    def copy(self, chunk, s):
        return remote(
            self.held[chunk][s].at[:, 1 - self.bit[s]],
            self.landed[chunk][s],
            self.sends.at[chunk, s],
            self.recvs.at[chunk, s],
            self.partner[s],
        )

    def start(self, chunk):
        self.copy(chunk, 0).start()

    def put(self, chunk, value):
        self.held[chunk][0][...] = value.astype(BF16).reshape(self.held[chunk][0].shape)
        self.start(chunk)

    def total(self, chunk, s):
        self.copy(chunk, s).wait_recv()
        mine = self.held[chunk][s][:, self.bit[s]].astype(F32)
        return mine + self.landed[chunk][s][...].astype(F32)

    def finish(self, chunk, s):
        total = self.total(chunk, s)
        if s + 1 < self.stages:
            held = self.held[chunk][s + 1]
            held[...] = total.astype(BF16).reshape(held.shape)
            self.copy(chunk, s + 1).start()
        return total[0]

    def drain(self, chunks, stages):
        for chunk in range(chunks):
            for s in stages:
                self.copy(chunk, s).wait_send()


def halving_buffers(peers, rows, widths, first=True):
    stages = bits_of(peers)
    held = [
        pltpu.VMEM((peers >> (s + 1), 2, rows, w), BF16)
        for w in widths
        for s in range(0 if first else 1, stages)
    ]
    landed = [pltpu.VMEM((peers >> (s + 1), rows, w), BF16) for w in widths for s in range(stages)]
    return held + landed + [pltpu.SemaphoreType.DMA((len(widths), stages))] * 2


class Exchange:
    def __init__(self, peers, source, target, sends, recvs, local):
        self.peers, self.peer = peers, lax.axis_index("fsdp")
        self.source, self.target = source, target
        self.sends, self.recvs, self.local = sends, recvs, local
        ring = [lax.rem(self.peer + d, peers) for d in range(peers)]
        self.others = [{"fsdp": device} for device in ring[1:]]
        self.ring = ring

    def copy(self, d):
        return remote(
            self.source.at[self.ring[d]],
            self.target.at[self.peer],
            self.sends.at[d],
            self.recvs.at[d],
            self.others[d - 1],
        )

    def own(self):
        return pltpu.make_async_copy(
            self.source.at[self.peer], self.target.at[self.peer], self.local
        )

    def start(self):
        for d in range(1, self.peers):
            self.copy(d).start()
        self.own().start()

    def wait(self):
        for d in range(1, self.peers):
            self.copy(d).wait()
        self.own().wait()


def exchange_sems(peers):
    kind = pltpu.SemaphoreType.DMA
    return [kind((peers,)), kind((peers,)), kind]


def gather_kernel(peers, *refs):
    first_ref, second_ref, rows_ref, far_ref, pair_ref, other_ref = refs[:6]
    first_out, second_out, rows_out, far_out, pair_out, near_in, near_out = refs[6:13]
    sends, recvs, local, far_sends, far_recvs = refs[13:]
    stages = bits_of(peers)
    across = {"seq": 1 - lax.axis_index("seq")}
    peer = lax.axis_index("fsdp")
    bits = list(range(stages))[::-1]
    mixed = [1] + [b for b in bits if b > 1] + [0]
    pieces = [
        (first_ref, first_out, 0, bits, 0),
        (first_ref, first_out, 1, bits, 1),
        (second_ref, second_out, 0, mixed, 0),
    ]
    value = {b: lax.rem(peer // (1 << b), 2) for b in bits}
    partner = {b: {"fsdp": peer + (1 - 2 * value[b]) * (1 << b)} for b in bits}
    own = [
        pltpu.make_async_copy(source, target.at[pl.ds(peer, 1)], local.at[i])
        for i, (source, target) in enumerate([(first_ref, first_out), (second_ref, second_out)])
    ]
    for each in own:
        each.start()
    greet([partner[b] for b in bits] + [across])
    far = [
        remote(source, target, far_sends.at[i], far_recvs.at[i], device)
        for i, (source, target, device) in enumerate(
            [
                (rows_ref, rows_out, across),
                (far_ref, far_out, across),
                (pair_ref, pair_out, partner[0]),
                (far_ref, near_in, partner[0]),
                (other_ref, near_out, partner[0]),
            ]
        )
    ]
    for each in far:
        each.start()

    def copy(which, k):
        source, target, piece, order, _ = pieces[which]
        view = target.reshape(*[2] * stages, *target.shape[1:])
        held = view.at[
            tuple(slice(None) if b in order[:k] else value[b] for b in bits) + (piece,)
        ]
        return remote(
            held if k else source.at[0, piece],
            held,
            sends.at[which, k],
            recvs.at[which, k],
            partner[order[k]],
        )

    for time in range(stages + 2):
        if time == 1:
            for each in own:
                each.wait()
        for which in range(len(pieces)):
            k = time - pieces[which][4]
            if 1 <= k <= stages:
                copy(which, k - 1).wait_recv()
            if 0 <= k < stages:
                copy(which, k).start()
    for which in range(len(pieces)):
        for k in range(stages):
            copy(which, k).wait_send()
    for each in far:
        each.wait()


def gather(peers, first, second, rows, weight, lent, other):
    stages = bits_of(peers)
    shape = lambda a, pieces: (pieces, a.shape[0] // pieces, a.shape[1])
    arrays = [(first, shape(first, 2)), (second, shape(second, 1))]
    outs = pl.pallas_call(
        functools.partial(gather_kernel, peers),
        out_shape=[jax.ShapeDtypeStruct((peers, *form), BF16) for _, form in arrays]
        + [
            jax.ShapeDtypeStruct(rows.shape, BF16),
            *[jax.ShapeDtypeStruct(a.shape, BF16) for a in (weight, lent, weight, other)],
        ],
        in_specs=[pl.BlockSpec(memory_space=pl.ANY)] * 6,
        out_specs=[pl.BlockSpec(memory_space=pl.ANY)] * 7,
        scratch_shapes=[
            pltpu.SemaphoreType.DMA((3, stages)),
            pltpu.SemaphoreType.DMA((3, stages)),
            pltpu.SemaphoreType.DMA((2,)),
            pltpu.SemaphoreType.DMA((5,)),
            pltpu.SemaphoreType.DMA((5,)),
        ],
        compiler_params=pltpu.CompilerParams(collective_id=2, has_side_effects=True),
        cost_estimate=pl.CostEstimate(
            flops=0, bytes_accessed=40 * first.size * peers, transcendentals=0
        ),
        name="gather",
    )(*[a.reshape(1, *form) for a, form in arrays], rows, weight, lent, other)
    return [out.reshape(-1, a.shape[1]) for out, (a, _) in zip(outs, arrays)] + list(outs[2:])


def causal_mask(scores):
    keys = lax.broadcasted_iota(jnp.int32, scores.shape, 0)
    queries = lax.broadcasted_iota(jnp.int32, scores.shape, 1)
    return jnp.where(keys <= queries, scores, MASKED)


def attention_forward_kernel(peers, size, *refs):
    rows_ref, other_ref, vector_ref = refs[:3]
    weights, cot_ref, order_ref, halves = refs[3:6], refs[6], refs[7], refs[8:10]
    mixed_ref, log_ref, arrived_ref, far_refs = refs[10], refs[11], refs[12], refs[13:15]
    normed_ref, gain_ref, q_ref, k_ref, v_ref = refs[15:20]
    o_all, o_far, mixed, slots_ref, sends, recvs, weight_sems, *exchange_refs = refs[20:]
    step, steps = pl.program_id(0), o_far.shape[0]
    length, tokens = q_ref.shape[0], o_far.shape[1]
    seq = lax.axis_index("seq")
    across = {"seq": 1 - seq}
    exchange = Exchange(peers, slots_ref, arrived_ref, *exchange_refs)
    beside = {"fsdp": exchange.peer + 1 - 2 * lax.rem(exchange.peer, 2)}
    copies = [
        remote(
            source.at[pl.ds(0, target.shape[0])],
            target,
            weight_sems.at[0, i],
            weight_sems.at[1, i],
            device,
        )
        for i, (source, target, device) in enumerate(zip(halves, far_refs, (across, beside)))
    ]

    def block(which):
        column = pl.multiple_of((seq * steps + which) * 128, 128)
        return remote(
            o_far.at[which],
            mixed.at[:, pl.ds(column, 128)],
            sends.at[which],
            recvs.at[which],
            across,
        )

    @pl.when(step == 0)
    def _():
        slots_ref[...] = placed(order_ref, cot_ref[...]).astype(BF16).reshape(slots_ref.shape)
        greet(exchange.others + [across])
        for each in copies:
            each.start()
        exchange.start()
        lines = vector_ref[...].astype(F32).T
        gain_ref[...] = jnp.broadcast_to(lines[0:1], gain_ref.shape)
        for which, source in ((seq, rows_ref), (1 - seq, other_ref)):
            xhat, _ = normalised(source[...].astype(F32))
            place = pl.ds(pl.multiple_of(which * tokens, tokens), tokens)
            normed_ref[place, :] = (xhat * lines[0:1] + lines[1:2]).astype(BF16)

    for target, matrix in zip((q_ref, k_ref, v_ref), weights):
        target[...] = dot(normed_ref[...], matrix[...]).astype(BF16)
    for head in range(q_ref.shape[1] // size):
        lanes = slice(head * size, (head + 1) * size)
        for start in range(0, length, BLOCK):
            query = q_ref[start : start + BLOCK, lanes] * BF16(size**-0.5)
            last = causal_mask(dot_last(k_ref[start : start + BLOCK, lanes], query))
            peak = jnp.max(last, axis=0, keepdims=True)
            if start:
                early = dot_last(k_ref[:start, lanes], query)
                peak = jnp.maximum(peak, jnp.max(early, axis=0, keepdims=True))
            last = jnp.exp(last - peak)
            total = jnp.sum(last, axis=0, keepdims=True)
            out = dot_first(v_ref[start : start + BLOCK, lanes], last.astype(BF16))
            if start:
                early = jnp.exp(early - peak)
                total = total + jnp.sum(early, axis=0, keepdims=True)
                out = out + dot_first(v_ref[:start, lanes], early.astype(BF16))
            at = start % tokens
            o_all[start // tokens, at : at + BLOCK, lanes] = (out / total).T.astype(BF16)
            log_ref[0, head : head + 1, start : start + BLOCK] = peak + jnp.log(total)
    column = pl.multiple_of((seq * steps + step) * 128, 128)
    mixed[:, pl.ds(column, 128)] = o_all[seq]
    o_far[step] = o_all[1 - seq]
    block(step).start()

    @pl.when(step == steps - 1)
    def _():
        for which in range(o_far.shape[0]):
            block(which).wait()
        mixed_ref[...] = mixed[...]
        for each in copies:
            each.wait()
        exchange.wait()


def placed(places_ref, rows):
    tokens = places_ref.shape[0]
    columns = lax.broadcasted_iota(jnp.int32, (tokens, tokens), 1)
    return dot(jnp.where(columns == places_ref[...], 1.0, 0.0).astype(BF16), rows)


def attention_backward_kernel(peers, size, *refs):
    q_ref, k_ref, v_ref, log_ref, arrived_ref, place_ref, cot_ref, w_ref, mixed_ref = refs[:9]
    gated_ref = refs[9]
    d_ref, sum_ref, middle_ref, home_ref = refs[10:14]
    dk_sum, dv_sum, grads, grad_all, far_sends, far_recvs = refs[14:20]
    exchange = Exchange(peers, gated_ref, home_ref, *refs[20:23])
    refs = refs[23:]
    stages = bits_of(peers)
    reducer = Halving(
        peers, [refs[:stages]], [refs[stages : 2 * stages]], *refs[2 * stages :]
    )
    step, steps = pl.program_id(0), 4
    parts, tokens = grads.shape[1], grads.shape[2]
    seq = lax.axis_index("seq")
    across = {"seq": 1 - seq}
    columns = lambda side, which: pl.ds(
        pl.multiple_of((side * parts + which) * 128, 128), 128
    )

    def block(which):
        return remote(
            grad_all.at[:, columns(1 - seq, which)],
            grads.at[seq, which],
            far_sends.at[which],
            far_recvs.at[which],
            across,
        )

    @pl.when(step == 0)
    def _():
        greet(exchange.others + [across])
        middle = cot_ref[...].astype(F32) + placed(place_ref, arrived_ref[...])
        middle_ref[...] = middle
        low = middle.astype(BF16)
        grad_all[...] = dot_last(low, w_ref[...]).astype(BF16)
        for which in range(parts):
            block(which).start()
        for which in range(parts):
            grads[seq, which] = grad_all[:, columns(seq, which)]
        reducer.put(0, dot_first(mixed_ref[...], low))
        exchange.start()

    block(step).wait()

    @pl.when(step == 1)
    def _():
        reducer.finish(0, 0)

    length = q_ref.shape[0]
    scale = size**-0.5
    for head in range(q_ref.shape[1] // size):
        lanes = slice(head * size, (head + 1) * size)
        dk_sum[...] = jnp.zeros_like(dk_sum)
        dv_sum[...] = jnp.zeros_like(dv_sum)
        for start in range(0, length, BLOCK):
            rows = slice(start, start + BLOCK)
            query = q_ref[rows, lanes] * BF16(scale)
            grad = grads[start // tokens, step, start % tokens : start % tokens + BLOCK, lanes]
            log_total = log_ref[0, head : head + 1, rows]
            spans = ([slice(0, start)] if start else []) + [rows]
            probs, weighted = [], []
            inner = jnp.zeros((1, BLOCK), F32)
            for span in spans:
                scores = dot_last(k_ref[span, lanes], query)
                if span is rows:
                    scores = causal_mask(scores)
                prob = jnp.exp(scores - log_total)
                grad_prob = dot_last(v_ref[span, lanes], grad)
                inner = inner + jnp.sum(prob * grad_prob, axis=0, keepdims=True)
                probs.append(prob)
                weighted.append(grad_prob)
            grad_query = jnp.zeros((BLOCK, size), F32)
            for span, prob, grad_prob in zip(spans, probs, weighted):
                low = (prob * (grad_prob - inner)).astype(BF16)
                dv_sum[span, :] += dot(prob.astype(BF16), grad)
                dk_sum[span, :] += dot(low, query)
                grad_query = grad_query + dot_first(low, k_ref[span, lanes])
            d_ref[0, rows, lanes] = (grad_query * scale).astype(BF16)
        d_ref[1, :, lanes] = dk_sum[...].astype(BF16)
        d_ref[2, :, lanes] = dv_sum[...].astype(BF16)

    @pl.when(step == steps - 1)
    def _():
        sum_ref[...] = reducer.total(0, 1).astype(BF16).reshape(sum_ref.shape)
        reducer.drain(1, range(2))
        exchange.wait()


def column(rows, first=0):
    return pl.BlockSpec((rows, 128), lambda i: (0, first + i))


def attention_forward(peers, rows, other, gathered, cot, order, weight, far, size):
    tokens, features = rows.shape
    length, half = 2 * tokens, features // 2
    parts, per = half // 128, 128 // size
    slots = (peers, tokens // peers, features)
    shape, kind = jax.ShapeDtypeStruct, pltpu.SemaphoreType.DMA
    anywhere = pl.BlockSpec(memory_space=pl.ANY)
    whole = lambda *form: pl.BlockSpec(form, lambda i: (0, 0))
    return pl.pallas_call(
        functools.partial(attention_forward_kernel, peers, size),
        grid=(parts,),
        out_shape=[
            shape((tokens, features), BF16),
            shape((parts, per, length), F32),
            shape(slots, BF16),
            shape((weight.shape[0] // 2, weight.shape[1]), BF16),
            shape(far.shape, BF16),
            shape((length, features), BF16),
            shape((8, features), F32),
        ]
        + [shape((length, half), BF16)] * 3,
        in_specs=[
            whole(tokens, features),
            whole(tokens, features),
            pl.BlockSpec((features, 128), lambda i: (0, 3 * parts)),
        ]
        + [column(features, first * parts) for first in range(3)]
        + [whole(tokens, features), whole(tokens, 1), anywhere, anywhere],
        out_specs=[
            whole(tokens, features),
            pl.BlockSpec((1, per, length), lambda i: (i, 0, 0)),
            anywhere,
            anywhere,
            anywhere,
            whole(length, features),
            whole(8, features),
        ]
        + [column(length)] * 3,
        scratch_shapes=[
            pltpu.VMEM((2, tokens, 128), BF16),
            pltpu.VMEM((parts, tokens, 128), BF16),
            pltpu.VMEM((tokens, features), BF16),
            pltpu.VMEM(slots, BF16),
            kind((parts,)),
            kind((parts,)),
            kind((2, 2)),
        ]
        + exchange_sems(peers),
        compiler_params=pltpu.CompilerParams(
            vmem_limit_bytes=VMEM_LIMIT, collective_id=3, has_side_effects=True
        ),
        cost_estimate=pl.CostEstimate(
            flops=16 * length * length * half, bytes_accessed=20 * length * half, transcendentals=0
        ),
        name="attention_forward",
    )(rows, other, gathered, gathered, gathered, gathered, cot, order.reshape(tokens, 1), weight, far)


def dispatch_kernel(peers, *refs):
    mixed_ref, output_ref, rows_ref, order_ref, weight_ref, lent_ref = refs[:6]
    middle_ref, arrived_ref, far_ref, near_ref, slots, weight_sems, *exchange_refs = refs[6:]
    exchange = Exchange(peers, slots, arrived_ref, *exchange_refs)
    across = {"seq": 1 - lax.axis_index("seq")}
    rows = far_ref.shape[0]
    beside = {"fsdp": exchange.peer + 1 - 2 * lax.rem(exchange.peer, 2)}
    copies = [
        remote(
            weight_ref.at[pl.ds(rows, rows)], far_ref, weight_sems.at[0], weight_sems.at[1], across
        ),
        remote(lent_ref, near_ref, weight_sems.at[2], weight_sems.at[3], beside),
    ]
    greet(exchange.others + [across])
    for each in copies:
        each.start()
    middle = rows_ref[...].astype(F32) + dot(mixed_ref[...], output_ref[...])
    middle_ref[...] = middle
    slots[...] = placed(order_ref, middle.astype(BF16)).astype(BF16).reshape(slots.shape)
    exchange.start()
    exchange.wait()
    for each in copies:
        each.wait()


def dispatch(peers, mixed, output, rows, order, weight, lent):
    tokens, features = rows.shape
    slots = (peers, tokens // peers, features)
    shape, kind = jax.ShapeDtypeStruct, pltpu.SemaphoreType.DMA
    here, anywhere = (
        pl.BlockSpec(memory_space=pltpu.VMEM),
        pl.BlockSpec(memory_space=pl.ANY),
    )
    middle, arrived, far, near = pl.pallas_call(
        functools.partial(dispatch_kernel, peers),
        out_shape=(
            shape((tokens, features), F32),
            shape(slots, BF16),
            shape((weight.shape[0] // 2, weight.shape[1]), BF16),
            shape(lent.shape, BF16),
        ),
        in_specs=[here, here, here, here, anywhere, anywhere],
        out_specs=(here, anywhere, anywhere, anywhere),
        scratch_shapes=[pltpu.VMEM(slots, BF16), kind((4,))] + exchange_sems(peers),
        compiler_params=pltpu.CompilerParams(
            vmem_limit_bytes=VMEM_LIMIT, collective_id=4, has_side_effects=True
        ),
        cost_estimate=pl.CostEstimate(
            flops=10**9, bytes_accessed=8 * 10**7, transcendentals=0
        ),
        name="dispatch",
    )(mixed, output, rows, order.reshape(tokens, 1), weight, lent)
    return middle, arrived.reshape(tokens, features), far, near


def attention_backward(peers, saved, arrived, inverse, cot, output, gated, size):
    query, keys, values, logs, mixed = saved
    length, half = query.shape
    tokens, features = cot.shape
    parts, per, rows = half // 128, 128 // size, features // peers
    carried = (peers >> 3, 2, rows, features)
    shape, kind = jax.ShapeDtypeStruct, pltpu.SemaphoreType.DMA
    whole = lambda *form: pl.BlockSpec(form, lambda i: (0, 0), pipeline_mode=pl.Buffered(1))
    return pl.pallas_call(
        functools.partial(attention_backward_kernel, peers, size),
        grid=(parts,),
        out_shape=(
            shape((3, length, half), BF16),
            shape(carried, BF16),
            shape((tokens, features), F32),
            shape((peers, tokens // peers, features), BF16),
        ),
        in_specs=[column(length)] * 3
        + [
            pl.BlockSpec((1, per, length), lambda i: (i, 0, 0)),
            whole(tokens, features),
            whole(tokens, 1),
            whole(tokens, features),
            whole(features, features),
            whole(tokens, features),
            pl.BlockSpec(memory_space=pl.ANY),
        ],
        out_specs=(
            pl.BlockSpec((3, length, 128), lambda i: (0, 0, i)),
            pl.BlockSpec(carried, lambda i: (0, 0, 0, 0)),
            pl.BlockSpec((tokens, features), lambda i: (0, 0)),
            pl.BlockSpec(memory_space=pl.ANY),
        ),
        scratch_shapes=[
            pltpu.VMEM((length, size), F32),
            pltpu.VMEM((length, size), F32),
            pltpu.VMEM((2, parts, tokens, 128), BF16),
            pltpu.VMEM((tokens, features), BF16),
            kind((parts,)),
            kind((parts,)),
        ]
        + exchange_sems(peers)
        + halving_buffers(peers, rows, [features]),
        compiler_params=pltpu.CompilerParams(
            vmem_limit_bytes=VMEM_LIMIT, collective_id=1, has_side_effects=True
        ),
        cost_estimate=pl.CostEstimate(
            flops=20 * length * length * half, bytes_accessed=16 * length * half, transcendentals=0
        ),
        name="attention_backward",
    )(
        query,
        keys,
        values,
        logs,
        arrived,
        inverse.reshape(tokens, 1),
        cot,
        output,
        mixed,
        gated.reshape(peers, tokens // peers, features),
    )


def stream(step, steps, pairs, buffers, sems):
    def fetch(which):
        slot = lax.rem(which, 2)
        for m, refs in enumerate(pairs):
            first = 0
            for ref in refs:
                count = ref.shape[0] // CHUNK

                @pl.when(jnp.logical_and(which >= first, which < first + count))
                def _(m=m, ref=ref, first=first):
                    row = pl.multiple_of((which - first) * CHUNK, CHUNK)
                    pltpu.make_async_copy(
                        ref.at[pl.ds(row, CHUNK)], buffers[m].at[slot], sems.at[m, slot]
                    ).start()

                first += count

    @pl.when(step == 0)
    def _():
        fetch(step)

    @pl.when(step + 1 < steps)
    def _():
        fetch(step + 1)

    slot = lax.rem(step, 2)
    for m, refs in enumerate(pairs):
        pltpu.make_async_copy(
            refs[0].at[pl.ds(0, CHUNK)], buffers[m].at[slot], sems.at[m, slot]
        ).wait()
    return slot


def gelu_parts(inner):
    cdf = 0.5 * (1.0 + lax.erf(inner * 0.7071067811865476))
    slope = cdf + inner * (jnp.exp(-0.5 * inner * inner) * 0.3989422804014327)
    return inner * cdf, slope


def forward_first_kernel(steps, *refs):
    z_ref, gain_ref, shift_ref, out_bias_ref, gain_two, shift_two, bias_ref = refs[:7]
    win, wout = refs[7:11], refs[11:17]
    first_ref, normed_ref, active_ref, slope_ref, normed_two = refs[17:22]
    in_buf, out_buf, sems = refs[22:]
    step = pl.program_id(0)

    @pl.when(step == 0)
    def _():
        z = z_ref[...].astype(F32)
        xhat, _ = normalised(z)
        normed_ref[...] = (xhat * gain_ref[...] + shift_ref[...]).astype(BF16)
        first_ref[...] = jnp.broadcast_to(out_bias_ref[...], first_ref.shape)

    slot = stream(step, steps, (win, wout), (in_buf, out_buf), sems)
    active, slope = gelu_parts(dot_last(normed_ref[...], in_buf[slot]) + bias_ref[0])
    low = active.astype(BF16)
    slope_ref[...] = slope.astype(BF16)
    first_ref[...] += dot(low, out_buf[slot])

    @pl.when(step < steps // 2)
    def _():
        active_ref[...] = low

    @pl.when(step == steps - 1)
    def _():
        xhat, _ = normalised(z_ref[...].astype(F32) + first_ref[...])
        normed_two[...] = (xhat * gain_two[...] + shift_two[...]).astype(BF16)


def second_kernel(parts, steps, normed_ref, grad_ref, bias_ref, *refs):
    win, wout = refs[:parts], refs[parts : 2 * parts]
    part_ref, back_ref, active_ref, inner_ref = refs[2 * parts : 2 * parts + 4]
    total, back, in_buf, out_buf, sems = refs[2 * parts + 4 :]
    step = pl.program_id(0)

    @pl.when(step == 0)
    def _():
        total[...] = jnp.zeros_like(total)
        back[...] = jnp.zeros_like(back)

    slot = stream(step, steps, (win, wout), (in_buf, out_buf), sems)
    grad_active = dot_last(grad_ref[...], out_buf[slot])
    active, slope = gelu_parts(dot_last(normed_ref[...], in_buf[slot]) + bias_ref[0])
    low, inner = active.astype(BF16), (slope * grad_active).astype(BF16)
    active_ref[...] = low
    inner_ref[...] = inner
    total[...] += dot(low, out_buf[slot])
    back[...] += dot(inner, in_buf[slot])

    @pl.when(step == steps - 1)
    def _():
        part_ref[...] = total[...].astype(part_ref.dtype)
        back_ref[...] = back[...].astype(back_ref.dtype)


def weights_second_kernel(parts, steps, *refs):
    inner, active, normed, grad = refs[:2], refs[2:4], refs[4:6], refs[6:8]
    bias_ref = refs[8]
    gwin, gwout = refs[9 : 9 + parts], refs[9 + parts : 9 + 2 * parts]
    step = pl.program_id(0)
    per = steps // parts
    one, two = inner[0][...], inner[1][...]
    bias_ref[0] = jnp.sum(one.astype(F32), axis=0, keepdims=True) + jnp.sum(
        two.astype(F32), axis=0, keepdims=True
    )
    grad_in = (dot_first(one, normed[0][...]) + dot_first(two, normed[1][...])).astype(BF16)
    grad_out = (
        dot_first(active[0][...], grad[0][...]) + dot_first(active[1][...], grad[1][...])
    ).astype(BF16)
    for quarter in range(parts):

        @pl.when(step // per == quarter)
        def _():
            gwin[quarter][...] = grad_in
            gwout[quarter][...] = grad_out


def backward_first_kernel(steps, *refs):
    own_ref, arrived_ref, grad_two_ref, z_ref, first_ref, cot_ref = refs[:6]
    slope_ref, gain_ref, gain_two, centre_ref, _ = refs[6:11]
    win, wout = refs[11:15], refs[15:21]
    back_ref, grad_low, vector_ref, inner_ref = refs[21:25]
    total, in_buf, out_buf, sems = refs[25:]
    step = pl.program_id(0)
    down = lambda value: jnp.sum(value, axis=0, keepdims=True)

    @pl.when(step == 0)
    def _():
        total[...] = jnp.zeros_like(total)
        z = z_ref[...].astype(F32)
        xhat, rate = normalised(z + first_ref[...])
        grad_normed = own_ref[...] + arrived_ref[...].astype(F32)
        grad_rows = norm_back(grad_normed, xhat, rate, gain_two[...])
        back_ref[...] = grad_rows
        gate = jax.nn.sigmoid(jnp.sum(z * centre_ref[...], axis=-1, keepdims=True))
        low = (gate * cot_ref[...].astype(F32) + grad_rows).astype(BF16)
        grad_low[...] = low
        vector_ref[2:3] = down(low.astype(F32))
        vector_ref[3:4] = down(grad_normed * xhat)
        vector_ref[4:5] = down(grad_normed)
        vector_ref[5:6] = down(grad_two_ref[...].astype(F32))
        vector_ref[6:8] = jnp.zeros_like(vector_ref[6:8])

    slot = stream(step, steps, (win, wout), (in_buf, out_buf), sems)
    inner = (slope_ref[...].astype(F32) * dot_last(grad_low[...], out_buf[slot])).astype(BF16)
    total[...] += dot(inner, in_buf[slot])

    @pl.when(step < steps // 2)
    def _():
        inner_ref[...] = inner

    @pl.when(step == steps - 1)
    def _():
        xhat, rate = normalised(z_ref[...].astype(F32))
        grad_normed = total[...]
        vector_ref[0:1] = down(grad_normed * xhat)
        vector_ref[1:2] = down(grad_normed)
        back_ref[...] += norm_back(grad_normed, xhat, rate, gain_ref[...])


def weights_first_kernel(steps, *refs):
    inner_ref, active_ref, normed_ref, grad_ref, normed_far, grad_far, in_bias = refs[:7]
    pairs = refs[7:11]
    win, wout = refs[11:13], refs[13:15]
    bias_ref, gwin, gwout, sums = refs[15], refs[16:18], refs[18:20], refs[20:22]
    in_buf, out_buf, sems = refs[22:]
    step = pl.program_id(0)
    for m in range(2):
        sums[m][...] = pairs[2 * m][...].astype(F32) + pairs[2 * m + 1][...].astype(F32)
    slot = stream(step, steps, (win, wout), (in_buf, out_buf), sems)
    active, slope = gelu_parts(dot_last(normed_far[...], in_buf[slot]) + in_bias[0])
    inner = (slope * dot_last(grad_far[...], out_buf[slot])).astype(BF16)
    own = inner_ref[...]
    bias_ref[0] = jnp.sum(own.astype(F32), axis=0, keepdims=True) + jnp.sum(
        inner.astype(F32), axis=0, keepdims=True
    )
    grad_in = (dot_first(own, normed_ref[...]) + dot_first(inner, normed_far[...])).astype(BF16)
    grad_out = (
        dot_first(active_ref[...], grad_ref[...]) + dot_first(active.astype(BF16), grad_far[...])
    ).astype(BF16)
    for quarter in range(2):

        @pl.when(step // (steps // 2) == quarter)
        def _():
            gwin[quarter][...] = grad_in
            gwout[quarter][...] = grad_out


def expert_call(kernel, name, steps, inputs, weights, outs, scratch, flops):
    whole = lambda shape: pl.BlockSpec(shape, lambda c: (0,) * len(shape))
    spec = lambda shape, block, at: whole(shape) if block is None else pl.BlockSpec(block, at)
    if weights:
        features = weights[0].shape[-1]
        scratch = scratch + [
            pltpu.VMEM((2, CHUNK, features), BF16),
            pltpu.VMEM((2, CHUNK, features), BF16),
            pltpu.SemaphoreType.DMA((2, 2)),
        ]
    moved = sum(a.size * a.dtype.itemsize for a, _, _ in inputs + outs)
    return pl.pallas_call(
        kernel,
        grid=(steps,),
        out_shape=tuple(s for s, _, _ in outs),
        in_specs=[spec(a.shape, b, m) for a, b, m in inputs]
        + [pl.BlockSpec(memory_space=pl.ANY)] * len(weights),
        out_specs=tuple(spec(s.shape, b, m) for s, b, m in outs),
        scratch_shapes=scratch,
        compiler_params=pltpu.CompilerParams(vmem_limit_bytes=VMEM_LIMIT),
        cost_estimate=pl.CostEstimate(
            flops=2 * flops,
            bytes_accessed=moved + 2 * sum(w.size for w in weights),
            transcendentals=0,
        ),
        name=name,
    )(*[a for a, _, _ in inputs], *weights)


def expert(z, cot, vectors, biases, one, two, over, beside):
    rows, features = z.shape
    hidden = biases.shape[1]
    steps = hidden // CHUNK
    near = steps // 2
    line = lambda i: (vectors[i : i + 1], None, None)
    flat = lambda array: (array, None, None)
    shape = jax.ShapeDtypeStruct
    low_rows, wide_rows = flat(shape((rows, features), BF16)), flat(shape((rows, features), F32))
    wide = ((rows, CHUNK), lambda c: (0, c))
    thin = ((1, 1, CHUNK), lambda c: (c, 0, 0))
    chunked = biases.reshape(2, steps, 1, CHUNK)
    matmul = 2 * rows * hidden * features

    def quarter_outs(parts, count):
        per = count // parts
        return [
            (
                shape((per * CHUNK, features), BF16),
                (CHUNK, features),
                lambda c, q=q: (jnp.clip(c - q * per, 0, per - 1), 0),
            )
            for q in range(parts)
        ]

    lines = [line(i) for i in range(7)]
    held = ((rows, CHUNK), lambda c: (0, jnp.minimum(c, near - 1)))
    half_hidden = shape((rows, hidden // 2), BF16)
    wide_z, wide_cot = z.astype(F32), cot.astype(F32)
    gate = jax.nn.sigmoid(jnp.sum(wide_z * vectors[6], axis=-1, keepdims=True))
    grad_two = (gate * wide_cot).astype(BF16)
    grad_far = over(grad_two)
    first, normed_one, active_one, slope_one, normed_two = expert_call(
        functools.partial(forward_first_kernel, steps),
        "forward_first",
        steps,
        [flat(z)] + lines[:5] + [(chunked[0], *thin)],
        one[0] + one[1],
        [wide_rows, low_rows, (half_hidden, *held), (shape((rows, hidden), BF16), *wide), low_rows],
        [],
        2 * matmul,
    )
    normed_far = over(after(normed_two, grad_far))

    def second(normed, grad, kind):
        return expert_call(
            functools.partial(second_kernel, 2, near),
            "second",
            near,
            [flat(normed), flat(grad), (chunked[1, :near], *thin)],
            two[0] + two[1],
            [flat(shape((rows, features), kind))] * 2 + [(half_hidden, *wide)] * 2,
            [pltpu.VMEM((rows, features), F32)] * 2,
            2 * matmul,
        )

    own_part, grad_own_part, active_own, inner_own = second(normed_two, grad_two, F32)
    normed_one_far = over(after(normed_one, normed_far))
    normed_far = after(normed_far, inner_own)
    far_part, grad_far_part, active_far, inner_far = second(normed_far, grad_far, BF16)
    grad_far_part = after(grad_far_part, normed_one_far)
    outs = expert_call(
        functools.partial(weights_second_kernel, 2, near),
        "weights_second",
        near,
        [(a, *wide) for a in (inner_own, inner_far, active_own, active_far)]
        + [flat(a) for a in (normed_two, normed_far, grad_two, grad_far)],
        [],
        [(shape((near, 1, CHUNK), F32), *thin)] + quarter_outs(2, near) + quarter_outs(2, near),
        [],
        2 * matmul,
    )
    bias_two, gwin_two, gwout_two = outs[0].reshape(hidden // 2), outs[1:3], outs[3:5]

    grad_arrived = over(grad_far_part)
    far_arrived = over(after(far_part, grad_arrived))
    back, grad_one, sums, inner_one = expert_call(
        functools.partial(backward_first_kernel, steps),
        "backward_first",
        steps,
        [flat(a) for a in (grad_own_part, grad_arrived, grad_two, z, first, cot)]
        + [(slope_one, *wide), line(0), line(3), line(6), flat(outs[0])],
        one[0] + one[1],
        [wide_rows, low_rows, flat(shape((8, features), F32)), (half_hidden, *held)],
        [pltpu.VMEM((rows, features), F32)],
        2 * matmul,
    )
    grad_one_far = over(grad_one)
    branch = first + (own_part + far_arrived.astype(F32) + vectors[5])
    gated = (gate * branch).astype(BF16)
    grad_gate = jnp.sum(wide_cot * branch, axis=-1, keepdims=True)
    score = grad_gate * gate * (1.0 - gate)
    grad_sent = (back + score * vectors[6]).astype(BF16)
    grad_centre = jnp.sum(score * wide_z, axis=0, keepdims=True)
    strip_rows = gwin_two[0].shape[0] // near
    strip = ((strip_rows, features), lambda c: (c, 0))
    outs = expert_call(
        functools.partial(weights_first_kernel, near),
        "weights_first",
        near,
        [(inner_one, *wide), (active_one, *wide)]
        + [flat(a) for a in (normed_one, grad_one, normed_one_far, grad_one_far)]
        + [(chunked[0, :near], *thin)]
        + [
            (array, *strip)
            for mine, other in (gwin_two, gwout_two)
            for array in (mine, beside(other))
        ],
        one[0][:2] + one[1][:2],
        [(shape((near, 1, CHUNK), F32), *thin)]
        + quarter_outs(2, near)
        + quarter_outs(2, near)
        + [(shape(gwin_two[0].shape, F32), *strip)] * 2,
        [],
        3 * matmul,
    )
    bias_one = outs[0].reshape(hidden // 2)
    sums = jnp.concatenate([sums[:6], grad_centre], axis=0)
    grads = [(outs[1], outs[2]), (outs[3], outs[4])]
    return gated, grad_sent, sums, jnp.stack([bias_one, bias_two]), grads, outs[5:]


def project_back_kernel(peers, *refs):
    stages = bits_of(peers)
    d_ref, w_ref, normed_ref, own_hbm, other_hbm, middle_hbm, gain_ref = refs[:7]
    ours, theirs = refs[7:9], refs[9:11]
    place_ref, gated_ref, start_hbm = refs[11:14]
    term_ref, small_ref, lent_ref = refs[14:17]
    grad_refs, tail_ref, out_ref, pair_refs = refs[17:20], refs[20], refs[21], refs[22:24]
    layer_ref, term_out, small_out = refs[24:27]
    refs = refs[27:]
    held = [refs[i * stages : (i + 1) * stages] for i in range(4)]
    landed = [refs[i * stages : (i + 1) * stages] for i in range(4, 8)]
    reducer = Halving(peers, held, landed, *refs[8 * stages : 8 * stages + 2])
    refs = refs[8 * stages + 2 :]
    rows_send, rows_recv, rows_own, shard_send, shard_recv, tail_send, tail_recv = refs[:7]
    turned, seq_ref, middle_ref, far_send, far_recv, local = refs[7:13]
    pair_in, pair_out, in_sems, out_sems, start_ref = refs[13:18]
    term_recv, small_near, small_sum, small_far, side_sends, side_recvs = refs[18:24]
    term_send, term_sends, term_recvs = refs[24:27]
    later = stages - 2
    term_held = [None, None, term_ref, *refs[27 : 26 + later]]
    term_landed = [None, None, *refs[26 + later :]]
    output_terms = Halving(peers, [term_held], [term_landed], term_sends, term_recvs)
    start_copy = pltpu.make_async_copy(start_hbm, start_ref, local.at[3])
    start_copy.start()
    seq = lax.axis_index("seq")
    tokens, features = middle_ref.shape
    half = d_ref.shape[2]
    across = {"seq": 1 - seq}
    own_copy = pltpu.make_async_copy(own_hbm, seq_ref.at[0], local.at[0])
    other_copy = pltpu.make_async_copy(other_hbm, seq_ref.at[1], local.at[2])
    middle_copy = pltpu.make_async_copy(middle_hbm, middle_ref, local.at[1])
    own_copy.start()
    other_copy.start()
    middle_copy.start()

    piece = pair_in.shape[2]
    pieces = [(m, at) for m in range(2) for at in range(0, ours[0].shape[0], piece)]
    place = lambda ref, at: ref.at[pl.ds(at, piece)]

    def pair_inputs(i):
        m, at = pieces[i]
        return [
            pltpu.make_async_copy(
                place(ref[m], at), pair_in.at[i % 2, side], in_sems.at[i % 2, side]
            )
            for side, ref in enumerate((ours, theirs))
        ]

    def pair_output(i):
        m, at = pieces[i]
        return pltpu.make_async_copy(
            pair_out.at[i % 2], place(pair_refs[m], at), out_sems.at[i % 2]
        )

    def pair_add(count):
        for i in range(added[0], min(added[0] + count, len(pieces))):
            for copy in pair_inputs(i):
                copy.wait()
            if i >= 2:
                pair_output(i - 2).wait()
            pair_out[i % 2] = pair_in[i % 2, 0].astype(F32) + pair_in[i % 2, 1].astype(F32)
            pair_output(i).start()
            if i + 2 < len(pieces):
                for copy in pair_inputs(i + 2):
                    copy.start()
        added[0] = min(added[0] + count, len(pieces))

    added = [0]
    for i in range(2):
        for copy in pair_inputs(i):
            copy.start()
    turned[...] = normed_ref[...].T
    terms = dot(turned[...], d_ref[0])
    greet(reducer.partner + [across])
    reducer.put(0, terms)
    output_terms.copy(0, 2).start()
    term_copy = remote(term_send, term_recv, side_sends.at[0], side_recvs.at[0], across)
    near_copy = remote(
        lent_ref, small_near, side_sends.at[1], side_recvs.at[1], reducer.partner[0]
    )
    far_copy = remote(small_sum, small_far, side_sends.at[2], side_recvs.at[2], across)
    near_copy.start()
    block = lambda which: pl.ds(pl.multiple_of(which * tokens, tokens), tokens)

    def grad_rows(which):
        total = dot_last(d_ref[0, block(which), :], w_ref[:, :half])
        total += dot_last(d_ref[1, block(which), :], w_ref[:, half : 2 * half])
        return total + dot_last(d_ref[2, block(which), :], w_ref[:, 2 * half : 3 * half])

    def norm_sums(which, grad):
        xhat, _ = normalised(seq_ref[which].astype(F32))
        return jnp.sum(grad * xhat, axis=0, keepdims=True), jnp.sum(grad, axis=0, keepdims=True)

    far = grad_rows(1 - seq)
    rows_send[...] = far.astype(BF16)
    rows_copy = remote(rows_send, rows_recv, far_send.at[0], far_recv.at[0], across)
    rows_copy.start()
    for chunk in range(1, 3):
        reducer.put(chunk, dot(turned[...], d_ref[chunk]))
        reducer.finish(chunk - 1, 0)
    reducer.finish(2, 0)
    near_copy.wait()
    small_sum[...] = small_ref[...] + small_near[...]
    far_copy.start()
    own_copy.wait()
    other_copy.wait()
    far_one, far_two = norm_sums(1, far)
    own = grad_rows(seq)
    rows_own[...] = own
    own_one, own_two = norm_sums(0, own)
    line = lambda value: jnp.broadcast_to(value, (64, features))
    lines = jnp.concatenate([line(far_one + own_one), line(far_two + own_two)], axis=0)
    reducer.put(3, lines.T)
    last_copies = [
        remote(
            shard_send.at[chunk] if chunk < 3 else tail_send,
            shard_recv.at[chunk] if chunk < 3 else tail_recv,
            far_send.at[1 + chunk],
            far_recv.at[1 + chunk],
            across,
        )
        for chunk in range(4)
    ]
    for time in range(1, stages + 2):
        pair_add(1)
        if time == 2:
            start_copy.wait()
            layer_ref[...] = (start_ref[...] + placed(place_ref, gated_ref[...])).astype(BF16)
        if time + 1 < stages:
            total = output_terms.finish(0, time + 1)
            if time + 2 == stages:
                term_send[...] = total
                term_copy.start()
        for chunk in range(4):
            s = time - chunk if chunk < 3 else time - 2
            if (1 if chunk < 3 else 0) <= s < stages:
                result = reducer.finish(chunk, s)
                if s == stages - 1:
                    if chunk < 3:
                        shard_send[chunk] = result.astype(BF16)
                    else:
                        tail_send[...] = result
                    last_copies[chunk].start()
    pair_add(len(pieces))
    for i in range(len(pieces) - 2, len(pieces)):
        pair_output(i).wait()
    rows_copy.wait_recv()
    middle_copy.wait()
    xhat, rate = normalised(seq_ref[0].astype(F32))
    grad = rows_own[...] + rows_recv[...].astype(F32)
    out_ref[...] = middle_ref[...] + norm_back(grad, xhat, rate, gain_ref[...])
    columns = lambda which: pl.ds(pl.multiple_of(which * half, half), half)
    for each in last_copies:
        each.wait_recv()
    for chunk in range(3):
        grad_refs[chunk][:, columns(seq)] = shard_send[chunk].astype(F32)
        grad_refs[chunk][:, columns(1 - seq)] = shard_recv[chunk].astype(F32)
    tail_ref[...] = tail_send[...] + tail_recv[...]
    term_copy.wait()
    term_out[...] = term_send[...] + term_recv[...]
    far_copy.wait()
    small_out[...] = small_sum[...] + small_far[...]
    rows_copy.wait_send()
    for each in last_copies:
        each.wait_send()
    reducer.drain(4, range(stages))
    output_terms.drain(1, range(2, stages))


def project_back(peers, grads, weight, normed, rows_own, rows_far, grad_middle, gain, pairs, forward, terms):
    tokens, features = grad_middle.shape
    half = grads.shape[2]
    rows, stages = features // peers, bits_of(peers)
    shape = jax.ShapeDtypeStruct
    return pl.pallas_call(
        functools.partial(project_back_kernel, peers),
        out_shape=[shape((rows, features), F32)] * 3
        + [shape((rows, 128), F32), shape((tokens, features), F32)]
        + [shape(array.shape, F32) for array, _ in pairs]
        + [shape((tokens, features), BF16)]
        + [shape((rows, features), F32), shape(terms[1].shape, F32)],
        in_specs=[pl.BlockSpec(memory_space=pltpu.VMEM)] * 3
        + [pl.BlockSpec(memory_space=pl.ANY)] * 3
        + [pl.BlockSpec(memory_space=pltpu.VMEM)]
        + [pl.BlockSpec(memory_space=pl.ANY)] * 4
        + [pl.BlockSpec(memory_space=pltpu.VMEM)] * 2
        + [pl.BlockSpec(memory_space=pl.ANY)]
        + [pl.BlockSpec(memory_space=pltpu.VMEM)] * 3,
        out_specs=[pl.BlockSpec(memory_space=pltpu.VMEM)] * 5
        + [pl.BlockSpec(memory_space=pl.ANY)] * 2
        + [pl.BlockSpec(memory_space=pltpu.VMEM)] * 3,
        scratch_shapes=halving_buffers(peers, rows, [half, half, half, 128])
        + [
            pltpu.VMEM((tokens, features), BF16),
            pltpu.VMEM((tokens, features), BF16),
            pltpu.VMEM((tokens, features), F32),
            pltpu.VMEM((3, rows, half), BF16),
            pltpu.VMEM((3, rows, half), BF16),
            pltpu.VMEM((rows, 128), F32),
            pltpu.VMEM((rows, 128), F32),
            pltpu.VMEM(normed.shape[::-1], BF16),
            pltpu.VMEM((2, tokens, features), BF16),
            pltpu.VMEM((tokens, features), F32),
            pltpu.SemaphoreType.DMA((5,)),
            pltpu.SemaphoreType.DMA((5,)),
            pltpu.SemaphoreType.DMA((4,)),
            pltpu.VMEM((2, 2, 256, features), BF16),
            pltpu.VMEM((2, 256, features), F32),
            pltpu.SemaphoreType.DMA((2, 2)),
            pltpu.SemaphoreType.DMA((2,)),
            pltpu.VMEM((tokens, features), F32),
            pltpu.VMEM((rows, features), F32),
        ]
        + [pltpu.VMEM(terms[1].shape, F32)] * 3
        + [pltpu.SemaphoreType.DMA((3,))] * 2
        + [pltpu.VMEM((rows, features), F32)]
        + [pltpu.SemaphoreType.DMA((1, stages))] * 2
        + [pltpu.VMEM((peers >> (s + 1), 2, rows, features), BF16) for s in range(3, stages)]
        + [pltpu.VMEM((peers >> (s + 1), rows, features), BF16) for s in range(2, stages)],
        compiler_params=pltpu.CompilerParams(
            vmem_limit_bytes=VMEM_LIMIT, collective_id=0, has_side_effects=True
        ),
        cost_estimate=pl.CostEstimate(
            flops=60 * 10**9, bytes_accessed=40 * 10**6, transcendentals=0
        ),
        name="project_back",
    )(
        grads,
        weight,
        normed,
        rows_own,
        rows_far,
        grad_middle,
        gain,
        *[mine for mine, _ in pairs],
        *[other for _, other in pairs],
        *forward,
        *terms,
    )


def body(
    inputs,
    ln_gain,
    ln_shift,
    w_query,
    w_key,
    w_value,
    w_output,
    exp_gain1,
    exp_shift1,
    w_in1,
    b_in1,
    w_out1,
    b_out1,
    exp_gain2,
    exp_shift2,
    w_in2,
    b_in2,
    w_out2,
    b_out2,
    centroid,
    order,
    inverse,
    cotangent,
):
    seq, peer = lax.axis_index("seq"), lax.axis_index("fsdp")
    peers = lax.axis_size("fsdp")
    rows = inputs[0]
    tokens, features = rows.shape
    half = features // 2
    size = features // HEADS
    left, even = seq == 0, lax.rem(peer, 2) == 0
    over = lambda value: swapped(value, "seq")
    beside = lambda value: swapped(value, "fsdp")
    ordered = lambda flag, mine, other, axis: jnp.where(
        flag, jnp.concatenate([mine, other], axis), jnp.concatenate([other, mine], axis)
    )

    columns = lambda w: lax.dynamic_slice_in_dim(w, seq * half, half, 1)
    norm_vectors = jnp.pad(jnp.stack([ln_gain, ln_shift], axis=1), ((0, 0), (0, 126)))
    own_vectors = jnp.concatenate(
        [exp_gain1, exp_shift1, b_out1, exp_gain2, exp_shift2, b_out2, centroid], axis=0
    )
    own_biases = jnp.concatenate([b_in1, b_in2], axis=0)
    gathered, output_full, other_rows, far_in, pair, near_in, near_out = gather(
        peers,
        jnp.concatenate([columns(w_query), columns(w_key), columns(w_value), norm_vectors], axis=1),
        w_output,
        rows,
        w_in1[0],
        jnp.concatenate([own_vectors.reshape(-1), own_biases.reshape(-1)]).reshape(-1, 128),
        w_out1[0],
    )
    pair = pair.reshape(-1)
    other_vectors = pair[: own_vectors.size].reshape(own_vectors.shape)
    other_biases = pair[own_vectors.size :].reshape(own_biases.shape)
    vectors = ordered(even, own_vectors, other_vectors, 1).astype(F32)

    quarter = w_in1.shape[1]
    pick = lambda table, which: lax.dynamic_slice_in_dim(table, which * quarter, quarter, 1)
    biases = jnp.concatenate(
        [
            pick(own_biases, seq),
            pick(other_biases, seq),
            pick(own_biases, 1 - seq),
            pick(other_biases, 1 - seq),
        ],
        axis=1,
    ).astype(F32)

    two = ([w_in2[0], beside(w_in2[0])], [w_out2[0], beside(w_out2[0])])
    cot = cotangent[0]
    exchange = lambda value: lax.all_to_all(
        value.reshape(peers, tokens // peers, features),
        "fsdp",
        split_axis=0,
        concat_axis=0,
        tiled=True,
    ).reshape(tokens, features)


    outs = attention_forward(peers, rows, other_rows, gathered, cot, order, w_out1[0], far_in, size)
    mixed, logs, cot_slots, far_out_a, cross_in, normed, gain, query, keys, values = outs
    cot_slots = cot_slots.reshape(tokens, features)
    middle, z, far_out_b, cross_out_a = dispatch(
        peers, mixed, output_full, rows, order, w_out1[0], far_out_a
    )
    one = (
        [w_in1[0], near_in, far_in, cross_in],
        [w_out1[0], near_out, far_out_a, far_out_b, cross_out_a, beside(far_out_b)],
    )

    gated, grad_sent, vector_grads, bias_grads, grads_one, grads_two = expert(
        z, cot_slots, vectors, biases, one, two, over, beside
    )
    returned = exchange(grad_sent)

    own_half = lambda table, which: lax.dynamic_slice_in_dim(table, which * half, half, 1)
    core = lax.rem(peer, 2)
    bias_quarters = jnp.pad(bias_grads, ((0, 0), (0, 2 * quarter))).reshape(2, 4, quarter)
    bias_rows = lambda first: ordered(left, bias_quarters[:, first], bias_quarters[:, first + 2], 1)
    flat = lambda table, bias: jnp.concatenate([table.reshape(-1), bias.reshape(-1)])
    small = flat(own_half(vector_grads, core), bias_rows(0)).reshape(-1, 128)
    lent = flat(own_half(vector_grads, 1 - core), bias_rows(1)).reshape(-1, 128)

    parts, wo_terms, grad_middle, home = attention_backward(
        peers, (query, keys, values, logs, mixed), returned, inverse, cot, output_full, gated, size
    )
    home = home.reshape(tokens, features)
    outs = project_back(
        peers,
        parts,
        gathered,
        normed,
        rows,
        other_rows,
        grad_middle,
        gain[:1],
        [(mine, beside(near)) for mine, near in grads_one],
        (inverse.reshape(tokens, 1), home, middle),
        (wo_terms, small, lent),
    )
    grad_q, grad_k, grad_v, norm_grads, grad_inputs = outs[:5]
    grad_win_one, grad_wout_one, layer_out, grad_wo, small = outs[5:]
    small = small.reshape(-1)
    count = vector_grads.shape[0]
    vector_out = small[: count * half].reshape(count, 1, half)
    bias_out = small[count * half :].reshape(2, 1, 2 * quarter)
    grad_win_two, grad_wout_two = grads_two
    return (
        layer_out[None],
        grad_inputs[None],
        norm_grads[:, 0],
        norm_grads[:, 64],
        grad_q,
        grad_k,
        grad_v,
        grad_wo,
        vector_out[0],
        vector_out[1],
        grad_win_one[None],
        bias_out[0],
        grad_wout_one[None],
        vector_out[2],
        vector_out[3],
        vector_out[4],
        grad_win_two[None],
        bias_out[1],
        grad_wout_two[None],
        vector_out[5],
        vector_out[6],
    )


def solution(mesh):
    both, rows, vector = P("fsdp", "seq", None), P("fsdp", None), P("fsdp")
    return jax.shard_map(
        body,
        mesh=mesh,
        in_specs=(both, vector, vector, rows, rows, rows, rows)
        + (rows, rows, both, rows, both, rows) * 2
        + (rows, P("fsdp", "seq"), P("fsdp", "seq"), both),
        out_specs=(both, both, vector, vector, rows, rows, rows, rows)
        + (rows, rows, both, rows, both, rows) * 2
        + (rows,),
        check_vma=False,
    )
```
